256 devices in a mesh: log: 32 (over z, x), ctx: 8 (over y, core).
Axes of the slice: x: 4, y: 4, z: 8, core: 2. Of those that a mesh axis runs over, the one named last changes fastest.
Arguments:
- events: bfloat16 [8, 32, 512, 512], P('ctx', 'log'), may hold values from -6 to 6
- owner_ids: int32 [8, 32, 512, 1], P('ctx', 'log'), may hold values from 0 to 31; in each aligned block of 512 rows (0 to 511, 512 to 1023, ..., all dimensions but the last counted through in order) at most 20 rows name the same one
- elapsed: float32 [8, 32, 512], P('ctx', 'log'), may hold values from 0.25 to 4
- resets: float32 [8, 32, 512], P('ctx', 'log'), may hold values from 0 to 0.7
- decay_rates: float32 [4, 8], replicated, may hold values from 4.8828125e-06 to 0.04
- weights: bfloat16 [4, 4, 512, 512], replicated, may hold values from -0.25 to 0.25
- cotangent: bfloat16 [8, 32, 512, 512], P('ctx', 'log'), may hold values from -6 to 6
Outputs:
- encoded: bfloat16 [8, 32, 512, 512], P('ctx', 'log')
- event_grad: bfloat16 [8, 32, 512, 512], P('ctx', 'log')
The draws below stay inside these ranges and needn't reach their ends.
Inputs may be any that keep to these rules, and one draw needn't show every extreme that they name: `owner_ids`: the 512 events of one device name at most 20 of them with one owner; some device names exactly 20 with some owner in every draw.
All inputs are finite; a program needn't handle non-finite values.
Results may differ from the reference program's by a relative error of at most 0.014.
Values may be sent and summed in bfloat16 or wider, within the bound.
No kernel may reach another device: no remote copies, remote signals or barrier semaphores. Data moves between devices by JAX's collectives and lax.ppermute only.
A program may use at most 64 MiB of HBM per device.

```python
import math
import jax
import jax.numpy as jnp
import numpy as np
from jax import lax

D = 512
HEADS = 8
TOWERS = 4
ROWS = 512
OWNERS = 32
CTX_BLOCKS = 8
CAP = 20
SUB = 640
LIVE = 4096


def draw_resets(key, part):
    choose_key, amount_key = jax.random.split(key)
    struck = jax.random.uniform(choose_key, (CTX_BLOCKS, OWNERS, ROWS), dtype=jnp.float32) < 4.0 / LIVE
    strength = jax.random.uniform(amount_key, (CTX_BLOCKS, OWNERS, ROWS), dtype=jnp.float32, minval=0.22, maxval=0.7)
    return jnp.where(struck, strength, 0.0).astype(jnp.float32)


def draw_decay_rates(key, part):
    lowest = 0.05 / LIVE
    highest = 0.04
    fraction = jax.random.uniform(key, (TOWERS, HEADS), dtype=jnp.float32)
    return jnp.exp(math.log(lowest) + fraction * (math.log(highest) - math.log(lowest))).astype(jnp.float32)


def levels(rng, dims, shards, smallest, largest):
    factor_of = 1.0
    for dim, shards_of in shards:
        heights = jax.random.uniform(jax.random.fold_in(jax.random.fold_in(rng, 6), dim), (shards_of,), jnp.float32, smallest / len(shards), largest / len(shards))
        factor_of = factor_of * jnp.repeat(jnp.exp(heights), dims[dim] // shards_of).reshape((-1,) + (1,) * (len(dims) - 1 - dim))
    return factor_of


def assign_block(rng, own, number, rows, count, top, bound, slope):
    sequence = jax.random.permutation(rng, count)
    packed, ordinary = portions_of(count, rows * top, bound, slope, True), portions_of(count, rows * top, bound, slope, False)
    places = jnp.arange(count)

    def named(sizes, turn):
        used = int((sizes > 0).sum())
        fixed = max(1, used // 4)
        passed = fixed + (places - fixed + turn * (used - fixed)) % max(1, count - fixed)
        return jnp.zeros((count,), jnp.int32).at[sequence[jnp.where(places < fixed, places, passed)]].set(jnp.asarray(sizes, jnp.int32))

    sizes = jnp.where(number % 4 == 0, named(packed, number // 4), named(ordinary, number - number // 4 - 1))
    mixed = jax.random.permutation(jax.random.fold_in(own, 3), count)
    donor, sink = mixed[0:count // 2 * 2:2], mixed[1:count // 2 * 2:2]
    margin = jnp.minimum(sizes[donor] - 1, bound - sizes[sink]) // 2
    margin = jnp.where((donor == sequence[0]) | (sink == sequence[0]) | (sizes[sink] == 0), 0, jnp.maximum(margin, 0))
    passed = jax.random.randint(jax.random.fold_in(own, 4), (count // 2,), 0, 1 << 20) % (margin + 1)
    sizes = sizes.at[donor].add(-passed).at[sink].add(passed)
    items = jnp.searchsorted(jnp.cumsum(sizes), jnp.arange(rows * top), side="right").astype(jnp.int32)
    table = items.reshape(top, rows).T
    table = table[jax.random.permutation(jax.random.fold_in(own, 1), rows)]
    turn = jax.random.randint(jax.random.fold_in(own, 2), (rows, 1), 0, top)
    return jnp.take_along_axis(table, (jnp.arange(top)[None, :] + turn) % top, axis=1)


def portions_of(amount, total, reach, slope, full):
    weights = [(1 << 20) // math.isqrt(rank ** slope) + 1 for rank in range(1, amount + 1)]
    largest = reach if full else min(reach, max(-(-total // amount), total * weights[0] // sum(weights)))
    least = 1 if total - largest >= amount - 1 else 0
    holding, spare = [largest] + [least] * (amount - 1), total - largest - least * (amount - 1)
    while spare > 0:
        free = [i for i in range(1, amount) if holding[i] < largest] or [i for i in range(1, amount) if holding[i] < reach]
        mass, left = sum([weights[i] for i in free]), spare
        for i in free:
            addition = min(reach - holding[i], max(1, left * weights[i] // mass), spare)
            holding[i] = holding[i] + addition
            spare = spare - addition
    return np.array(holding)


def centred(stream_key, shape, scale, reach, cuts=(), kind=jnp.bfloat16):
    factor_of = levels(stream_key, shape, cuts, -0.22, 0.18) if cuts else 1.0
    result = jax.random.normal(stream_key, shape, jnp.float32) * scale * factor_of
    return jnp.minimum(jnp.maximum(result, -reach), reach).astype(kind)


def setup_inputs(seed: int = 0) -> dict:
    arg_keys = jax.random.split(jax.random.key(seed), 8)
    events = centred(arg_keys[0], (CTX_BLOCKS, OWNERS, ROWS, D), 1.0, 6.0, ((0, 8), (1, 32)))
    owner_ids_keys = jax.random.split(jax.random.fold_in(arg_keys[1], 1), CTX_BLOCKS * OWNERS * ROWS // ROWS)
    owner_ids_turns = jax.random.permutation(jax.random.fold_in(arg_keys[1], 3), CTX_BLOCKS * OWNERS * ROWS // ROWS)
    owner_ids = jax.vmap(lambda own, number: assign_block(jax.random.fold_in(arg_keys[1], 2), own, number, ROWS, OWNERS, 1, CAP, 1))(owner_ids_keys, owner_ids_turns).reshape((CTX_BLOCKS, OWNERS, ROWS, 1))
    elapsed = jnp.clip(jnp.exp(math.log(4.0) - 2.7725887 * jax.random.uniform(arg_keys[2], (CTX_BLOCKS, OWNERS, ROWS), jnp.float32) ** levels(arg_keys[2], (CTX_BLOCKS, OWNERS, ROWS), ((0, 8), (1, 32)), -0.2, 0.2)), 0.25, 4.0)
    resets = draw_resets(jax.random.fold_in(arg_keys[7], 71), 0)
    decay_rates = draw_decay_rates(jax.random.fold_in(arg_keys[7], 71), 0)
    weights = centred(arg_keys[5], (TOWERS, 4, D, D), D ** -0.5, 0.25)
    cotangent = centred(arg_keys[6], (CTX_BLOCKS, OWNERS, ROWS, D), 1.0, 6.0, ((0, 8), (1, 32)))
    return dict(events=events, owner_ids=owner_ids, elapsed=elapsed, resets=resets, decay_rates=decay_rates, weights=weights, cotangent=cotangent)


def widen(values):
    return lax.optimization_barrier(values).astype(jnp.float32)

def place_rows(targets, owner_count, capacity):
    matches = (targets[:, None] == jnp.arange(owner_count, dtype=jnp.int32)[None, :]).astype(jnp.int32)
    before = (jnp.cumsum(matches, axis=0) - matches).astype(jnp.int32)
    return (targets * capacity + lax.optimization_barrier(jnp.sum(before * matches, axis=1)).astype(jnp.int32)).astype(jnp.int32)

def block_step(memory, inputs):
    queries, key_rows, value_rows, log_fade = inputs
    length, head_count, head_dim = queries.shape
    factor = 1.0 / math.sqrt(head_dim)
    running = jnp.cumsum(log_fade, axis=0)
    causal = (jnp.arange(length)[:, None] >= jnp.arange(length)[None, :])[None]
    spread_log = running.T[:, :, None] - running.T[:, None, :]
    fading = jnp.where(causal, jnp.exp(jnp.where(causal, spread_log, 0.0)), 0.0)
    query_wide = widen(queries)
    key_wide = widen(key_rows)
    value_wide = widen(value_rows)
    scores = jnp.einsum('thd,shd->hts', query_wide, key_wide, precision=lax.Precision.HIGHEST) * factor
    mixing = (scores * fading).astype(jnp.bfloat16)
    within = jnp.einsum('hts,shd->thd', widen(mixing), value_wide, precision=lax.Precision.HIGHEST)
    lifted = query_wide * (jnp.exp(running) * factor)[:, :, None]
    carried = jnp.einsum('thd,hde->the', lifted, memory, precision=lax.Precision.HIGHEST)
    block_end = running[-1]
    keys_faded = (key_wide * jnp.exp(block_end[None, :] - running)[:, :, None]).astype(jnp.bfloat16)
    update = jnp.einsum('shd,she->hde', widen(keys_faded), value_wide, precision=lax.Precision.HIGHEST)
    return (jnp.exp(block_end)[:, None, None] * memory + update, within + carried)

def finish_rows(attended, events_wide, out_weight):
    mean_square = lax.optimization_barrier(jnp.mean(attended * attended, axis=(1, 2), keepdims=True))
    normed = (attended * lax.rsqrt(mean_square + 1e-06)).reshape(events_wide.shape).astype(jnp.bfloat16)
    return events_wide + jnp.dot(normed, out_weight, preferred_element_type=jnp.float32)

def tower_sequence(seq_events, seq_grads, seq_elapse, seq_resets, tower_id, decay_rates, weights):
    tower_weights = lax.dynamic_index_in_dim(weights, tower_id, 0, False)
    tower_rates = lax.dynamic_index_in_dim(decay_rates, tower_id, 0, False)
    log_fade = -(seq_elapse[:, None] * tower_rates[None, :] + seq_resets[:, None])
    seq_length, model_width = seq_events.shape
    head_count = tower_rates.shape[0]
    head_dim = model_width // head_count
    blocks = seq_length // SUB

    def forward(events_wide):
        narrow = events_wide.astype(jnp.bfloat16)
        projected = [jnp.dot(narrow, tower_weights[member], preferred_element_type=jnp.float32).astype(jnp.bfloat16).reshape(blocks, SUB, head_count, head_dim) for member in range(3)]
        blank_state = jnp.zeros((head_count, head_dim, head_dim), jnp.float32)
        memory_end, attended = lax.scan(block_step, blank_state, (projected[0], projected[1], projected[2], log_fade.reshape(blocks, SUB, head_count)))
        return finish_rows(attended.reshape(seq_length, head_count, head_dim), events_wide, tower_weights[3])
    encoded_wide, pullback = jax.vjp(forward, seq_events.astype(jnp.float32))
    grads, = pullback(seq_grads.astype(jnp.float32))
    return (encoded_wide.astype(jnp.bfloat16), grads.astype(jnp.bfloat16))

def reference(events, owner_ids, elapsed, resets, decay_rates, weights, cotangent):
    ctx_count, owner_count, row_count, model_width = events.shape
    capacity = 5 * row_count // (4 * owner_count)
    slot_count = owner_count * capacity
    groups = owner_count // decay_rates.shape[0]

    def plan_block(targets):
        return place_rows(targets, owner_count, capacity)
    slot_index = jax.vmap(jax.vmap(plan_block))(owner_ids[..., 0])

    def place_one(values, indices):
        return jnp.zeros((slot_count,) + values.shape[1:], values.dtype).at[indices].set(values)

    def spread(values):
        placed = jax.vmap(jax.vmap(place_one))(values, slot_index)
        placed = placed.reshape((ctx_count, owner_count, owner_count, capacity) + values.shape[3:])
        moved = jnp.moveaxis(placed, 2, 0)
        return moved.reshape((owner_count, ctx_count * slot_count) + values.shape[3:])
    seq_events = spread(events)
    seq_grads = spread(cotangent)
    seq_elapse = spread(elapsed)
    seq_resets = spread(resets)
    owner_list = jnp.arange(owner_count, dtype=jnp.int32)

    def per_owner(bundle):
        one_events, one_grads, one_elapse, one_resets, owner = bundle
        return tower_sequence(one_events, one_grads, one_elapse, one_resets, (owner // groups).astype(jnp.int32), decay_rates, weights)
    seq_encoded, seq_event_grads = lax.map(per_owner, (seq_events, seq_grads, seq_elapse, seq_resets, owner_list))

    def gather_back(values):
        shaped = values.reshape(owner_count, ctx_count, owner_count, capacity, model_width)
        moved = jnp.moveaxis(shaped, 0, 2).reshape(ctx_count, owner_count, slot_count, model_width)
        return jnp.take_along_axis(moved, slot_index[..., None], axis=2)
    return (gather_back(seq_encoded), gather_back(seq_event_grads))
```

```python
import jax
import jax.numpy as jnp
from jax import lax
from jax.experimental import pallas as pl
from jax.experimental.pallas import tpu as pltpu
from jax.sharding import PartitionSpec as P


bf16 = jnp.bfloat16
f32 = jnp.float32
CH = 128
NN = (((1,), (0,)), ((), ()))
NT = (((1,), (1,)), ((), ()))
TN = (((0,), (0,)), ((), ()))
EXACT = lax.Precision.HIGHEST
LIMIT = 40 << 20


def dot(a, b, dims=NN, precision=None):
    return lax.dot_general(a, b, dims, preferred_element_type=f32, precision=precision)


def iota(shape, dim):
    return lax.broadcasted_iota(jnp.int32, shape, dim)


def ones_where(cond, dtype=bf16):
    return jnp.where(cond, 1.0, 0.0).astype(dtype)


def call(body, outs, ins, scratch=()):
    return pl.pallas_call(
        body,
        out_shape=[jax.ShapeDtypeStruct(s, d) for s, d in outs],
        scratch_shapes=list(scratch),
        compiler_params=pltpu.CompilerParams(vmem_limit_bytes=LIMIT),
        name=body.__name__.strip("_"),
    )(*ins)


def write_message(message, scratch, rows_of, width):
    parts = width // 128
    count = scratch.shape[0] // parts
    for j in range(parts):
        scratch[pl.ds(j, count, stride=parts), :] = rows_of(j)
    owners = message.shape[0]
    per = scratch.shape[0] // owners
    message[:, 0:per, :] = scratch[...].reshape(owners, per, 128).astype(bf16)


def read_message(message, scratch, width):
    parts = width // 128
    count = scratch.shape[0] // parts
    owners = message.shape[0]
    per = scratch.shape[0] // owners
    scratch[...] = message[:, 0:per, :].astype(f32).reshape(scratch.shape)
    return [scratch[pl.ds(j, count, stride=parts), :] for j in range(parts)]


def pack_events(owner, events, elapsed, resets, message, place, scratch):
    rows, width = events.shape
    owners = message.shape[0]
    slots = place.shape[0]
    cap = slots // owners
    own = owner[...]
    hit = iota((owners, rows), 0) == own
    earlier = ones_where(iota((rows, rows), 0) < iota((rows, rows), 1))
    before = dot(ones_where(hit), earlier)
    rank = jnp.sum(jnp.where(hit, before, 0.0), axis=0, keepdims=True).astype(jnp.int32)
    place[...] = ones_where(iota((slots, rows), 0) == own * cap + rank)
    write_message(
        message,
        scratch,
        lambda j: dot(place[...], events[:, 128 * j : 128 * (j + 1)]),
        width,
    )
    lanes = iota((128, rows), 0)
    times = jnp.zeros((owners, 128), f32)
    for k, ref in enumerate((elapsed, resets)):
        value = ref[...]
        high = value.astype(bf16).astype(f32)
        for m, part in enumerate((high, value - high)):
            spot = ones_where(lanes == rank + cap * (2 * k + m))
            times += dot(jnp.where(hit, part, 0.0).astype(bf16), spot, NT)
    spread = ones_where(iota((owners * 8, owners), 0) == 8 * iota((owners * 8, owners), 1))
    extra = dot(spread, times.astype(bf16)).reshape(owners, 8, 128)
    per = scratch.shape[0] // owners
    message[:, per : per + 8, :] = extra.astype(bf16)


def pack_grads(place, grads, message, back, scratch):
    rows, width = grads.shape
    write_message(
        message,
        scratch,
        lambda j: dot(place[...], grads[:, 128 * j : 128 * (j + 1)]),
        width,
    )
    same = ones_where(iota((rows, rows), 0) == iota((rows, rows), 1))
    back[...] = dot(same, place[...], NT).astype(bf16)


def unpack_rows(back, message, out, scratch):
    width = out.shape[1]
    for j, part in enumerate(read_message(message, scratch, width)):
        out[:, 128 * j : 128 * (j + 1)] = dot(back[...], part.astype(bf16)).astype(bf16)


def halves():
    low = ones_where(iota((CH, 128), 1) < 64)
    return low, ones_where(iota((CH, 128), 1) >= 64)


def block_mask():
    return (iota((128, 128), 0) < 64) == (iota((128, 128), 1) < 64)


def stacked(value, low, high):
    return jnp.concatenate([value * low, value * high], axis=0)


def decay_pair(fade, fade_t, rows, j, p):
    causal = iota((CH, CH), 0) >= iota((CH, CH), 1)
    both = []
    turned = fade_t[j]
    here = fade[rows, :]
    for h in (2 * p, 2 * p + 1):
        spread = here[:, h : h + 1] - turned[h : h + 1, :]
        both.append(jnp.exp(jnp.where(causal, spread, -1e30)))
    return jnp.concatenate(both, axis=1)


def write_state(send, state, marks_t, pairs):
    for p in range(pairs):
        full = state[p]
        send[64 * p : 64 * (p + 1), :] = (full[0:64, :] + full[64:128, :]).astype(bf16)
    high = marks_t.astype(bf16).astype(f32)
    lane = iota(marks_t.shape, 1)
    send[64 * pairs : 64 * pairs + 8, :] = jnp.where(lane < 64, high, marks_t - high).astype(bf16)


def gathered_state(received, pairs):
    lane = iota((1, 128), 1)
    total = [jnp.zeros((64, 128), f32) for _ in range(pairs)]
    log = jnp.zeros((8, 1), f32)
    for ref in received:
        for p in range(pairs):
            factor = jnp.exp(
                jnp.where(
                    lane < 64,
                    jnp.broadcast_to(log[2 * p : 2 * p + 1, :], (1, 128)),
                    jnp.broadcast_to(log[2 * p + 1 : 2 * p + 2, :], (1, 128)),
                )
            )
            total[p] += factor * ref[64 * p : 64 * (p + 1), :].astype(f32)
        marks = ref[64 * pairs : 64 * pairs + 8, :].astype(f32)
        log = log + marks[:, 0:1] + marks[:, 64:65]
    mask = ones_where(block_mask(), f32)
    return [jnp.concatenate([t, t], axis=0) * mask for t in total]


def forward_local(
    message, rate_row, rate_col, wq, wk, wv,
    x, q8, keys, values, fade, fade_t, fade_x, marks, attended, states, send,
    scratch, memory,
):
    slots, width = x.shape
    pairs = width // 128
    blocks = slots // CH
    owners = message.shape[0]
    cap = slots // owners
    per = cap * pairs
    for j, part in enumerate(read_message(message, scratch, width)):
        x[:, 128 * j : 128 * (j + 1)] = part.astype(bf16)
    times = message[:, per : per + 8, :].astype(f32).reshape(owners * 8, 128).astype(bf16)
    r = iota((slots, owners * 8), 0)
    c = iota((slots, owners * 8), 1)
    expand = ones_where(((c & 7) == 0) & (8 * r >= cap * c) & (8 * r < cap * (c + 8)))
    wide = dot(expand, times)
    row = iota((slots, 128), 0).astype(f32)
    lane = iota((slots, 128), 1).astype(f32)
    s = row - cap * jnp.floor((row + 0.5) * (1.0 / cap))
    hit = (lane == s) | (lane == s + cap) | (lane == s + 2 * cap) | (lane == s + 3 * cap)
    own = jnp.where(hit, wide, 0.0).astype(bf16)
    tri = ones_where(iota((slots, slots), 0) >= iota((slots, slots), 1))
    running = dot(tri, own)
    kind = iota((128, 128), 0)
    to_heads = jnp.where(kind < 2 * cap, -rate_row[...], jnp.where(kind < 4 * cap, -1.0, 0.0))
    fade[...] = dot(running, to_heads, NN, EXACT)
    kind = iota((8, 128), 1)
    to_heads = jnp.where(kind < 2 * cap, -rate_col[...], jnp.where(kind < 4 * cap, -1.0, 0.0))
    turned = dot(to_heads, running, NT, EXACT)
    for j in range(blocks):
        fade_t[j] = turned[:, CH * j : CH * (j + 1)]
    lower = iota((slots, 128), 1) < 64
    for p in range(pairs):
        fade_x[:, 128 * p : 128 * (p + 1)] = jnp.where(
            lower,
            jnp.broadcast_to(fade[:, 2 * p : 2 * p + 1], (slots, 128)),
            jnp.broadcast_to(fade[:, 2 * p + 1 : 2 * p + 2], (slots, 128)),
        )
    for j in range(blocks):
        for p in range(pairs):
            cols = slice(128 * p, 128 * (p + 1))
            if j == 0:
                marks[j, p : p + 1, :] = jnp.zeros((1, 128), f32)
            else:
                marks[j, p : p + 1, :] = fade_x[CH * j - 1 : CH * j, cols]
            marks[j, pairs + p : pairs + p + 1, :] = fade_x[CH * j + CH - 1 : CH * j + CH, cols]

    def project(j, carry):
        rows = pl.ds(pl.multiple_of(j * CH, CH), CH)
        here = x[rows, :]
        q8[rows, :] = (dot(here, wq[...]).astype(bf16).astype(f32) * 0.125).astype(bf16)
        keys[rows, :] = dot(here, wk[...]).astype(bf16)
        values[rows, :] = dot(here, wv[...]).astype(bf16)
        return carry

    lax.fori_loop(0, blocks, project, 0)
    low, high = halves()
    mask = block_mask()
    memory[...] = jnp.zeros(memory.shape, f32)

    def block(j, carry):
        rows = pl.ds(pl.multiple_of(j * CH, CH), CH)
        edge = marks[j]
        for p in range(pairs):
            cols = slice(128 * p, 128 * (p + 1))
            start, end = edge[p : p + 1, :], edge[pairs + p : pairs + p + 1, :]
            qp, kp, vp, g = q8[rows, cols], keys[rows, cols], values[rows, cols], fade_x[rows, cols]
            scores = dot(qp, stacked(kp, low, high), NT)
            mix = (scores * decay_pair(fade, fade_t, rows, j, p)).astype(bf16)
            within = dot(mix, stacked(vp, low, high))
            now = memory[p]
            states[j, p] = now
            lifted = (qp.astype(f32) * jnp.exp(g - start)).astype(bf16)
            attended[rows, cols] = within + dot(lifted, now.astype(bf16))
            kf = (kp.astype(f32) * jnp.exp(end - g)).astype(bf16)
            memory[p] = jnp.exp(end - start) * now + jnp.where(mask, dot(kf, vp, TN), 0.0)
        return carry

    lax.fori_loop(0, blocks, block, 0)
    last = turned[:, slots - 1 : slots]
    write_state(send, memory, jnp.broadcast_to(last, (8, 128)), pairs)


def forward_finish(q8, fade_x, attended, x, wo, *rest):
    received = rest[:-4]
    message, full, incoming, scratch = rest[-4:]
    slots, width = x.shape
    pairs = width // 128
    states = gathered_state(received, pairs)
    for p in range(pairs):
        incoming[p] = states[p]
    narrow = [state.astype(bf16) for state in states]
    blocks = slots // CH

    def block(j, carry):
        rows = pl.ds(pl.multiple_of(j * CH, CH), CH)
        square = jnp.zeros((CH, 1), f32)
        for p in range(pairs):
            cols = slice(128 * p, 128 * (p + 1))
            lifted = (q8[rows, cols].astype(f32) * jnp.exp(fade_x[rows, cols])).astype(bf16)
            value = attended[rows, cols] + dot(lifted, incoming[p].astype(bf16))
            full[rows, cols] = value
            square += jnp.sum(value * value, axis=1, keepdims=True)
        scale = lax.rsqrt(square * (1.0 / width) + 1e-06)
        normed = (full[rows, :] * scale).astype(bf16)
        encoded = x[rows, :].astype(f32) + dot(normed, wo[...])
        for p in range(pairs):
            scratch[pl.ds(j * CH * pairs + p, CH, stride=pairs), :] = encoded[
                :, 128 * p : 128 * (p + 1)
            ]
        return carry

    lax.fori_loop(0, blocks, block, 0)
    owners = message.shape[0]
    message[...] = scratch[...].reshape(owners, slots * pairs // owners, 128).astype(bf16)


def backward_local(
    message, q8, keys, values, fade, fade_t, fade_x, marks, full, states, incoming, wq, wo,
    partial, grad_keys, grad_values, send,
    scratch, grad_full, memory, grad_q, grads,
):
    slots, width = full.shape
    pairs = width // 128
    blocks = slots // CH
    for j, part in enumerate(read_message(message, scratch, width)):
        grads[:, 128 * j : 128 * (j + 1)] = part.astype(bf16)

    def normed(j, carry):
        rows = pl.ds(pl.multiple_of(j * CH, CH), CH)
        here = full[rows, :]
        grad = dot(grads[rows, :], wo[...], NT).astype(bf16).astype(f32)
        scale = lax.rsqrt(jnp.mean(here * here, axis=1, keepdims=True) + 1e-06)
        along = jnp.mean(here * grad, axis=1, keepdims=True)
        grad_full[rows, :] = (scale * grad - here * (scale * scale * scale * along)).astype(bf16)
        return carry

    lax.fori_loop(0, blocks, normed, 0)
    low, high = halves()
    lower = iota((CH, 128), 1) < 64
    mask = block_mask()
    memory[...] = jnp.zeros(memory.shape, f32)

    def block(i, carry):
        j = blocks - 1 - i
        rows = pl.ds(pl.multiple_of(j * CH, CH), CH)
        edge = marks[j]
        for p in range(pairs):
            cols = slice(128 * p, 128 * (p + 1))
            start, end = edge[p : p + 1, :], edge[pairs + p : pairs + p + 1, :]
            qp, kp, vp, g = q8[rows, cols], keys[rows, cols], values[rows, cols], fade_x[rows, cols]
            da = grad_full[rows, cols]
            ks, vs = stacked(kp, low, high), stacked(vp, low, high)
            fading = decay_pair(fade, fade_t, rows, j, p)
            mix = (dot(qp, ks, NT) * fading).astype(bf16)
            grad_scores = (dot(da, vs, NT) * fading).astype(bf16)
            lift = jnp.exp(g - start)
            fall = jnp.exp(end - g)
            state = (states[j, p] + jnp.exp(start) * incoming[p]).astype(bf16)
            grad_q[rows, cols] = (
                0.125 * (dot(grad_scores, ks) + lift * dot(da, state, NT))
            ).astype(bf16)
            gk = dot(grad_scores, qp, TN)
            gv = dot(mix, da, TN)
            now = memory[p]
            narrow = now.astype(bf16)
            kf = (kp.astype(f32) * fall).astype(bf16)
            grad_keys[rows, cols] = jnp.where(lower, gk[0:CH], gk[CH:]) + fall * dot(vp, narrow, NT)
            grad_values[rows, cols] = jnp.where(lower, gv[0:CH], gv[CH:]) + dot(kf, narrow)
            lifted = (qp.astype(f32) * lift).astype(bf16)
            memory[p] = jnp.exp(end - start) * now + jnp.where(mask, dot(lifted, da, TN), 0.0)
        return carry

    lax.fori_loop(0, blocks, block, 0)
    last = fade_t[blocks - 1][:, CH - 1 : CH]
    write_state(send, memory, jnp.broadcast_to(last, (8, 128)), pairs)

    def project(j, carry):
        rows = pl.ds(pl.multiple_of(j * CH, CH), CH)
        partial[rows, :] = grads[rows, :].astype(f32) + dot(grad_q[rows, :], wq[...], NT)
        return carry

    lax.fori_loop(0, blocks, project, 0)


def backward_finish(partial, grad_keys, grad_values, keys, values, fade_x, marks, wk, wv, *rest):
    received = rest[:-5]
    message, scratch, incoming, gk, gv = rest[-5:]
    slots, width = partial.shape
    pairs = width // 128
    blocks = slots // CH
    states = gathered_state(received, pairs)
    for p in range(pairs):
        incoming[p] = states[p].astype(bf16)

    def block(j, carry):
        rows = pl.ds(pl.multiple_of(j * CH, CH), CH)
        for p in range(pairs):
            cols = slice(128 * p, 128 * (p + 1))
            end = marks[blocks - 1, pairs + p : pairs + p + 1, :]
            fall = jnp.exp(end - fade_x[rows, cols])
            kf = (keys[rows, cols].astype(f32) * fall).astype(bf16)
            state = incoming[p]
            gk[:, cols] = (grad_keys[rows, cols] + fall * dot(values[rows, cols], state, NT)).astype(bf16)
            gv[:, cols] = (grad_values[rows, cols] + dot(kf, state)).astype(bf16)
        total = partial[rows, :] + dot(gk[...], wk[...], NT) + dot(gv[...], wv[...], NT)
        for p in range(pairs):
            scratch[pl.ds(j * CH * pairs + p, CH, stride=pairs), :] = total[:, 128 * p : 128 * (p + 1)]
        return carry

    lax.fori_loop(0, blocks, block, 0)
    owners = message.shape[0]
    message[...] = scratch[...].reshape(owners, slots * pairs // owners, 128).astype(bf16)


def exchange(value, axis, sign):
    count = lax.axis_size(axis)
    return [
        lax.ppermute(
            value, axis, [(i, i + sign * k) for i in range(count) if 0 <= i + sign * k < count]
        )
        for k in range(1, count)
    ]


def regroup(value):
    return lax.all_to_all(value, "log", split_axis=0, concat_axis=0, tiled=True)


def shards(events, owner_ids, elapsed, resets, decay_rates, weights, cotangent):
    rows, width = events.shape[2:]
    owners = lax.axis_size("log")
    cap = 5 * rows // (4 * owners)
    slots = owners * cap
    pairs = width // 128
    blocks = slots // CH
    heads = decay_rates.shape[1]
    per = cap * pairs
    flat = pltpu.VMEM((slots * pairs, 128), f32)
    states = ((pairs, 128, 128), f32)
    state_vmem = pltpu.VMEM(*states)
    state_msg = ((64 * pairs + 8, 128), bf16)
    wide_msg = ((owners, per, 128), bf16)
    wide16, wide32 = ((slots, width), bf16), ((slots, width), f32)

    tower = lax.axis_index("log") // (owners // decay_rates.shape[0])
    mine = lax.dynamic_index_in_dim(weights, tower, 0, False)
    wq, wk, wv, wo = [mine[i] for i in range(4)]
    rates = lax.dynamic_index_in_dim(decay_rates, tower, 0, False)
    rate_row = jnp.pad(rates, (0, 128 - heads)).reshape(1, 128)
    rate_col = jnp.broadcast_to(rates[:, None], (heads, 128))

    message, place = call(
        pack_events,
        [((owners, per + 8, 128), bf16), ((slots, rows), bf16)],
        [
            owner_ids.reshape(1, rows),
            events.reshape(rows, width),
            elapsed.reshape(1, rows),
            resets.reshape(1, rows),
        ],
        [flat],
    )
    events_in = regroup(message)
    message, back = call(
        pack_grads,
        [wide_msg, ((rows, slots), bf16)],
        [place, cotangent.reshape(rows, width)],
        [flat],
    )
    grads_in = regroup(message)
    x, q8, keys, values, fade, fade_t, fade_x, marks, attended, kept, send = call(
        forward_local,
        [
            wide16, wide16, wide16, wide16,
            ((slots, 128), f32), ((blocks, 8, 128), f32), wide32, ((blocks, 2 * pairs, 128), f32),
            wide32, ((blocks, pairs, 128, 128), f32), state_msg,
        ],
        [events_in, rate_row, rate_col, wq, wk, wv],
        [flat, state_vmem],
    )
    received = exchange(send, "ctx", 1)
    message, full, incoming = call(
        forward_finish,
        [wide_msg, wide32, states],
        [q8, fade_x, attended, x, wo, *received],
        [flat],
    )
    encoded_in = regroup(message)
    partial, grad_keys, grad_values, send = call(
        backward_local,
        [wide32, wide32, wide32, state_msg],
        [grads_in, q8, keys, values, fade, fade_t, fade_x, marks, full, kept, incoming, wq, wo],
        [
            flat,
            pltpu.VMEM((slots, width), bf16),
            state_vmem,
            pltpu.VMEM((slots, width), bf16),
            pltpu.VMEM((slots, width), bf16),
        ],
    )
    received = exchange(send, "ctx", -1)
    (message,) = call(
        backward_finish,
        [wide_msg],
        [partial, grad_keys, grad_values, keys, values, fade_x, marks, wk, wv, *received],
        [
            flat,
            pltpu.VMEM((pairs, 128, 128), bf16),
            pltpu.VMEM((CH, width), bf16),
            pltpu.VMEM((CH, width), bf16),
        ],
    )
    grad_in = regroup(message)
    (encoded,) = call(unpack_rows, [((rows, width), bf16)], [back, encoded_in], [flat])
    (grad,) = call(unpack_rows, [((rows, width), bf16)], [back, grad_in], [flat])
    return encoded.reshape(events.shape), grad.reshape(events.shape)


def solution(mesh):
    wide = P("ctx", "log", None, None)
    flat = P("ctx", "log", None)
    return jax.shard_map(
        shards,
        mesh=mesh,
        in_specs=(wide, wide, flat, flat, P(), P(), wide),
        out_specs=(wide, wide),
        check_vma=False,
    )
```

```python
import jax
import jax.numpy as jnp
from jax import lax
from jax.experimental import pallas as pl
from jax.experimental.pallas import tpu as pltpu
from jax.sharding import PartitionSpec as P


bf16 = jnp.bfloat16
f32 = jnp.float32
CH = 128
NN = (((1,), (0,)), ((), ()))
NT = (((1,), (1,)), ((), ()))
TN = (((0,), (0,)), ((), ()))
EXACT = lax.Precision.HIGHEST
LIMIT = 16 << 20


def dot(a, b, dims=NN, precision=None):
    return lax.dot_general(a, b, dims, preferred_element_type=f32, precision=precision)


def iota(shape, dim):
    return lax.broadcasted_iota(jnp.int32, shape, dim)


def ones_where(cond, dtype=bf16):
    return jnp.where(cond, 1.0, 0.0).astype(dtype)


VMEM = pl.BlockSpec(memory_space=pltpu.VMEM)
SMEM = pl.BlockSpec(memory_space=pltpu.SMEM)
HBM = pl.BlockSpec(memory_space=pltpu.HBM)


def call(body, outs, ins, scratch=(), spaces=None, out_hbm=()):
    ins = [
        pltpu.with_memory_space_constraint(v, pltpu.HBM) if (spaces or {}).get(i) is HBM else v
        for i, v in enumerate(ins)
    ]
    return pl.pallas_call(
        body,
        out_shape=[
            pltpu.HBM(s, d) if i in out_hbm else jax.ShapeDtypeStruct(s, d)
            for i, (s, d) in enumerate(outs)
        ],
        in_specs=[(spaces or {}).get(i, VMEM) for i in range(len(ins))],
        out_specs=[HBM if i in out_hbm else VMEM for i in range(len(outs))],
        scratch_shapes=list(scratch),
        compiler_params=pltpu.CompilerParams(vmem_limit_bytes=LIMIT),
    )(*ins)


def write_rows(scratch, rows_of, parts):
    count = scratch.shape[0] // parts
    for j in range(parts):
        scratch[pl.ds(j, count, stride=parts), :] = rows_of(j)


def write_message(message, scratch, rows_of, width):
    write_rows(scratch, rows_of, width // 128)
    owners = message.shape[0]
    per = scratch.shape[0] // owners
    message[:, 0:per, :] = scratch[...].reshape(owners, per, 128).astype(bf16)


def read_message(message, scratch, width):
    parts = width // 128
    count = scratch.shape[0] // parts
    owners = message.shape[0]
    per = scratch.shape[0] // owners
    scratch[...] = message[:, 0:per, :].astype(f32).reshape(scratch.shape)
    return [scratch[pl.ds(j, count, stride=parts), :] for j in range(parts)]


class Sender:
    def __init__(self, out, wide, narrow, sems, parts):
        self.out, self.wide, self.narrow, self.sems, self.parts = out, wide, narrow, sems, parts

    def copy(self, j):
        size = CH * self.parts
        span = pl.ds(pl.multiple_of(j * size, size), size)
        return pltpu.make_async_copy(self.narrow.at[span, :], self.out.at[span, :], self.sems.at[j])

    def put(self, j, value):
        size = CH * self.parts
        for p in range(self.parts):
            self.wide[pl.ds(p, CH, stride=self.parts), :] = value[:, 128 * p : 128 * (p + 1)]
        span = pl.ds(pl.multiple_of(j * size, size), size)
        self.narrow[span, :] = self.wide[...].astype(bf16)
        self.copy(j).start()

    def finish(self, blocks):
        for j in range(blocks):
            self.copy(j).wait()


def fetched(source, target, sem):
    copy = pltpu.make_async_copy(source, target, sem)
    copy.start()
    return copy


def expanded(fade, rows, p):
    here = fade[rows, :]
    shape = (here.shape[0], 128)
    return jnp.where(
        iota(shape, 1) < 64,
        jnp.broadcast_to(here[:, 2 * p : 2 * p + 1], shape),
        jnp.broadcast_to(here[:, 2 * p + 1 : 2 * p + 2], shape),
    )


def pack_events(
    owner_in, events_in, elapsed_in, resets_in, message, place,
    scratch, owner, events, elapsed, resets, sems,
):
    copies = [
        pltpu.make_async_copy(source, target, sems.at[i])
        for i, (source, target) in enumerate(
            (
                (owner_in, owner),
                (elapsed_in, elapsed),
                (resets_in, resets),
                (events_in, events),
            )
        )
    ]
    for copy in copies:
        copy.start()
    copies[0].wait()
    rows, width = events.shape
    owners = message.shape[0]
    slots = place.shape[0]
    cap = slots // owners
    own = owner[...]
    hit = iota((owners, rows), 0) == own
    earlier = ones_where(iota((rows, rows), 0) < iota((rows, rows), 1))
    before = dot(ones_where(hit), earlier)
    rank = jnp.sum(jnp.where(hit, before, 0.0), axis=0, keepdims=True).astype(jnp.int32)
    place[...] = ones_where(iota((slots, rows), 0) == own * cap + rank)
    for copy in copies[1:]:
        copy.wait()
    write_message(
        message,
        scratch,
        lambda j: dot(place[...], events[:, 128 * j : 128 * (j + 1)]),
        width,
    )
    lanes = iota((128, rows), 0)
    times = jnp.zeros((owners, 128), f32)
    for k, ref in enumerate((elapsed, resets)):
        value = ref[...]
        high = value.astype(bf16).astype(f32)
        for m, part in enumerate((high, value - high)):
            spot = ones_where(lanes == rank + cap * (2 * k + m))
            times += dot(jnp.where(hit, part, 0.0).astype(bf16), spot, NT)
    spread = ones_where(iota((owners * 8, owners), 0) == 8 * iota((owners * 8, owners), 1))
    extra = dot(spread, times.astype(bf16)).reshape(owners, 8, 128)
    per = scratch.shape[0] // owners
    message[:, per : per + 8, :] = extra.astype(bf16)


def pack_grads(info, place, grads, message, back, scratch):
    rows, width = grads.shape
    write_message(
        message,
        scratch,
        lambda j: dot(place[...], grads[:, 128 * j : 128 * (j + 1)]),
        width,
    )
    same = ones_where(iota((rows, rows), 0) == iota((rows, rows), 1))
    back[...] = dot(same, place[...], NT).astype(bf16)


def unpack_rows(back, message, out, scratch):
    width = out.shape[1]
    for j, part in enumerate(read_message(message, scratch, width)):
        out[:, 128 * j : 128 * (j + 1)] = dot(back[...], part.astype(bf16)).astype(bf16)


def halves():
    low = ones_where(iota((CH, 128), 1) < 64)
    return low, ones_where(iota((CH, 128), 1) >= 64)


def block_mask():
    return (iota((128, 128), 0) < 64) == (iota((128, 128), 1) < 64)


def stacked(value, low, high):
    return jnp.concatenate([value * low, value * high], axis=0)


def decay_pair(fade, fade_t, rows, j, p):
    causal = iota((CH, CH), 0) >= iota((CH, CH), 1)
    both, wide = [], []
    turned = fade_t[j]
    here = fade[rows, :]
    for h in (2 * p, 2 * p + 1):
        column = jnp.broadcast_to(here[:, h : h + 1], (CH, CH))
        wide.append(column)
        spread = column - turned[h : h + 1, :]
        both.append(jnp.exp(jnp.where(causal, spread, -1e30)))
    return jnp.concatenate(both, axis=1), jnp.where(iota((CH, CH), 1) < 64, wide[0], wide[1])


def folded(full):
    return full[0:64, :] + full[64:128, :]


def unfolded(half, mask):
    return jnp.where(mask, jnp.concatenate([half, half], axis=0), 0.0)


def write_state(send, state, last, pairs):
    for p in range(pairs):
        send[64 * p : 64 * (p + 1), :] = folded(state[p]).astype(bf16)
    write_marks(send, last, pairs)


def write_marks(send, last, pairs):
    last = jnp.broadcast_to(last, (8, 128))
    high = last.astype(bf16).astype(f32)
    lane = iota(last.shape, 1)
    send[64 * pairs : 64 * pairs + 8, :] = jnp.where(lane < 64, high, last - high).astype(bf16)


def read_marks(ref, pairs):
    marks = ref[64 * pairs : 64 * pairs + 8, :].astype(f32)
    return marks[:, 0:1] + marks[:, 64:65]


def lane_factors(log, p):
    return jnp.exp(
        jnp.where(
            iota((1, 128), 1) < 64,
            jnp.broadcast_to(log[2 * p : 2 * p + 1, :], (1, 128)),
            jnp.broadcast_to(log[2 * p + 1 : 2 * p + 2, :], (1, 128)),
        )
    )


def join_pair(near, far, out, pairs):
    log = read_marks(near, pairs)
    for p in range(pairs):
        rows = slice(64 * p, 64 * (p + 1))
        joined = near[rows, :].astype(f32) + lane_factors(log, p) * far[rows, :].astype(f32)
        out[rows, :] = joined.astype(bf16)
    write_marks(out, log + read_marks(far, pairs), pairs)


def join_ahead(info, own, other, out):
    join(info[1] == 1, own, other, out)


def join_back(info, own, other, out):
    join(info[1] == 0, own, other, out)


def join(own_is_near, own, other, out):
    pairs = own.shape[0] // 64

    @pl.when(own_is_near)
    def _():
        join_pair(own, other, out, pairs)

    @pl.when(jnp.logical_not(own_is_near))
    def _():
        join_pair(other, own, out, pairs)


def gathered_state(partner_counts, partner, received, pairs):
    log = read_marks(partner, pairs) * partner_counts
    total = [partner[64 * p : 64 * (p + 1), :].astype(f32) * partner_counts for p in range(pairs)]
    for ref in received:
        for p in range(pairs):
            total[p] += lane_factors(log, p) * ref[64 * p : 64 * (p + 1), :].astype(f32)
        log = log + read_marks(ref, pairs)
    return total


def forward_state(
    info, rates, message_in, weights,
    x_out, keys, values, keys_out, values_out, fade, fade_t, marks, send,
    scratch, memory, message, mine, x, sems,
):
    arrival = fetched(message_in, message, sems.at[0])
    fetch = fetched(weights.at[info[0], pl.ds(1, 2)], mine, sems.at[1])
    slots, width = x.shape
    pairs = width // 128
    blocks = slots // CH
    owners = message.shape[0]
    cap = slots // owners
    per = cap * pairs
    arrival.wait()
    for j, part in enumerate(read_message(message, scratch, width)):
        x[:, 128 * j : 128 * (j + 1)] = part.astype(bf16)
    stores = [fetched(x, x_out, sems.at[2])]
    times = message[:, per : per + 8, :].astype(f32).reshape(owners * 8, 128).astype(bf16)
    r = iota((slots, owners * 8), 0)
    c = iota((slots, owners * 8), 1)
    expand = ones_where(((c & 7) == 0) & (8 * r >= cap * c) & (8 * r < cap * (c + 8)))
    wide = dot(expand, times)
    row = iota((slots, 128), 0).astype(f32)
    lane = iota((slots, 128), 1).astype(f32)
    s = row - cap * jnp.floor((row + 0.5) * (1.0 / cap))
    hit = (lane == s) | (lane == s + cap) | (lane == s + 2 * cap) | (lane == s + 3 * cap)
    own = jnp.where(hit, wide, 0.0).astype(bf16)
    tri = ones_where(iota((slots, slots), 0) >= iota((slots, slots), 1))
    running = dot(tri, own)
    kind = iota((128, 128), 0)
    head = iota((128, 128), 1)
    kind_t = iota((8, 128), 1)
    head_t = iota((8, 128), 0)
    rate = jnp.zeros((128, 128), f32)
    rate_t = jnp.zeros((8, 128), f32)
    for h in range(rates.shape[1]):
        value = rates[info[0], h]
        rate = jnp.where(head == h, value, rate)
        rate_t = jnp.where(head_t == h, value, rate_t)
    to_heads = jnp.where(kind < 2 * cap, -rate, jnp.where(kind < 4 * cap, -1.0, 0.0))
    fade[...] = dot(running, to_heads, NN, EXACT)
    to_heads = jnp.where(kind_t < 2 * cap, -rate_t, jnp.where(kind_t < 4 * cap, -1.0, 0.0))
    turned = dot(to_heads, running, NT, EXACT)
    for j in range(blocks):
        fade_t[j] = turned[:, CH * j : CH * (j + 1)]
    for j in range(blocks):
        for p in range(pairs):
            if j == 0:
                marks[j, p : p + 1, :] = jnp.zeros((1, 128), f32)
            else:
                marks[j, p : p + 1, :] = expanded(fade, slice(CH * j - 1, CH * j), p)
            end = slice(CH * j + CH - 1, CH * j + CH)
            marks[j, pairs + p : pairs + p + 1, :] = expanded(fade, end, p)
    fetch.wait()
    memory[...] = jnp.zeros(memory.shape, f32)
    mask = block_mask()

    def project(j, carry):
        rows = pl.ds(pl.multiple_of(j * CH, CH), CH)
        here = x[rows, :]
        k = dot(here, mine[0]).astype(bf16)
        v = dot(here, mine[1]).astype(bf16)
        keys[rows, :] = k
        values[rows, :] = v
        for p in range(pairs):
            cols = slice(128 * p, 128 * (p + 1))
            end = marks[blocks - 1, pairs + p : pairs + p + 1, :]
            kf = (k[:, cols].astype(f32) * jnp.exp(end - expanded(fade, rows, p))).astype(bf16)
            memory[p] += jnp.where(mask, dot(kf, v[:, cols], TN), 0.0)
        return carry

    lax.fori_loop(0, blocks, project, 0)
    stores.append(fetched(keys, keys_out, sems.at[3]))
    stores.append(fetched(values, values_out, sems.at[4]))
    write_state(send, memory, turned[:, slots - 1 : slots], pairs)
    for store in stores:
        store.wait()


def project_queries(info, x_in, weights, q8, mine, x, sems):
    arrival = fetched(x_in, x, sems.at[0])
    fetched(weights.at[info[0], 0], mine, sems.at[1]).wait()
    arrival.wait()

    def project(j, carry):
        rows = pl.ds(pl.multiple_of(j * CH, CH), CH)
        q8[rows, :] = (dot(x[rows, :], mine[...]).astype(bf16).astype(f32) * 0.125).astype(bf16)
        return carry

    lax.fori_loop(0, x.shape[0] // CH, project, 0)


def attend(q8, keys, values, fade, fade_t, marks, attended, states, memory):
    slots, width = q8.shape
    pairs = width // 128
    low, high = halves()
    mask = block_mask()
    memory[...] = jnp.zeros(memory.shape, f32)

    def block(j, carry):
        rows = pl.ds(pl.multiple_of(j * CH, CH), CH)
        edge = marks[j]
        for p in range(pairs):
            cols = slice(128 * p, 128 * (p + 1))
            start, end = edge[p : p + 1, :], edge[pairs + p : pairs + p + 1, :]
            qp, kp, vp = q8[rows, cols], keys[rows, cols], values[rows, cols]
            scores = dot(qp, stacked(kp, low, high), NT)
            fading, g = decay_pair(fade, fade_t, rows, j, p)
            mix = (scores * fading).astype(bf16)
            within = dot(mix, stacked(vp, low, high))
            now = memory[p]
            states[j, p] = folded(now).astype(bf16)
            lifted = (qp.astype(f32) * jnp.exp(g - start)).astype(bf16)
            attended[rows, cols] = within + dot(lifted, now.astype(bf16))
            kf = (kp.astype(f32) * jnp.exp(end - g)).astype(bf16)
            memory[p] = jnp.exp(end - start) * now + jnp.where(mask, dot(kf, vp, TN), 0.0)
        return carry

    lax.fori_loop(0, slots // CH, block, 0)


def turn(info, q8, fade, fade_t, attended, x_in, weights, message_in, partner, *rest):
    received = rest[:-15]
    (
        encoded, grads, grad_full, incoming, send,
        scratch, message, mine, x, wide, narrow, states, memory, sems, out_sems,
    ) = rest[-15:]
    arrival = fetched(message_in, message, sems.at[0])
    fetch = fetched(weights.at[info[0], 3], mine, sems.at[1])
    rows_in = fetched(x_in, x, sems.at[2])
    slots, width = x.shape
    pairs = width // 128
    blocks = slots // CH
    mask = block_mask()
    for p, state in enumerate(gathered_state(info[1].astype(f32), partner, received, pairs)):
        incoming[p] = state
        states[p] = unfolded(state, mask).astype(bf16)
    memory[...] = jnp.zeros(memory.shape, f32)
    arrival.wait()
    for j, part in enumerate(read_message(message, scratch, width)):
        grads[:, 128 * j : 128 * (j + 1)] = part.astype(bf16)
    fetch.wait()
    rows_in.wait()
    sender = Sender(encoded, wide, narrow, out_sems, pairs)

    def block(j, carry):
        rows = pl.ds(pl.multiple_of(j * CH, CH), CH)
        values, lifts = [], []
        square = jnp.zeros((CH, 1), f32)
        for p in range(pairs):
            cols = slice(128 * p, 128 * (p + 1))
            lifted = (q8[rows, cols].astype(f32) * jnp.exp(expanded(fade, rows, p))).astype(bf16)
            lifts.append(lifted)
            value = attended[rows, cols] + dot(lifted, states[p])
            values.append(value)
            square += jnp.sum(value * value, axis=1, keepdims=True)
        here = jnp.concatenate(values, axis=1)
        scale = lax.rsqrt(square * (1.0 / width) + 1e-06)
        normed = (here * scale).astype(bf16)
        sender.put(j, x[rows, :].astype(f32) + dot(normed, mine[...]))
        grad = dot(grads[rows, :], mine[...], NT).astype(bf16).astype(f32)
        along = jnp.mean(here * grad, axis=1, keepdims=True)
        da = (scale * grad - here * (scale * scale * scale * along)).astype(bf16)
        grad_full[rows, :] = da
        for p in range(pairs):
            cols = slice(128 * p, 128 * (p + 1))
            memory[p] += jnp.where(mask, dot(lifts[p], da[:, cols], TN), 0.0)
        return carry

    lax.fori_loop(0, blocks, block, 0)
    write_state(send, memory, fade_t[blocks - 1][:, CH - 1 : CH], pairs)
    sender.finish(blocks)


def backward_local(
    q8, keys, values, fade, fade_t, marks, grad_full, states, incoming,
    grad_q, grad_keys, grad_values, memory,
):
    slots, width = q8.shape
    pairs = width // 128
    blocks = slots // CH
    low, high = halves()
    lower = iota((CH, 128), 1) < 64
    mask = block_mask()
    memory[...] = jnp.zeros(memory.shape, f32)

    def block(i, carry):
        j = blocks - 1 - i
        rows = pl.ds(pl.multiple_of(j * CH, CH), CH)
        edge = marks[j]
        for p in range(pairs):
            cols = slice(128 * p, 128 * (p + 1))
            start, end = edge[p : p + 1, :], edge[pairs + p : pairs + p + 1, :]
            qp, kp, vp = q8[rows, cols], keys[rows, cols], values[rows, cols]
            da = grad_full[rows, cols]
            ks, vs = stacked(kp, low, high), stacked(vp, low, high)
            fading, g = decay_pair(fade, fade_t, rows, j, p)
            mix = (dot(qp, ks, NT) * fading).astype(bf16)
            grad_scores = (dot(da, vs, NT) * fading).astype(bf16)
            lift = jnp.exp(g - start)
            fall = jnp.exp(end - g)
            state = states[j, p].astype(f32) + jnp.exp(start) * incoming[p]
            state = unfolded(state, mask).astype(bf16)
            grad_q[rows, cols] = (
                0.125 * (dot(grad_scores, ks) + lift * dot(da, state, NT))
            ).astype(bf16)
            gk = dot(grad_scores, qp, TN)
            gv = dot(mix, da, TN)
            now = memory[p]
            narrow = now.astype(bf16)
            kf = (kp.astype(f32) * fall).astype(bf16)
            grad_keys[rows, cols] = jnp.where(lower, gk[0:CH], gk[CH:]) + fall * dot(vp, narrow, NT)
            grad_values[rows, cols] = jnp.where(lower, gv[0:CH], gv[CH:]) + dot(kf, narrow)
            lifted = (qp.astype(f32) * lift).astype(bf16)
            memory[p] = jnp.exp(end - start) * now + jnp.where(mask, dot(lifted, da, TN), 0.0)
        return carry

    lax.fori_loop(0, blocks, block, 0)


def project_back(info, grads, grad_q, weights, partial, mine, sem):
    fetched(weights.at[info[0], 0], mine, sem).wait()

    def project(j, carry):
        rows = pl.ds(pl.multiple_of(j * CH, CH), CH)
        partial[rows, :] = grads[rows, :].astype(f32) + dot(grad_q[rows, :], mine[...], NT)
        return carry

    lax.fori_loop(0, grads.shape[0] // CH, project, 0)


def backward_finish(
    info, partial, grad_keys, grad_values, keys, values, fade, marks, weights, partner, *rest
):
    received = rest[:-9]
    out, mine, wide, narrow, states, gk, gv, sem, out_sems = rest[-9:]
    fetch = fetched(weights.at[info[0], pl.ds(1, 2)], mine, sem)
    slots, width = partial.shape
    pairs = width // 128
    blocks = slots // CH
    mask = block_mask()
    arrived = gathered_state((1 - info[1]).astype(f32), partner, received, pairs)
    for p, state in enumerate(arrived):
        states[p] = unfolded(state, mask).astype(bf16)
    sender = Sender(out, wide, narrow, out_sems, pairs)
    fetch.wait()

    def block(j, carry):
        rows = pl.ds(pl.multiple_of(j * CH, CH), CH)
        for p in range(pairs):
            cols = slice(128 * p, 128 * (p + 1))
            end = marks[blocks - 1, pairs + p : pairs + p + 1, :]
            fall = jnp.exp(end - expanded(fade, rows, p))
            kf = (keys[rows, cols].astype(f32) * fall).astype(bf16)
            state = states[p]
            gk[:, cols] = (grad_keys[rows, cols] + fall * dot(values[rows, cols], state, NT)).astype(bf16)
            gv[:, cols] = (grad_values[rows, cols] + dot(kf, state)).astype(bf16)
        sender.put(j, partial[rows, :] + dot(gk[...], mine[0], NT) + dot(gv[...], mine[1], NT))
        return carry

    lax.fori_loop(0, blocks, block, 0)
    sender.finish(blocks)


def swapped(value, axis):
    return lax.ppermute(value, axis, [(i, i ^ 1) for i in range(lax.axis_size(axis))])


def exchange(value, axis, sign):
    count = lax.axis_size(axis)
    return [
        lax.ppermute(
            value, axis, [(i, i + sign * k) for i in range(count) if 0 <= i + sign * k < count]
        )
        for k in range(2, count, 2)
    ]


def regroup(value):
    return lax.all_to_all(value, "log", split_axis=0, concat_axis=0, tiled=True)


def shards(events, owner_ids, elapsed, resets, decay_rates, weights, cotangent):
    rows, width = events.shape[2:]
    owners = lax.axis_size("log")
    cap = 5 * rows // (4 * owners)
    slots = owners * cap
    pairs = width // 128
    blocks = slots // CH
    per = cap * pairs
    flat = pltpu.VMEM((slots * pairs, 128), f32)
    state_vmem = pltpu.VMEM((pairs, 128, 128), f32)
    state_msg = ((64 * pairs + 8, 128), bf16)
    wide_msg = ((owners, per, 128), bf16)
    wide16, wide32 = ((slots, width), bf16), ((slots, width), f32)

    tower = lax.axis_index("log") // (owners // decay_rates.shape[0])
    info = jnp.stack([tower, lax.axis_index("ctx") % 2]).astype(jnp.int32)

    message, place = call(
        pack_events,
        [((owners, per + 8, 128), bf16), ((slots, rows), bf16)],
        [
            owner_ids.reshape(1, rows),
            events.reshape(rows, width),
            elapsed.reshape(1, rows),
            resets.reshape(1, rows),
        ],
        [
            flat,
            pltpu.VMEM((1, rows), jnp.int32),
            pltpu.VMEM((rows, width), bf16),
            pltpu.VMEM((1, rows), f32),
            pltpu.VMEM((1, rows), f32),
            pltpu.SemaphoreType.DMA((4,)),
        ],
        {0: HBM, 1: HBM, 2: HBM, 3: HBM},
    )
    events_in = regroup(message)
    message, back = call(
        pack_grads,
        [wide_msg, ((rows, slots), bf16)],
        [info, place, cotangent.reshape(rows, width)],
        [flat],
        {0: SMEM},
    )
    grads_in = regroup(message)
    one = pltpu.VMEM((width, width), bf16)
    two = pltpu.VMEM((2, width, width), bf16)
    sem = pltpu.SemaphoreType.DMA
    half_states = ((pairs, 64, 128), f32)
    flat_msg = ((slots * pairs, 128), bf16)
    block_wide = pltpu.VMEM((CH * pairs, 128), f32)
    flat_narrow = pltpu.VMEM(*flat_msg)
    rows16 = pltpu.VMEM(*wide16)
    narrow_states = pltpu.VMEM((pairs, 128, 128), bf16)
    x, keys, values, keys_far, values_far, fade, fade_t, marks, send = call(
        forward_state,
        [
            wide16, wide16, wide16, wide16, wide16, ((slots, 128), f32), ((blocks, 8, 128), f32),
            ((blocks, 2 * pairs, 128), f32), state_msg,
        ],
        [info, decay_rates, events_in, weights],
        [flat, state_vmem, pltpu.VMEM((owners, per + 8, 128), bf16), two, rows16, sem((5,))],
        {0: SMEM, 1: SMEM, 2: HBM, 3: HBM},
        (0, 3, 4),
    )
    partner = swapped(send, "ctx")
    (q8,) = call(
        project_queries,
        [wide16],
        [info, x, weights],
        [one, rows16, sem((2,))],
        {0: SMEM, 1: HBM, 2: HBM},
    )
    (joined,) = call(join_ahead, [state_msg], [info, send, partner], (), {0: SMEM})
    received = exchange(joined, "ctx", 1)
    attended, kept = call(
        attend,
        [wide32, ((blocks, pairs, 64, 128), bf16)],
        [q8, keys, values, fade, fade_t, marks],
        [state_vmem],
    )
    message, grads, grad_full, incoming, send = call(
        turn,
        [flat_msg, wide16, wide16, half_states, state_msg],
        [info, q8, fade, fade_t, attended, x, weights, grads_in, partner, *received],
        [
            flat, pltpu.VMEM(*wide_msg), one, rows16, block_wide, flat_narrow, narrow_states,
            state_vmem, sem((3,)), sem((blocks,)),
        ],
        {0: SMEM, 5: HBM, 6: HBM, 7: HBM},
        (0,),
    )
    partner = swapped(send, "ctx")
    encoded_in = regroup(message.reshape(owners, per, 128))
    grad_q, grad_keys, grad_values = call(
        backward_local,
        [wide16, wide32, wide32],
        [q8, keys_far, values_far, fade, fade_t, marks, grad_full, kept, incoming],
        [state_vmem],
    )
    (joined,) = call(join_back, [state_msg], [info, send, partner], (), {0: SMEM})
    received = exchange(joined, "ctx", -1)
    (partial,) = call(
        project_back, [wide32], [info, grads, grad_q, weights], [one, sem], {0: SMEM, 3: HBM}
    )
    (message,) = call(
        backward_finish,
        [flat_msg],
        [
            info, partial, grad_keys, grad_values, keys_far, values_far, fade, marks, weights,
            partner, *received,
        ],
        [
            two, block_wide, flat_narrow, narrow_states,
            pltpu.VMEM((CH, width), bf16), pltpu.VMEM((CH, width), bf16), sem, sem((blocks,)),
        ],
        {0: SMEM, 8: HBM},
        (0,),
    )
    grad_in = regroup(message.reshape(owners, per, 128))
    (encoded,) = call(unpack_rows, [((rows, width), bf16)], [back, encoded_in], [flat])
    (grad,) = call(unpack_rows, [((rows, width), bf16)], [back, grad_in], [flat])
    return encoded.reshape(events.shape), grad.reshape(events.shape)


def solution(mesh):
    wide = P("ctx", "log", None, None)
    flat = P("ctx", "log", None)
    return jax.shard_map(
        shards,
        mesh=mesh,
        in_specs=(wide, wide, flat, flat, P(), P(), wide),
        out_specs=(wide, wide),
        check_vma=False,
    )
```

```python
import jax
import jax.numpy as jnp
from jax import lax
from jax.experimental import pallas as pl
from jax.experimental.pallas import tpu as pltpu
from jax.sharding import PartitionSpec as P


bf16 = jnp.bfloat16
f32 = jnp.float32
CH = 128
NN = (((1,), (0,)), ((), ()))
NT = (((1,), (1,)), ((), ()))
TN = (((0,), (0,)), ((), ()))
EXACT = lax.Precision.HIGHEST
LIMIT = 16 << 20
NX = 4


def dot(a, b, dims=NN, precision=None):
    return lax.dot_general(a, b, dims, preferred_element_type=f32, precision=precision)


def iota(shape, dim):
    return lax.broadcasted_iota(jnp.int32, shape, dim)


def ones_where(cond, dtype=bf16):
    return jnp.where(cond, 1.0, 0.0).astype(dtype)


VMEM = pl.BlockSpec(memory_space=pltpu.VMEM)
SMEM = pl.BlockSpec(memory_space=pltpu.SMEM)
HBM = pl.BlockSpec(memory_space=pltpu.HBM)
ANY = pl.BlockSpec(memory_space=pl.ANY)


def call(body, outs, ins, scratch=(), spaces=None, out_hbm=()):
    ins = [
        pltpu.with_memory_space_constraint(v, pltpu.HBM) if (spaces or {}).get(i) is HBM else v
        for i, v in enumerate(ins)
    ]
    return pl.pallas_call(
        body,
        out_shape=[
            pltpu.HBM(s, d) if i in out_hbm else jax.ShapeDtypeStruct(s, d)
            for i, (s, d) in enumerate(outs)
        ],
        in_specs=[(spaces or {}).get(i, VMEM) for i in range(len(ins))],
        out_specs=[HBM if i in out_hbm else VMEM for i in range(len(outs))],
        scratch_shapes=list(scratch),
        compiler_params=pltpu.CompilerParams(vmem_limit_bytes=LIMIT),
    )(*ins)


def write_rows(scratch, rows_of, parts):
    count = scratch.shape[0] // parts
    for j in range(parts):
        scratch[pl.ds(j, count, stride=parts), :] = rows_of(j)


def write_message(message, scratch, rows_of, width):
    write_rows(scratch, rows_of, width // 128)
    owners = message.shape[0]
    per = scratch.shape[0] // owners
    message[:, 0:per, :] = scratch[...].reshape(owners, per, 128).astype(bf16)


def read_message(message, scratch, width):
    parts = width // 128
    count = scratch.shape[0] // parts
    owners = message.shape[0]
    per = scratch.shape[0] // owners
    scratch[...] = message[:, 0:per, :].astype(f32).reshape(scratch.shape)
    return [scratch[pl.ds(j, count, stride=parts), :] for j in range(parts)]


class Sender:
    def __init__(self, out, wide, narrow, sems, parts):
        self.out, self.wide, self.narrow, self.sems, self.parts = out, wide, narrow, sems, parts

    def copy(self, j):
        size = CH * self.parts
        span = pl.ds(pl.multiple_of(j * size, size), size)
        return pltpu.make_async_copy(self.narrow.at[span, :], self.out.at[span, :], self.sems.at[j])

    def put(self, j, value):
        size = CH * self.parts
        for p in range(self.parts):
            self.wide[pl.ds(p, CH, stride=self.parts), :] = value[:, 128 * p : 128 * (p + 1)]
        span = pl.ds(pl.multiple_of(j * size, size), size)
        self.narrow[span, :] = self.wide[...].astype(bf16)
        self.copy(j).start()

    def finish(self, blocks):
        for j in range(blocks):
            self.copy(j).wait()


def fetched(source, target, sem):
    copy = pltpu.make_async_copy(source, target, sem)
    copy.start()
    return copy


def rows_copy(source, target, sems, j):
    rows = pl.ds(pl.multiple_of(j * CH, CH), CH)
    return pltpu.make_async_copy(source.at[rows, :], target.at[rows, :], sems.at[j])


def expanded(fade, rows, p):
    here = fade[rows, :]
    shape = (here.shape[0], 128)
    return jnp.where(
        iota(shape, 1) < 64,
        jnp.broadcast_to(here[:, 2 * p : 2 * p + 1], shape),
        jnp.broadcast_to(here[:, 2 * p + 1 : 2 * p + 2], shape),
    )


def pack_events(
    owner_in, events_in, elapsed_in, resets_in, message, spots,
    scratch, place, owner, events, elapsed, resets, sems,
):
    copies = [
        pltpu.make_async_copy(source, target, sems.at[i])
        for i, (source, target) in enumerate(
            (
                (owner_in, owner),
                (elapsed_in, elapsed),
                (resets_in, resets),
                (events_in, events),
            )
        )
    ]
    for copy in copies:
        copy.start()
    copies[0].wait()
    rows, width = events.shape
    owners = message.shape[0]
    slots = place.shape[0]
    cap = slots // owners
    own = owner[...]
    hit = iota((owners, rows), 0) == own
    earlier = ones_where(iota((rows, rows), 0) < iota((rows, rows), 1))
    before = dot(ones_where(hit), earlier)
    rank = jnp.sum(jnp.where(hit, before, 0.0), axis=0, keepdims=True).astype(jnp.int32)
    spots[0:1, :] = own
    spots[1:2, :] = rank
    place[...] = ones_where(iota((slots, rows), 0) == own * cap + rank)
    for copy in copies[1:]:
        copy.wait()
    write_message(
        message,
        scratch,
        lambda j: dot(place[...], events[:, 128 * j : 128 * (j + 1)]),
        width,
    )
    lanes = iota((128, rows), 0)
    times = jnp.zeros((owners, 128), f32)
    for k, ref in enumerate((elapsed, resets)):
        value = ref[...]
        high = value.astype(bf16).astype(f32)
        for m, part in enumerate((high, value - high)):
            spot = ones_where(lanes == rank + cap * (2 * k + m))
            times += dot(jnp.where(hit, part, 0.0).astype(bf16), spot, NT)
    spread = ones_where(iota((owners * 8, owners), 0) == 8 * iota((owners * 8, owners), 1))
    extra = dot(spread, times.astype(bf16)).reshape(owners, 8, 128)
    per = scratch.shape[0] // owners
    message[:, per : per + 8, :] = extra.astype(bf16)


def pack_grads(info, spots, grads, *rest):
    pieces, (back, back_far, scratch, narrow, turned, turned_far, sems) = rest[:NX], rest[NX:]
    rows, width = grads.shape
    slots = turned.shape[1]
    own, rank = spots[0:1, :], spots[1:2, :]
    count = pieces[0].shape[0]
    cap = slots // (count * NX)
    z, x = own >> (NX.bit_length() - 1), own & (NX - 1)
    place = ones_where(iota((slots, rows), 0) == (((x - info[2]) & (NX - 1)) * count + z) * cap + rank)
    write_rows(
        scratch, lambda j: dot(place, grads[:, 128 * j : 128 * (j + 1)]), width // 128
    )
    narrow[...] = scratch[...].reshape(narrow.shape).astype(bf16)
    copies = [
        fetched(narrow.at[k], pieces[k], sems.at[k]) for k in range(NX)
    ]
    same = ones_where(iota((rows, rows), 0) == iota((rows, rows), 1))
    place = ones_where(iota((slots, rows), 0) == own * cap + rank)
    turned[...] = dot(same, place, NT).astype(bf16)
    copies.append(fetched(turned, back, sems.at[NX]))
    place = ones_where(iota((slots, rows), 0) == (((info[2] - x) & (NX - 1)) * count + z) * cap + rank)
    turned_far[...] = dot(same, place, NT).astype(bf16)
    copies.append(fetched(turned_far, back_far, sems.at[NX + 1]))
    for copy in copies:
        copy.wait()


def merge_pieces(*rest):
    pieces, (out, sems) = rest[:NX], rest[NX:]
    copies = [fetched(pieces[k], out.at[:, k], sems.at[k]) for k in range(NX)]
    for copy in copies:
        copy.wait()


def split_pieces(info, merged, *rest):
    pieces, sems = rest[:NX], rest[NX]
    copies = [
        fetched(merged.at[:, (info[2] + k) & (NX - 1)], pieces[k], sems.at[k]) for k in range(NX)
    ]
    for copy in copies:
        copy.wait()


def unpack_pieces(back, *rest):
    pieces, (out, scratch) = rest[:NX], rest[NX:]
    width = out.shape[1]
    parts = width // 128
    size = scratch.shape[0] // NX
    for k in range(NX):
        scratch[size * k : size * (k + 1), :] = pieces[k][...].astype(f32).reshape(size, 128)
    for j in range(parts):
        part = scratch[pl.ds(j, scratch.shape[0] // parts, stride=parts), :].astype(bf16)
        out[:, 128 * j : 128 * (j + 1)] = dot(back[...], part).astype(bf16)


def unpack_rows(back, message, out, scratch):
    width = out.shape[1]
    for j, part in enumerate(read_message(message, scratch, width)):
        out[:, 128 * j : 128 * (j + 1)] = dot(back[...], part.astype(bf16)).astype(bf16)


def halves():
    low = ones_where(iota((CH, 128), 1) < 64)
    return low, ones_where(iota((CH, 128), 1) >= 64)


def block_mask():
    return (iota((128, 128), 0) < 64) == (iota((128, 128), 1) < 64)


def stacked(value, low, high):
    return jnp.concatenate([value * low, value * high], axis=0)


def decay_pair(fade, fade_t, rows, j, p):
    causal = iota((CH, CH), 0) >= iota((CH, CH), 1)
    both, wide = [], []
    turned = fade_t[j]
    here = fade[rows, :]
    for h in (2 * p, 2 * p + 1):
        column = jnp.broadcast_to(here[:, h : h + 1], (CH, CH))
        wide.append(column)
        spread = column - turned[h : h + 1, :]
        both.append(jnp.exp(jnp.where(causal, spread, -1e30)))
    return jnp.concatenate(both, axis=1), jnp.where(iota((CH, CH), 1) < 64, wide[0], wide[1])


def folded(full):
    return full[0:64, :] + full[64:128, :]


def unfolded(half, mask):
    return jnp.where(mask, jnp.concatenate([half, half], axis=0), 0.0)


def write_state(send, state, last, pairs):
    for p in range(pairs):
        send[64 * p : 64 * (p + 1), :] = folded(state[p]).astype(bf16)
    write_marks(send, last, pairs)


def write_marks(send, last, pairs):
    last = jnp.broadcast_to(last, (8, 128))
    high = last.astype(bf16).astype(f32)
    lane = iota(last.shape, 1)
    send[64 * pairs : 64 * pairs + 8, :] = jnp.where(lane < 64, high, last - high).astype(bf16)


def read_marks(ref, pairs):
    marks = ref[64 * pairs : 64 * pairs + 8, :].astype(f32)
    return marks[:, 0:1] + marks[:, 64:65]


def lane_factors(log, p):
    return jnp.exp(
        jnp.where(
            iota((1, 128), 1) < 64,
            jnp.broadcast_to(log[2 * p : 2 * p + 1, :], (1, 128)),
            jnp.broadcast_to(log[2 * p + 1 : 2 * p + 2, :], (1, 128)),
        )
    )


def join_pair(near, far, out, pairs):
    log = read_marks(near, pairs)
    for p in range(pairs):
        rows = slice(64 * p, 64 * (p + 1))
        joined = near[rows, :].astype(f32) + lane_factors(log, p) * far[rows, :].astype(f32)
        out[rows, :] = joined.astype(bf16)
    write_marks(out, log + read_marks(far, pairs), pairs)


def join_ahead(info, own, other, out):
    join(info[1] == 1, own, other, out)


def join_back(info, own, other, out):
    join(info[1] == 0, own, other, out)


def join(own_is_near, own, other, out):
    pairs = own.shape[0] // 64

    @pl.when(own_is_near)
    def _():
        join_pair(own, other, out, pairs)

    @pl.when(jnp.logical_not(own_is_near))
    def _():
        join_pair(other, own, out, pairs)


def gathered_state(partner_counts, partner, received, pairs):
    log = read_marks(partner, pairs) * partner_counts
    total = [partner[64 * p : 64 * (p + 1), :].astype(f32) * partner_counts for p in range(pairs)]
    for ref in received:
        for p in range(pairs):
            total[p] += lane_factors(log, p) * ref[64 * p : 64 * (p + 1), :].astype(f32)
        log = log + read_marks(ref, pairs)
    return total


def forward_state(
    info, rates, message_in, weights,
    x_out, keys, values, keys_out, values_out, fade, fade_t, marks, send,
    scratch, memory, message, mine, x, sems,
):
    arrival = fetched(message_in, message, sems.at[0])
    fetch = fetched(weights.at[info[0], pl.ds(1, 2)], mine, sems.at[1])
    slots, width = x.shape
    pairs = width // 128
    blocks = slots // CH
    owners = message.shape[0]
    cap = slots // owners
    per = cap * pairs
    arrival.wait()
    for j, part in enumerate(read_message(message, scratch, width)):
        x[:, 128 * j : 128 * (j + 1)] = part.astype(bf16)
    stores = [fetched(x, x_out, sems.at[2])]
    times = message[:, per : per + 8, :].astype(f32).reshape(owners * 8, 128).astype(bf16)
    r = iota((slots, owners * 8), 0)
    c = iota((slots, owners * 8), 1)
    expand = ones_where(((c & 7) == 0) & (8 * r >= cap * c) & (8 * r < cap * (c + 8)))
    wide = dot(expand, times)
    row = iota((slots, 128), 0).astype(f32)
    lane = iota((slots, 128), 1).astype(f32)
    s = row - cap * jnp.floor((row + 0.5) * (1.0 / cap))
    hit = (lane == s) | (lane == s + cap) | (lane == s + 2 * cap) | (lane == s + 3 * cap)
    own = jnp.where(hit, wide, 0.0).astype(bf16)
    tri = ones_where(iota((slots, slots), 0) >= iota((slots, slots), 1))
    running = dot(tri, own)
    kind = iota((128, 128), 0)
    head = iota((128, 128), 1)
    kind_t = iota((8, 128), 1)
    head_t = iota((8, 128), 0)
    rate = jnp.zeros((128, 128), f32)
    rate_t = jnp.zeros((8, 128), f32)
    for h in range(rates.shape[1]):
        value = rates[info[0], h]
        rate = jnp.where(head == h, value, rate)
        rate_t = jnp.where(head_t == h, value, rate_t)
    to_heads = jnp.where(kind < 2 * cap, -rate, jnp.where(kind < 4 * cap, -1.0, 0.0))
    fade[...] = dot(running, to_heads, NN, EXACT)
    to_heads = jnp.where(kind_t < 2 * cap, -rate_t, jnp.where(kind_t < 4 * cap, -1.0, 0.0))
    turned = dot(to_heads, running, NT, EXACT)
    for j in range(blocks):
        fade_t[j] = turned[:, CH * j : CH * (j + 1)]
    for j in range(blocks):
        for p in range(pairs):
            if j == 0:
                marks[j, p : p + 1, :] = jnp.zeros((1, 128), f32)
            else:
                marks[j, p : p + 1, :] = expanded(fade, slice(CH * j - 1, CH * j), p)
            end = slice(CH * j + CH - 1, CH * j + CH)
            marks[j, pairs + p : pairs + p + 1, :] = expanded(fade, end, p)
    fetch.wait()
    memory[...] = jnp.zeros(memory.shape, f32)
    mask = block_mask()

    def project(j, carry):
        rows = pl.ds(pl.multiple_of(j * CH, CH), CH)
        here = x[rows, :]
        k = dot(here, mine[0]).astype(bf16)
        v = dot(here, mine[1]).astype(bf16)
        keys[rows, :] = k
        values[rows, :] = v
        for p in range(pairs):
            cols = slice(128 * p, 128 * (p + 1))
            end = marks[blocks - 1, pairs + p : pairs + p + 1, :]
            kf = (k[:, cols].astype(f32) * jnp.exp(end - expanded(fade, rows, p))).astype(bf16)
            memory[p] += jnp.where(mask, dot(kf, v[:, cols], TN), 0.0)
        return carry

    lax.fori_loop(0, blocks, project, 0)
    stores.append(fetched(keys, keys_out, sems.at[3]))
    stores.append(fetched(values, values_out, sems.at[4]))
    write_state(send, memory, turned[:, slots - 1 : slots], pairs)
    for store in stores:
        store.wait()


def project_queries(info, x_in, weights, q8, mine, x, sems):
    arrival = fetched(x_in, x, sems.at[0])
    fetched(weights.at[info[0], 0], mine, sems.at[1]).wait()
    arrival.wait()

    def project(j, carry):
        rows = pl.ds(pl.multiple_of(j * CH, CH), CH)
        q8[rows, :] = (dot(x[rows, :], mine[...]).astype(bf16).astype(f32) * 0.125).astype(bf16)
        return carry

    lax.fori_loop(0, x.shape[0] // CH, project, 0)


def attend(
    q8, keys, values, fade, fade_t, marks, attended_out, states, memory, attended, sems
):
    slots, width = q8.shape
    pairs = width // 128
    low, high = halves()
    mask = block_mask()
    memory[...] = jnp.zeros(memory.shape, f32)

    def block(j, carry):
        rows = pl.ds(pl.multiple_of(j * CH, CH), CH)
        edge = marks[j]
        for p in range(pairs):
            cols = slice(128 * p, 128 * (p + 1))
            start, end = edge[p : p + 1, :], edge[pairs + p : pairs + p + 1, :]
            qp, kp, vp = q8[rows, cols], keys[rows, cols], values[rows, cols]
            scores = dot(qp, stacked(kp, low, high), NT)
            fading, g = decay_pair(fade, fade_t, rows, j, p)
            mix = (scores * fading).astype(bf16)
            within = dot(mix, stacked(vp, low, high))
            now = memory[p]
            states[j, p] = folded(now).astype(bf16)
            lifted = (qp.astype(f32) * jnp.exp(g - start)).astype(bf16)
            attended[rows, cols] = within + dot(lifted, now.astype(bf16))
            kf = (kp.astype(f32) * jnp.exp(end - g)).astype(bf16)
            memory[p] = jnp.exp(end - start) * now + jnp.where(mask, dot(kf, vp, TN), 0.0)
        rows_copy(attended, attended_out, sems, j).start()
        return carry

    lax.fori_loop(0, slots // CH, block, 0)
    for j in range(slots // CH):
        rows_copy(attended, attended_out, sems, j).wait()


def turn(info, q8, fade, fade_t, attended_in, x_in, weights, message_in, partner, *rest):
    received = rest[:-17]
    (
        encoded, grads_out, grad_full, incoming, send,
        scratch, message, mine, x, attended, grads,
        wide, narrow, states, memory, sems, out_sems,
    ) = rest[-17:]
    arrivals = [
        fetched(message_in.at[:, (info[2] - k) & (NX - 1)], message.at[:, k], sems.at[2 + k])
        for k in range(NX)
    ]
    fetch = fetched(weights.at[info[0], 3], mine, sems.at[0])
    rows_in = fetched(x_in, x, sems.at[1])
    attended_here = fetched(attended_in, attended, sems.at[2 + NX])
    slots, width = x.shape
    pairs = width // 128
    blocks = slots // CH
    mask = block_mask()
    for p, state in enumerate(gathered_state(info[1].astype(f32), partner, received, pairs)):
        incoming[p] = state
        states[p] = unfolded(state, mask).astype(bf16)
    memory[...] = jnp.zeros(memory.shape, f32)
    for arrival in arrivals:
        arrival.wait()
    scratch[...] = message[...].astype(f32).reshape(scratch.shape)
    for j in range(pairs):
        part = scratch[pl.ds(j, slots, stride=pairs), :]
        grads[:, 128 * j : 128 * (j + 1)] = part.astype(bf16)
    fetch.wait()
    rows_in.wait()
    attended_here.wait()
    store = fetched(grads, grads_out, sems.at[3 + NX])
    sender = Sender(encoded, wide, narrow, out_sems, pairs)

    def block(j, carry):
        rows = pl.ds(pl.multiple_of(j * CH, CH), CH)
        values, lifts = [], []
        square = jnp.zeros((CH, 1), f32)
        for p in range(pairs):
            cols = slice(128 * p, 128 * (p + 1))
            lifted = (q8[rows, cols].astype(f32) * jnp.exp(expanded(fade, rows, p))).astype(bf16)
            lifts.append(lifted)
            value = attended[rows, cols] + dot(lifted, states[p])
            values.append(value)
            square += jnp.sum(value * value, axis=1, keepdims=True)
        here = jnp.concatenate(values, axis=1)
        scale = lax.rsqrt(square * (1.0 / width) + 1e-06)
        normed = (here * scale).astype(bf16)
        sender.put(j, x[rows, :].astype(f32) + dot(normed, mine[...]))
        grad = dot(grads[rows, :], mine[...], NT).astype(bf16).astype(f32)
        along = jnp.mean(here * grad, axis=1, keepdims=True)
        da = (scale * grad - here * (scale * scale * scale * along)).astype(bf16)
        grad_full[rows, :] = da
        for p in range(pairs):
            cols = slice(128 * p, 128 * (p + 1))
            memory[p] += jnp.where(mask, dot(lifts[p], da[:, cols], TN), 0.0)
        return carry

    lax.fori_loop(0, blocks, block, 0)
    write_state(send, memory, fade_t[blocks - 1][:, CH - 1 : CH], pairs)
    sender.finish(blocks)
    store.wait()


def backward_local(
    q8, keys, values, fade, fade_t, marks, grad_full, states, incoming,
    grad_q, grad_keys, grad_values, memory,
):
    slots, width = q8.shape
    pairs = width // 128
    blocks = slots // CH
    low, high = halves()
    lower = iota((CH, 128), 1) < 64
    mask = block_mask()
    memory[...] = jnp.zeros(memory.shape, f32)

    def block(i, carry):
        j = blocks - 1 - i
        rows = pl.ds(pl.multiple_of(j * CH, CH), CH)
        edge = marks[j]
        for p in range(pairs):
            cols = slice(128 * p, 128 * (p + 1))
            start, end = edge[p : p + 1, :], edge[pairs + p : pairs + p + 1, :]
            qp, kp, vp = q8[rows, cols], keys[rows, cols], values[rows, cols]
            da = grad_full[rows, cols]
            ks, vs = stacked(kp, low, high), stacked(vp, low, high)
            fading, g = decay_pair(fade, fade_t, rows, j, p)
            mix = (dot(qp, ks, NT) * fading).astype(bf16)
            grad_scores = (dot(da, vs, NT) * fading).astype(bf16)
            lift = jnp.exp(g - start)
            fall = jnp.exp(end - g)
            state = states[j, p].astype(f32) + jnp.exp(start) * incoming[p]
            state = unfolded(state, mask).astype(bf16)
            grad_q[rows, cols] = (
                0.125 * (dot(grad_scores, ks) + lift * dot(da, state, NT))
            ).astype(bf16)
            gk = dot(grad_scores, qp, TN)
            gv = dot(mix, da, TN)
            now = memory[p]
            narrow = now.astype(bf16)
            kf = (kp.astype(f32) * fall).astype(bf16)
            grad_keys[rows, cols] = jnp.where(lower, gk[0:CH], gk[CH:]) + fall * dot(vp, narrow, NT)
            grad_values[rows, cols] = jnp.where(lower, gv[0:CH], gv[CH:]) + dot(kf, narrow)
            lifted = (qp.astype(f32) * lift).astype(bf16)
            memory[p] = jnp.exp(end - start) * now + jnp.where(mask, dot(lifted, da, TN), 0.0)
        return carry

    lax.fori_loop(0, blocks, block, 0)


def project_back(info, grads_in, grad_q, weights, partial, mine, grads, sems):
    arrival = fetched(grads_in, grads, sems.at[0])
    fetched(weights.at[info[0], 0], mine, sems.at[1]).wait()
    arrival.wait()

    def project(j, carry):
        rows = pl.ds(pl.multiple_of(j * CH, CH), CH)
        partial[rows, :] = grads[rows, :].astype(f32) + dot(grad_q[rows, :], mine[...], NT)
        return carry

    lax.fori_loop(0, grads.shape[0] // CH, project, 0)


def backward_finish(
    info, partial, grad_keys, grad_values, keys, values, fade, marks, weights, partner, *rest
):
    received = rest[:-9]
    out, mine, wide, narrow, states, gk, gv, sem, out_sems = rest[-9:]
    fetch = fetched(weights.at[info[0], pl.ds(1, 2)], mine, sem)
    slots, width = partial.shape
    pairs = width // 128
    blocks = slots // CH
    mask = block_mask()
    arrived = gathered_state((1 - info[1]).astype(f32), partner, received, pairs)
    for p, state in enumerate(arrived):
        states[p] = unfolded(state, mask).astype(bf16)
    sender = Sender(out, wide, narrow, out_sems, pairs)
    fetch.wait()

    def block(j, carry):
        rows = pl.ds(pl.multiple_of(j * CH, CH), CH)
        for p in range(pairs):
            cols = slice(128 * p, 128 * (p + 1))
            end = marks[blocks - 1, pairs + p : pairs + p + 1, :]
            fall = jnp.exp(end - expanded(fade, rows, p))
            kf = (keys[rows, cols].astype(f32) * fall).astype(bf16)
            state = states[p]
            gk[:, cols] = (grad_keys[rows, cols] + fall * dot(values[rows, cols], state, NT)).astype(bf16)
            gv[:, cols] = (grad_values[rows, cols] + dot(kf, state)).astype(bf16)
        sender.put(j, partial[rows, :] + dot(gk[...], mine[0], NT) + dot(gv[...], mine[1], NT))
        return carry

    lax.fori_loop(0, blocks, block, 0)
    sender.finish(blocks)


def swapped(value, axis):
    return lax.ppermute(value, axis, [(i, i ^ 1) for i in range(lax.axis_size(axis))])


def exchange(value, axis, sign):
    count = lax.axis_size(axis)
    return [
        lax.ppermute(
            value, axis, [(i, i + sign * k) for i in range(count) if 0 <= i + sign * k < count]
        )
        for k in range(2, count, 2)
    ]


def regroup(value):
    return lax.all_to_all(value, "log", split_axis=0, concat_axis=0, tiled=True)


def shards(events, owner_ids, elapsed, resets, decay_rates, weights, cotangent):
    rows, width = events.shape[2:]
    owners = lax.axis_size("log")
    cap = 5 * rows // (4 * owners)
    slots = owners * cap
    pairs = width // 128
    blocks = slots // CH
    per = cap * pairs
    flat = pltpu.VMEM((slots * pairs, 128), f32)
    state_vmem = pltpu.VMEM((pairs, 128, 128), f32)
    state_msg = ((64 * pairs + 8, 128), bf16)
    wide16, wide32 = ((slots, width), bf16), ((slots, width), f32)

    tower = lax.axis_index("log") // (owners // decay_rates.shape[0])
    place_x = lax.axis_index("log") % NX
    info = jnp.stack([tower, lax.axis_index("ctx") % 2, place_x]).astype(jnp.int32)
    depth = owners // NX
    piece = ((depth, per, 128), bf16)
    sem = pltpu.SemaphoreType.DMA
    along_x = [
        [(i, i // NX * NX + (i + k) % NX) for i in range(owners)] for k in range(NX)
    ]
    along_z = [[z * NX + i for z in range(depth)] for i in range(NX)]

    def over_x(pieces):
        return [pieces[0]] + [lax.ppermute(pieces[k], "log", along_x[k]) for k in range(1, NX)]

    def over_z(value):
        moved = lax.all_to_all(
            value.reshape(depth, NX * per, 128), "log", split_axis=0, concat_axis=0,
            axis_index_groups=along_z, tiled=True,
        )
        return moved.reshape(depth, NX, per, 128)

    message, spots = call(
        pack_events,
        [((owners, per + 8, 128), bf16), ((2, rows), jnp.int32)],
        [
            owner_ids.reshape(1, rows),
            events.reshape(rows, width),
            elapsed.reshape(1, rows),
            resets.reshape(1, rows),
        ],
        [
            flat,
            pltpu.VMEM((slots, rows), bf16),
            pltpu.VMEM((1, rows), jnp.int32),
            pltpu.VMEM((rows, width), bf16),
            pltpu.VMEM((1, rows), f32),
            pltpu.VMEM((1, rows), f32),
            pltpu.SemaphoreType.DMA((4,)),
        ],
        {0: HBM, 1: HBM, 2: HBM, 3: HBM},
    )
    events_in = regroup(message)
    *pieces, back, back_far = call(
        pack_grads,
        [piece] * NX + [((rows, slots), bf16)] * 2,
        [info, spots, cotangent.reshape(rows, width)],
        [
            flat,
            pltpu.VMEM((NX, depth, per, 128), bf16),
            pltpu.VMEM((rows, slots), bf16),
            pltpu.VMEM((rows, slots), bf16),
            sem((NX + 2,)),
        ],
        {0: SMEM},
        range(NX + 2),
    )
    (merged,) = call(
        merge_pieces,
        [((depth, NX, per, 128), bf16)],
        over_x(pieces),
        [sem((NX,))],
        {k: HBM for k in range(NX)},
        (0,),
    )
    grads_in = over_z(merged)
    one = pltpu.VMEM((width, width), bf16)
    two = pltpu.VMEM((2, width, width), bf16)
    half_states = ((pairs, 64, 128), f32)
    flat_msg = ((slots * pairs, 128), bf16)
    block_wide = pltpu.VMEM((CH * pairs, 128), f32)
    flat_narrow = pltpu.VMEM(*flat_msg)
    rows16, rows32 = pltpu.VMEM(*wide16), pltpu.VMEM(*wide32)
    narrow_states = pltpu.VMEM((pairs, 128, 128), bf16)
    x, keys, values, keys_far, values_far, fade, fade_t, marks, send = call(
        forward_state,
        [
            wide16, wide16, wide16, wide16, wide16, ((slots, 128), f32), ((blocks, 8, 128), f32),
            ((blocks, 2 * pairs, 128), f32), state_msg,
        ],
        [info, decay_rates, events_in, weights],
        [flat, state_vmem, pltpu.VMEM((owners, per + 8, 128), bf16), two, rows16, sem((5,))],
        {0: SMEM, 1: SMEM, 2: HBM, 3: HBM},
        (0, 3, 4),
    )
    partner = swapped(send, "ctx")
    (q8,) = call(
        project_queries,
        [wide16],
        [info, x, weights],
        [one, rows16, sem((2,))],
        {0: SMEM, 1: HBM, 2: HBM},
    )
    (joined,) = call(join_ahead, [state_msg], [info, send, partner], (), {0: SMEM})
    received = exchange(joined, "ctx", 1)
    attended, kept = call(
        attend,
        [wide32, ((blocks, pairs, 64, 128), bf16)],
        [q8, keys, values, fade, fade_t, marks],
        [state_vmem, rows32, sem((blocks,))],
        None,
        (0,),
    )
    message, grads, grad_full, incoming, send = call(
        turn,
        [flat_msg, wide16, wide16, half_states, state_msg],
        [info, q8, fade, fade_t, attended, x, weights, grads_in, partner, *received],
        [
            flat, pltpu.VMEM((depth, NX, per, 128), bf16), one, rows16, rows32, rows16,
            block_wide, flat_narrow, narrow_states, state_vmem, sem((4 + NX,)), sem((blocks,)),
        ],
        {0: SMEM, 4: HBM, 5: HBM, 6: HBM, 7: ANY},
        (0, 1),
    )
    partner = swapped(send, "ctx")
    encoded_in = over_z(message)
    grad_q, grad_keys, grad_values = call(
        backward_local,
        [wide16, wide32, wide32],
        [q8, keys_far, values_far, fade, fade_t, marks, grad_full, kept, incoming],
        [state_vmem],
    )
    (joined,) = call(join_back, [state_msg], [info, send, partner], (), {0: SMEM})
    received = exchange(joined, "ctx", -1)
    (partial,) = call(
        project_back,
        [wide32],
        [info, grads, grad_q, weights],
        [one, rows16, sem((2,))],
        {0: SMEM, 1: HBM, 3: HBM},
    )
    (message,) = call(
        backward_finish,
        [flat_msg],
        [
            info, partial, grad_keys, grad_values, keys_far, values_far, fade, marks, weights,
            partner, *received,
        ],
        [
            two, block_wide, flat_narrow, narrow_states,
            pltpu.VMEM((CH, width), bf16), pltpu.VMEM((CH, width), bf16), sem, sem((blocks,)),
        ],
        {0: SMEM, 8: HBM},
        (0,),
    )
    grad_in = regroup(message.reshape(owners, per, 128))
    pieces = call(
        split_pieces,
        [piece] * NX,
        [info, encoded_in],
        [sem((NX,))],
        {0: SMEM, 1: HBM},
        range(NX),
    )
    (encoded,) = call(
        unpack_pieces, [((rows, width), bf16)], [back_far, *over_x(pieces)], [flat]
    )
    (grad,) = call(unpack_rows, [((rows, width), bf16)], [back, grad_in], [flat])
    return encoded.reshape(events.shape), grad.reshape(events.shape)


def solution(mesh):
    wide = P("ctx", "log", None, None)
    flat = P("ctx", "log", None)
    return jax.shard_map(
        shards,
        mesh=mesh,
        in_specs=(wide, wide, flat, flat, P(), P(), wide),
        out_specs=(wide, wide),
        check_vma=False,
    )
```

```python
import jax
import jax.numpy as jnp
from jax import lax
from jax.experimental import pallas as pl
from jax.experimental.pallas import tpu as pltpu
from jax.sharding import PartitionSpec as P


bf16 = jnp.bfloat16
f32 = jnp.float32
CH = 128
NN = (((1,), (0,)), ((), ()))
NT = (((1,), (1,)), ((), ()))
TN = (((0,), (0,)), ((), ()))
EXACT = lax.Precision.HIGHEST
LIMIT = 16 << 20
WIDE = 256


def dot(a, b, dims=NN, precision=None):
    return lax.dot_general(a, b, dims, preferred_element_type=f32, precision=precision)


def iota(shape, dim):
    return lax.broadcasted_iota(jnp.int32, shape, dim)


def ones_where(cond, dtype=bf16):
    return jnp.where(cond, 1.0, 0.0).astype(dtype)


VMEM = pl.BlockSpec(memory_space=pltpu.VMEM)
SMEM = pl.BlockSpec(memory_space=pltpu.SMEM)
HBM = pl.BlockSpec(memory_space=pltpu.HBM)
ANY = pl.BlockSpec(memory_space=pl.ANY)


def call(body, outs, ins, scratch=(), spaces=None, out_hbm=()):
    ins = [
        pltpu.with_memory_space_constraint(v, pltpu.HBM) if (spaces or {}).get(i) is HBM else v
        for i, v in enumerate(ins)
    ]
    return pl.pallas_call(
        body,
        out_shape=[
            pltpu.HBM(s, d) if i in out_hbm else jax.ShapeDtypeStruct(s, d)
            for i, (s, d) in enumerate(outs)
        ],
        in_specs=[(spaces or {}).get(i, VMEM) for i in range(len(ins))],
        out_specs=[HBM if i in out_hbm else VMEM for i in range(len(outs))],
        scratch_shapes=list(scratch),
        compiler_params=pltpu.CompilerParams(vmem_limit_bytes=LIMIT),
    )(*ins)


def write_rows(scratch, rows_of, parts):
    count = scratch.shape[0] // parts
    for j in range(parts):
        scratch[pl.ds(j, count, stride=parts), :] = rows_of(j)


def write_message(message, scratch, rows_of, width):
    write_rows(scratch, rows_of, width // 128)
    owners = message.shape[0]
    per = scratch.shape[0] // owners
    message[:, 0:per, :] = scratch[...].reshape(owners, per, 128).astype(bf16)


def read_message(message, scratch, width):
    parts = width // 128
    count = scratch.shape[0] // parts
    owners = message.shape[0]
    per = scratch.shape[0] // owners
    scratch[...] = message[:, 0:per, :].astype(f32).reshape(scratch.shape)
    return [scratch[pl.ds(j, count, stride=parts), :] for j in range(parts)]


class Sender:
    def __init__(self, out, wide, narrow, sems, parts):
        self.out, self.wide, self.narrow, self.sems, self.parts = out, wide, narrow, sems, parts

    def copy(self, j):
        size = CH * self.parts
        span = pl.ds(pl.multiple_of(j * size, size), size)
        return pltpu.make_async_copy(self.narrow.at[span, :], self.out.at[span, :], self.sems.at[j])

    def put(self, j, value):
        size = CH * self.parts
        for p in range(self.parts):
            self.wide[pl.ds(p, CH, stride=self.parts), :] = value[:, 128 * p : 128 * (p + 1)]
        span = pl.ds(pl.multiple_of(j * size, size), size)
        self.narrow[span, :] = self.wide[...].astype(bf16)
        self.copy(j).start()

    def finish(self, blocks):
        for j in range(blocks):
            self.copy(j).wait()


def fetched(source, target, sem):
    copy = pltpu.make_async_copy(source, target, sem)
    copy.start()
    return copy


def rows_copy(source, target, sems, j):
    rows = pl.ds(pl.multiple_of(j * CH, CH), CH)
    return pltpu.make_async_copy(source.at[rows, :], target.at[rows, :], sems.at[j])


def expanded(fade, rows, p):
    here = fade[rows, :]
    shape = (here.shape[0], 128)
    return jnp.where(
        iota(shape, 1) < 64,
        jnp.broadcast_to(here[:, 2 * p : 2 * p + 1], shape),
        jnp.broadcast_to(here[:, 2 * p + 1 : 2 * p + 2], shape),
    )


def pack_events(
    owner_in, events_in, elapsed_in, resets_in, message, spots,
    scratch, place, owner, events, elapsed, resets, sems,
):
    copies = [
        pltpu.make_async_copy(source, target, sems.at[i])
        for i, (source, target) in enumerate(
            (
                (owner_in, owner),
                (elapsed_in, elapsed),
                (resets_in, resets),
                (events_in, events),
            )
        )
    ]
    for copy in copies:
        copy.start()
    copies[0].wait()
    rows, width = events.shape
    owners = message.shape[0]
    slots = place.shape[0]
    cap = slots // owners
    own = owner[...]
    hit = iota((owners, rows), 0) == own
    earlier = ones_where(iota((rows, rows), 0) < iota((rows, rows), 1))
    before = dot(ones_where(hit), earlier)
    rank = jnp.sum(jnp.where(hit, before, 0.0), axis=0, keepdims=True).astype(jnp.int32)
    spots[0:1, :] = own
    spots[1:2, :] = own * cap + rank
    place[...] = ones_where(iota((slots, rows), 0) == own * cap + rank)
    for copy in copies[1:]:
        copy.wait()
    write_message(
        message,
        scratch,
        lambda j: dot(place[...], events[:, 128 * j : 128 * (j + 1)]),
        width,
    )
    lanes = iota((128, rows), 0)
    times = jnp.zeros((owners, 128), f32)
    for k, ref in enumerate((elapsed, resets)):
        value = ref[...]
        high = value.astype(bf16).astype(f32)
        for m, part in enumerate((high, value - high)):
            spot = ones_where(lanes == rank + cap * (2 * k + m))
            times += dot(jnp.where(hit, part, 0.0).astype(bf16), spot, NT)
    spread = ones_where(iota((owners * 8, owners), 0) == 8 * iota((owners * 8, owners), 1))
    extra = dot(spread, times.astype(bf16)).reshape(owners, 8, 128)
    per = scratch.shape[0] // owners
    message[:, per : per + 8, :] = extra.astype(bf16)


def pack_grads(info, spots, grads, message, back, scratch, narrow, turned, sems):
    rows, width = grads.shape
    slots = turned.shape[1]
    place = ones_where(iota((slots, rows), 0) == spots[1:2, :])
    write_rows(scratch, lambda j: dot(place, grads[:, 128 * j : 128 * (j + 1)]), width // 128)
    narrow[...] = scratch[...].astype(bf16)
    copies = [fetched(narrow, message, sems.at[0])]
    same = ones_where(iota((rows, rows), 0) == iota((rows, rows), 1))
    turned[...] = dot(same, place, NT).astype(bf16)
    copies.append(fetched(turned, back, sems.at[1]))
    for copy in copies:
        copy.wait()


def unpack_rows(back, message, out, scratch):
    width = out.shape[1]
    for j, part in enumerate(read_message(message, scratch, width)):
        out[:, 128 * j : 128 * (j + 1)] = dot(back[...], part.astype(bf16)).astype(bf16)


def halves():
    low = ones_where(iota((CH, 128), 1) < 64)
    return low, ones_where(iota((CH, 128), 1) >= 64)


def block_mask():
    return (iota((128, 128), 0) < 64) == (iota((128, 128), 1) < 64)


def stacked(value, low, high):
    return jnp.concatenate([value * low, value * high], axis=0)


def decay_pair(fade, fade_t, rows, j, p):
    causal = iota((CH, CH), 0) >= iota((CH, CH), 1)
    both, wide = [], []
    turned = fade_t[j]
    here = fade[rows, :]
    for h in (2 * p, 2 * p + 1):
        column = jnp.broadcast_to(here[:, h : h + 1], (CH, CH))
        wide.append(column)
        spread = column - turned[h : h + 1, :]
        both.append(jnp.exp(jnp.where(causal, spread, -1e30)))
    return jnp.concatenate(both, axis=1), jnp.where(iota((CH, CH), 1) < 64, wide[0], wide[1])


def folded(full):
    return full[0:64, :] + full[64:128, :]


def unfolded(half, mask):
    return jnp.where(mask, jnp.concatenate([half, half], axis=0), 0.0)


def write_state(send, state, last, pairs):
    for p in range(pairs):
        send[64 * p : 64 * (p + 1), :] = folded(state[p]).astype(bf16)
    write_marks(send, last, pairs)


def write_marks(send, last, pairs):
    last = jnp.broadcast_to(last, (8, 128))
    high = last.astype(bf16).astype(f32)
    lane = iota(last.shape, 1)
    send[64 * pairs : 64 * pairs + 8, :] = jnp.where(lane < 64, high, last - high).astype(bf16)


def read_marks(ref, pairs):
    marks = ref[64 * pairs : 64 * pairs + 8, :].astype(f32)
    return marks[:, 0:1] + marks[:, 64:65]


def lane_factors(log, p):
    return jnp.exp(
        jnp.where(
            iota((1, 128), 1) < 64,
            jnp.broadcast_to(log[2 * p : 2 * p + 1, :], (1, 128)),
            jnp.broadcast_to(log[2 * p + 1 : 2 * p + 2, :], (1, 128)),
        )
    )


def join_pair(near, far, out, pairs):
    log = read_marks(near, pairs)
    for p in range(pairs):
        rows = slice(64 * p, 64 * (p + 1))
        joined = near[rows, :].astype(f32) + lane_factors(log, p) * far[rows, :].astype(f32)
        out[rows, :] = joined.astype(bf16)
    write_marks(out, log + read_marks(far, pairs), pairs)


def join_ahead(info, own, other, out):
    join(info[1] == 1, own, other, out)


def join_back(info, own, other, out):
    join(info[1] == 0, own, other, out)


def join(own_is_near, own, other, out):
    pairs = own.shape[0] // 64

    @pl.when(own_is_near)
    def _():
        join_pair(own, other, out, pairs)

    @pl.when(jnp.logical_not(own_is_near))
    def _():
        join_pair(other, own, out, pairs)


def gathered_state(partner_counts, partner, received, pairs):
    log = read_marks(partner, pairs) * partner_counts
    total = [partner[64 * p : 64 * (p + 1), :].astype(f32) * partner_counts for p in range(pairs)]
    for ref in received:
        for p in range(pairs):
            total[p] += lane_factors(log, p) * ref[64 * p : 64 * (p + 1), :].astype(f32)
        log = log + read_marks(ref, pairs)
    return total


def forward_state(
    info, rates, message_in, weights,
    x_out, keys, values, keys_out, values_out, fade, fade_t, marks, send,
    scratch, memory, message, mine, x, sems,
):
    arrival = fetched(message_in, message, sems.at[0])
    fetch = fetched(weights.at[info[0], pl.ds(1, 2)], mine, sems.at[1])
    slots, width = x.shape
    pairs = width // 128
    blocks = slots // CH
    owners = message.shape[0]
    cap = slots // owners
    per = cap * pairs
    arrival.wait()
    for j, part in enumerate(read_message(message, scratch, width)):
        x[:, 128 * j : 128 * (j + 1)] = part.astype(bf16)
    stores = [fetched(x, x_out, sems.at[2])]
    times = message[:, per : per + 8, :].astype(f32).reshape(owners * 8, 128).astype(bf16)
    r = iota((slots, owners * 8), 0)
    c = iota((slots, owners * 8), 1)
    expand = ones_where(((c & 7) == 0) & (8 * r >= cap * c) & (8 * r < cap * (c + 8)))
    wide = dot(expand, times)
    row = iota((slots, 128), 0).astype(f32)
    lane = iota((slots, 128), 1).astype(f32)
    s = row - cap * jnp.floor((row + 0.5) * (1.0 / cap))
    hit = (lane == s) | (lane == s + cap) | (lane == s + 2 * cap) | (lane == s + 3 * cap)
    own = jnp.where(hit, wide, 0.0).astype(bf16)
    tri = ones_where(iota((slots, slots), 0) >= iota((slots, slots), 1))
    running = dot(tri, own)
    kind = iota((128, 128), 0)
    head = iota((128, 128), 1)
    kind_t = iota((8, 128), 1)
    head_t = iota((8, 128), 0)
    rate = jnp.zeros((128, 128), f32)
    rate_t = jnp.zeros((8, 128), f32)
    for h in range(rates.shape[1]):
        value = rates[info[0], h]
        rate = jnp.where(head == h, value, rate)
        rate_t = jnp.where(head_t == h, value, rate_t)
    to_heads = jnp.where(kind < 2 * cap, -rate, jnp.where(kind < 4 * cap, -1.0, 0.0))
    fade[...] = dot(running, to_heads, NN, EXACT)
    to_heads = jnp.where(kind_t < 2 * cap, -rate_t, jnp.where(kind_t < 4 * cap, -1.0, 0.0))
    turned = dot(to_heads, running, NT, EXACT)
    for j in range(blocks):
        fade_t[j] = turned[:, CH * j : CH * (j + 1)]
    for j in range(blocks):
        for p in range(pairs):
            if j == 0:
                marks[j, p : p + 1, :] = jnp.zeros((1, 128), f32)
            else:
                marks[j, p : p + 1, :] = expanded(fade, slice(CH * j - 1, CH * j), p)
            end = slice(CH * j + CH - 1, CH * j + CH)
            marks[j, pairs + p : pairs + p + 1, :] = expanded(fade, end, p)
    fetch.wait()
    mask = block_mask()
    for n in range(0, width, WIDE):
        cols = slice(n, n + WIDE)
        keys[:, cols] = dot(x[...], mine[0, :, cols]).astype(bf16)
        values[:, cols] = dot(x[...], mine[1, :, cols]).astype(bf16)
    every = slice(0, slots)
    for p in range(pairs):
        cols = slice(128 * p, 128 * (p + 1))
        end = marks[blocks - 1, pairs + p : pairs + p + 1, :]
        kf = (keys[:, cols].astype(f32) * jnp.exp(end - expanded(fade, every, p))).astype(bf16)
        memory[p] = jnp.where(mask, dot(kf, values[:, cols], TN), 0.0)
    stores.append(fetched(keys, keys_out, sems.at[3]))
    stores.append(fetched(values, values_out, sems.at[4]))
    write_state(send, memory, turned[:, slots - 1 : slots], pairs)
    for store in stores:
        store.wait()


def attend(
    info, x_in, weights, keys, values, fade, fade_t, marks,
    q8, attended_out, states,
    memory, attended, x, mine, in_sems, sems,
):
    arrival = fetched(x_in, x, in_sems.at[0])
    fetch = fetched(weights.at[info[0], 0], mine, in_sems.at[1])
    arrival.wait()
    fetch.wait()
    for n in range(0, x.shape[1], WIDE):
        cols = slice(n, n + WIDE)
        query = dot(x[...], mine[:, cols]).astype(bf16).astype(f32)
        q8[:, cols] = (query * 0.125).astype(bf16)
    slots, width = q8.shape
    pairs = width // 128
    low, high = halves()
    mask = block_mask()
    memory[...] = jnp.zeros(memory.shape, f32)

    def block(j, carry):
        rows = pl.ds(pl.multiple_of(j * CH, CH), CH)
        edge = marks[j]
        for p in range(pairs):
            cols = slice(128 * p, 128 * (p + 1))
            start, end = edge[p : p + 1, :], edge[pairs + p : pairs + p + 1, :]
            qp, kp, vp = q8[rows, cols], keys[rows, cols], values[rows, cols]
            scores = dot(qp, stacked(kp, low, high), NT)
            fading, g = decay_pair(fade, fade_t, rows, j, p)
            mix = (scores * fading).astype(bf16)
            within = dot(mix, stacked(vp, low, high))
            now = memory[p]
            states[j, p] = folded(now).astype(bf16)
            lifted = (qp.astype(f32) * jnp.exp(g - start)).astype(bf16)
            attended[rows, cols] = within + dot(lifted, now.astype(bf16))
            kf = (kp.astype(f32) * jnp.exp(end - g)).astype(bf16)
            memory[p] = jnp.exp(end - start) * now + jnp.where(mask, dot(kf, vp, TN), 0.0)
        rows_copy(attended, attended_out, sems, j).start()
        return carry

    lax.fori_loop(0, slots // CH, block, 0)
    for j in range(slots // CH):
        rows_copy(attended, attended_out, sems, j).wait()


def turn(info, q8, fade, fade_t, attended_in, x_in, weights, message_in, partner, *rest):
    received = rest[:-20]
    (
        encoded, grads_out, grad_full, incoming, send,
        scratch, message, mine, x, attended, grads, grad_normed, normed, lifts,
        wide, narrow, states, memory, sems, out_sems,
    ) = rest[-20:]
    arrival = fetched(message_in, message, sems.at[2])
    fetch = fetched(weights.at[info[0], 3], mine, sems.at[0])
    rows_in = fetched(x_in, x, sems.at[1])
    attended_here = fetched(attended_in, attended, sems.at[3])
    slots, width = x.shape
    pairs = width // 128
    blocks = slots // CH
    mask = block_mask()
    for p, state in enumerate(gathered_state(info[1].astype(f32), partner, received, pairs)):
        incoming[p] = state
        states[p] = unfolded(state, mask).astype(bf16)
    arrival.wait()
    for j, part in enumerate(read_message(message, scratch, width)):
        grads[:, 128 * j : 128 * (j + 1)] = part.astype(bf16)
    store = fetched(grads, grads_out, sems.at[4])
    fetch.wait()
    for n in range(0, width, WIDE):
        cols = slice(n, n + WIDE)
        grad_normed[:, cols] = dot(grads[...], mine[cols, :], NT).astype(bf16)
    attended_here.wait()

    def block(j, carry):
        rows = pl.ds(pl.multiple_of(j * CH, CH), CH)
        values = []
        square = jnp.zeros((CH, 1), f32)
        for p in range(pairs):
            cols = slice(128 * p, 128 * (p + 1))
            lifted = (q8[rows, cols].astype(f32) * jnp.exp(expanded(fade, rows, p))).astype(bf16)
            lifts[rows, cols] = lifted
            value = attended[rows, cols] + dot(lifted, states[p])
            values.append(value)
            square += jnp.sum(value * value, axis=1, keepdims=True)
        here = jnp.concatenate(values, axis=1)
        scale = lax.rsqrt(square * (1.0 / width) + 1e-06)
        normed[rows, :] = (here * scale).astype(bf16)
        grad = grad_normed[rows, :].astype(f32)
        along = jnp.mean(here * grad, axis=1, keepdims=True)
        grad_full[rows, :] = (scale * grad - here * (scale * scale * scale * along)).astype(bf16)
        return carry

    lax.fori_loop(0, blocks, block, 0)
    for p in range(pairs):
        cols = slice(128 * p, 128 * (p + 1))
        memory[p] = jnp.where(mask, dot(lifts[:, cols], grad_full[:, cols], TN), 0.0)
    write_state(send, memory, fade_t[blocks - 1][:, CH - 1 : CH], pairs)
    rows_in.wait()
    for n in range(0, width, WIDE):
        cols = slice(n, n + WIDE)
        attended[:, cols] = x[:, cols].astype(f32) + dot(normed[...], mine[:, cols])
    sender = Sender(encoded, wide, narrow, out_sems, pairs)

    def put(j, carry):
        sender.put(j, attended[pl.ds(pl.multiple_of(j * CH, CH), CH), :])
        return carry

    lax.fori_loop(0, blocks, put, 0)
    sender.finish(blocks)
    store.wait()


def backward_local(
    info, q8, keys_in, values_in, fade, fade_t, marks, grad_full, states, incoming, grads_in,
    weights,
    grad_keys, grad_values, partial,
    memory, grad_q, grads, mine, keys, values, sems, key_sems, value_sems,
):
    for j in reversed(range(q8.shape[0] // CH)):
        rows_copy(keys_in, keys, key_sems, j).start()
        rows_copy(values_in, values, value_sems, j).start()
    arrival = fetched(grads_in, grads, sems.at[0])
    fetch = fetched(weights.at[info[0], 0], mine, sems.at[1])
    slots, width = q8.shape
    pairs = width // 128
    blocks = slots // CH
    low, high = halves()
    lower = iota((CH, 128), 1) < 64
    mask = block_mask()
    memory[...] = jnp.zeros(memory.shape, f32)

    def block(i, carry):
        j = blocks - 1 - i
        rows_copy(keys_in, keys, key_sems, j).wait()
        rows_copy(values_in, values, value_sems, j).wait()
        rows = pl.ds(pl.multiple_of(j * CH, CH), CH)
        edge = marks[j]
        for p in range(pairs):
            cols = slice(128 * p, 128 * (p + 1))
            start, end = edge[p : p + 1, :], edge[pairs + p : pairs + p + 1, :]
            qp, kp, vp = q8[rows, cols], keys[rows, cols], values[rows, cols]
            da = grad_full[rows, cols]
            ks, vs = stacked(kp, low, high), stacked(vp, low, high)
            fading, g = decay_pair(fade, fade_t, rows, j, p)
            mix = (dot(qp, ks, NT) * fading).astype(bf16)
            grad_scores = (dot(da, vs, NT) * fading).astype(bf16)
            lift = jnp.exp(g - start)
            fall = jnp.exp(end - g)
            state = states[j, p].astype(f32) + jnp.exp(start) * incoming[p]
            state = unfolded(state, mask).astype(bf16)
            grad_q[rows, cols] = (
                0.125 * (dot(grad_scores, ks) + lift * dot(da, state, NT))
            ).astype(bf16)
            gk = dot(grad_scores, qp, TN)
            gv = dot(mix, da, TN)
            now = memory[p]
            narrow = now.astype(bf16)
            kf = (kp.astype(f32) * fall).astype(bf16)
            grad_keys[rows, cols] = jnp.where(lower, gk[0:CH], gk[CH:]) + fall * dot(vp, narrow, NT)
            grad_values[rows, cols] = jnp.where(lower, gv[0:CH], gv[CH:]) + dot(kf, narrow)
            lifted = (qp.astype(f32) * lift).astype(bf16)
            memory[p] = jnp.exp(end - start) * now + jnp.where(mask, dot(lifted, da, TN), 0.0)
        return carry

    lax.fori_loop(0, blocks, block, 0)
    arrival.wait()
    fetch.wait()
    for n in range(0, width, WIDE):
        cols = slice(n, n + WIDE)
        partial[:, cols] = grads[:, cols].astype(f32) + dot(grad_q[...], mine[cols, :], NT)


def backward_finish(
    info, partial, grad_keys, grad_values, keys_in, values_in, fade, marks, weights, partner, *rest
):
    received = rest[:-12]
    out, mine, wide, narrow, states, gk, gv, total, keys, values, sems, out_sems = rest[-12:]
    keys_here = fetched(keys_in, keys, sems.at[1])
    values_here = fetched(values_in, values, sems.at[2])
    fetch = fetched(weights.at[info[0], pl.ds(1, 2)], mine, sems.at[0])
    slots, width = partial.shape
    pairs = width // 128
    blocks = slots // CH
    mask = block_mask()
    arrived = gathered_state((1 - info[1]).astype(f32), partner, received, pairs)
    for p, state in enumerate(arrived):
        states[p] = unfolded(state, mask).astype(bf16)
    every = slice(0, slots)
    keys_here.wait()
    values_here.wait()
    for p in range(pairs):
        cols = slice(128 * p, 128 * (p + 1))
        end = marks[blocks - 1, pairs + p : pairs + p + 1, :]
        fall = jnp.exp(end - expanded(fade, every, p))
        kf = (keys[:, cols].astype(f32) * fall).astype(bf16)
        state = states[p]
        gk[:, cols] = (grad_keys[:, cols] + fall * dot(values[:, cols], state, NT)).astype(bf16)
        gv[:, cols] = (grad_values[:, cols] + dot(kf, state)).astype(bf16)
    fetch.wait()
    for n in range(0, width, WIDE):
        cols = slice(n, n + WIDE)
        total[:, cols] = (
            partial[:, cols] + dot(gk[...], mine[0, cols, :], NT) + dot(gv[...], mine[1, cols, :], NT)
        )
    sender = Sender(out, wide, narrow, out_sems, pairs)

    def put(j, carry):
        sender.put(j, total[pl.ds(pl.multiple_of(j * CH, CH), CH), :])
        return carry

    lax.fori_loop(0, blocks, put, 0)
    sender.finish(blocks)


def swapped(value, axis):
    return lax.ppermute(value, axis, [(i, i ^ 1) for i in range(lax.axis_size(axis))])


def exchange(value, axis, sign):
    count = lax.axis_size(axis)
    return [
        lax.ppermute(
            value, axis, [(i, i + sign * k) for i in range(count) if 0 <= i + sign * k < count]
        )
        for k in range(2, count, 2)
    ]


def regroup(value):
    return lax.all_to_all(value, "log", split_axis=0, concat_axis=0, tiled=True)


def shards(events, owner_ids, elapsed, resets, decay_rates, weights, cotangent):
    rows, width = events.shape[2:]
    owners = lax.axis_size("log")
    cap = 5 * rows // (4 * owners)
    slots = owners * cap
    pairs = width // 128
    blocks = slots // CH
    per = cap * pairs
    flat = pltpu.VMEM((slots * pairs, 128), f32)
    state_vmem = pltpu.VMEM((pairs, 128, 128), f32)
    state_msg = ((64 * pairs + 8, 128), bf16)
    wide16, wide32 = ((slots, width), bf16), ((slots, width), f32)

    tower = lax.axis_index("log") // (owners // decay_rates.shape[0])
    info = jnp.stack([tower, lax.axis_index("ctx") % 2]).astype(jnp.int32)
    sem = pltpu.SemaphoreType.DMA

    message, spots = call(
        pack_events,
        [((owners, per + 8, 128), bf16), ((2, rows), jnp.int32)],
        [
            owner_ids.reshape(1, rows),
            events.reshape(rows, width),
            elapsed.reshape(1, rows),
            resets.reshape(1, rows),
        ],
        [
            flat,
            pltpu.VMEM((slots, rows), bf16),
            pltpu.VMEM((1, rows), jnp.int32),
            pltpu.VMEM((rows, width), bf16),
            pltpu.VMEM((1, rows), f32),
            pltpu.VMEM((1, rows), f32),
            pltpu.SemaphoreType.DMA((4,)),
        ],
        {0: HBM, 1: HBM, 2: HBM, 3: HBM},
    )
    events_in = regroup(message)
    flat_msg = ((slots * pairs, 128), bf16)
    message, back = call(
        pack_grads,
        [flat_msg, ((rows, slots), bf16)],
        [info, spots, cotangent.reshape(rows, width)],
        [flat, pltpu.VMEM(*flat_msg), pltpu.VMEM((rows, slots), bf16), sem((2,))],
        {0: SMEM},
        (0, 1),
    )
    grads_in = regroup(message.reshape(owners, per, 128))
    one = pltpu.VMEM((width, width), bf16)
    two = pltpu.VMEM((2, width, width), bf16)
    half_states = ((pairs, 64, 128), f32)
    block_wide = pltpu.VMEM((CH * pairs, 128), f32)
    flat_narrow = pltpu.VMEM(*flat_msg)
    rows16, rows32 = pltpu.VMEM(*wide16), pltpu.VMEM(*wide32)
    narrow_states = pltpu.VMEM((pairs, 128, 128), bf16)
    x, keys, values, keys_far, values_far, fade, fade_t, marks, send = call(
        forward_state,
        [
            wide16, wide16, wide16, wide16, wide16, ((slots, 128), f32), ((blocks, 8, 128), f32),
            ((blocks, 2 * pairs, 128), f32), state_msg,
        ],
        [info, decay_rates, events_in, weights],
        [flat, state_vmem, pltpu.VMEM((owners, per + 8, 128), bf16), two, rows16, sem((5,))],
        {0: SMEM, 1: SMEM, 2: HBM, 3: HBM},
        (0, 3, 4),
    )
    partner = swapped(send, "ctx")
    (joined,) = call(join_ahead, [state_msg], [info, send, partner], (), {0: SMEM})
    received = exchange(joined, "ctx", 1)
    q8, attended, kept = call(
        attend,
        [wide16, wide32, ((blocks, pairs, 64, 128), bf16)],
        [info, x, weights, keys, values, fade, fade_t, marks],
        [state_vmem, rows32, rows16, one, sem((2,)), sem((blocks,))],
        {0: SMEM, 1: HBM, 2: HBM},
        (1,),
    )
    message, grads, grad_full, incoming, send = call(
        turn,
        [flat_msg, wide16, wide16, half_states, state_msg],
        [info, q8, fade, fade_t, attended, x, weights, grads_in, partner, *received],
        [
            flat, pltpu.VMEM((owners, per, 128), bf16), one, rows16, rows32, rows16, rows16, rows16,
            rows16, block_wide, flat_narrow, narrow_states, state_vmem, sem((5,)), sem((blocks,)),
        ],
        {0: SMEM, 4: HBM, 5: HBM, 6: HBM, 7: ANY},
        (0, 1),
    )
    partner = swapped(send, "ctx")
    encoded_in = regroup(message.reshape(owners, per, 128))
    grad_keys, grad_values, partial = call(
        backward_local,
        [wide32, wide32, wide32],
        [
            info, q8, keys_far, values_far, fade, fade_t, marks, grad_full, kept, incoming, grads,
            weights,
        ],
        [
            state_vmem, rows16, rows16, one, rows16, rows16, sem((2,)), sem((blocks,)),
            sem((blocks,)),
        ],
        {0: SMEM, 2: HBM, 3: HBM, 10: HBM, 11: HBM},
    )
    (joined,) = call(join_back, [state_msg], [info, send, partner], (), {0: SMEM})
    received = exchange(joined, "ctx", -1)
    (message,) = call(
        backward_finish,
        [flat_msg],
        [
            info, partial, grad_keys, grad_values, keys_far, values_far, fade, marks, weights,
            partner, *received,
        ],
        [
            two, block_wide, flat_narrow, narrow_states,
            rows16, rows16, rows32, rows16, rows16, sem((3,)), sem((blocks,)),
        ],
        {0: SMEM, 4: HBM, 5: HBM, 8: HBM},
        (0,),
    )
    grad_in = regroup(message.reshape(owners, per, 128))
    (encoded,) = call(unpack_rows, [((rows, width), bf16)], [back, encoded_in], [flat])
    (grad,) = call(unpack_rows, [((rows, width), bf16)], [back, grad_in], [flat])
    return encoded.reshape(events.shape), grad.reshape(events.shape)


def solution(mesh):
    wide = P("ctx", "log", None, None)
    flat = P("ctx", "log", None)
    return jax.shard_map(
        shards,
        mesh=mesh,
        in_specs=(wide, wide, flat, flat, P(), P(), wide),
        out_specs=(wide, wide),
        check_vma=False,
    )
```

```python
import jax
import jax.numpy as jnp
from jax import lax
from jax.experimental import pallas as pl
from jax.experimental.pallas import tpu as pltpu
from jax.sharding import PartitionSpec as P


bf16 = jnp.bfloat16
f32 = jnp.float32
CH = 128
NN = (((1,), (0,)), ((), ()))
NT = (((1,), (1,)), ((), ()))
TN = (((0,), (0,)), ((), ()))
EXACT = lax.Precision.HIGHEST
LIMIT = 16 << 20
WIDE = 256


def dot(a, b, dims=NN, precision=None):
    return lax.dot_general(a, b, dims, preferred_element_type=f32, precision=precision)


def iota(shape, dim):
    return lax.broadcasted_iota(jnp.int32, shape, dim)


def ones_where(cond, dtype=bf16):
    return jnp.where(cond, 1.0, 0.0).astype(dtype)


VMEM = pl.BlockSpec(memory_space=pltpu.VMEM)
SMEM = pl.BlockSpec(memory_space=pltpu.SMEM)
HBM = pl.BlockSpec(memory_space=pltpu.HBM)
ANY = pl.BlockSpec(memory_space=pl.ANY)


def call(body, outs, ins, scratch=(), spaces=None, out_hbm=()):
    ins = [
        pltpu.with_memory_space_constraint(v, pltpu.HBM) if (spaces or {}).get(i) is HBM else v
        for i, v in enumerate(ins)
    ]
    return pl.pallas_call(
        body,
        out_shape=[
            pltpu.HBM(s, d) if i in out_hbm else jax.ShapeDtypeStruct(s, d)
            for i, (s, d) in enumerate(outs)
        ],
        in_specs=[(spaces or {}).get(i, VMEM) for i in range(len(ins))],
        out_specs=[HBM if i in out_hbm else VMEM for i in range(len(outs))],
        scratch_shapes=list(scratch),
        compiler_params=pltpu.CompilerParams(vmem_limit_bytes=LIMIT),
    )(*ins)


def write_rows(scratch, rows_of, parts):
    count = scratch.shape[0] // parts
    for j in range(parts):
        scratch[pl.ds(j, count, stride=parts), :] = rows_of(j)


def write_message(message, scratch, rows_of, width):
    write_rows(scratch, rows_of, width // 128)
    owners = message.shape[0]
    per = scratch.shape[0] // owners
    message[:, 0:per, :] = scratch[...].reshape(owners, per, 128).astype(bf16)


def read_message(message, scratch, width):
    parts = width // 128
    count = scratch.shape[0] // parts
    owners = message.shape[0]
    per = scratch.shape[0] // owners
    scratch[...] = message[:, 0:per, :].astype(f32).reshape(scratch.shape)
    return [scratch[pl.ds(j, count, stride=parts), :] for j in range(parts)]


class Sender:
    def __init__(self, out, wide, narrow, sems, parts):
        self.out, self.wide, self.narrow, self.sems, self.parts = out, wide, narrow, sems, parts

    def copy(self, j):
        size = CH * self.parts
        span = pl.ds(pl.multiple_of(j * size, size), size)
        return pltpu.make_async_copy(self.narrow.at[span, :], self.out.at[span, :], self.sems.at[j])

    def put(self, j, value):
        size = CH * self.parts
        for p in range(self.parts):
            self.wide[pl.ds(p, CH, stride=self.parts), :] = value[:, 128 * p : 128 * (p + 1)]
        span = pl.ds(pl.multiple_of(j * size, size), size)
        self.narrow[span, :] = self.wide[...].astype(bf16)
        self.copy(j).start()

    def finish(self, blocks):
        for j in range(blocks):
            self.copy(j).wait()


def fetched(source, target, sem):
    copy = pltpu.make_async_copy(source, target, sem)
    copy.start()
    return copy


def rows_copy(source, target, sems, j):
    rows = pl.ds(pl.multiple_of(j * CH, CH), CH)
    return pltpu.make_async_copy(source.at[rows, :], target.at[rows, :], sems.at[j])


def parts_of(value, count):
    group = iota(value.shape, 1) >> 3
    out = jnp.zeros(value.shape, f32)
    for n in range(count):
        part = value.astype(bf16).astype(f32)
        out = jnp.where(group == n, part, out)
        value = value - part
    return out.astype(bf16)


def spread_all(count, width):
    q, c = iota((128, width), 0), iota((128, width), 1)
    return ones_where((q < 8 * count) & ((q & 7) == (c >> 6)))


def pack_events(
    owner_in, events_in, elapsed_in, resets_in, message, spots,
    scratch, place, owner, events, elapsed, resets, sems,
):
    copies = [
        pltpu.make_async_copy(source, target, sems.at[i])
        for i, (source, target) in enumerate(
            (
                (owner_in, owner),
                (elapsed_in, elapsed),
                (resets_in, resets),
                (events_in, events),
            )
        )
    ]
    for copy in copies:
        copy.start()
    copies[0].wait()
    rows, width = events.shape
    owners = message.shape[0]
    slots = place.shape[0]
    cap = slots // owners
    own = owner[...]
    hit = iota((owners, rows), 0) == own
    earlier = ones_where(iota((rows, rows), 0) < iota((rows, rows), 1))
    before = dot(ones_where(hit), earlier)
    rank = jnp.sum(jnp.where(hit, before, 0.0), axis=0, keepdims=True).astype(jnp.int32)
    spots[0:1, :] = own
    spots[1:2, :] = own * cap + rank
    place[...] = ones_where(iota((slots, rows), 0) == own * cap + rank)
    for copy in copies[1:]:
        copy.wait()
    write_message(
        message,
        scratch,
        lambda j: dot(place[...], events[:, 128 * j : 128 * (j + 1)]),
        width,
    )
    lanes = iota((128, rows), 0)
    times = jnp.zeros((owners, 128), f32)
    for k, ref in enumerate((elapsed, resets)):
        value = ref[...]
        high = value.astype(bf16).astype(f32)
        for m, part in enumerate((high, value - high)):
            spot = ones_where(lanes == rank + cap * (2 * k + m))
            times += dot(jnp.where(hit, part, 0.0).astype(bf16), spot, NT)
    spread = ones_where(iota((owners * 8, owners), 0) == 8 * iota((owners * 8, owners), 1))
    extra = dot(spread, times.astype(bf16)).reshape(owners, 8, 128)
    per = scratch.shape[0] // owners
    message[:, per : per + 8, :] = extra.astype(bf16)


def pack_grads(info, spots, grads, message, back, expand, mine, scratch, narrow, turned, sems):
    rows, width = grads.shape
    slots = turned.shape[1]
    place = ones_where(iota((slots, rows), 0) == spots[1:2, :])
    write_rows(scratch, lambda j: dot(place, grads[:, 128 * j : 128 * (j + 1)]), width // 128)
    narrow[...] = scratch[...].astype(bf16)
    copies = [fetched(narrow, message, sems.at[0])]
    same = ones_where(iota((rows, rows), 0) == iota((rows, rows), 1))
    turned[...] = dot(same, place, NT).astype(bf16)
    copies.append(fetched(turned, back, sems.at[1]))
    cap = slots * 8 // expand.shape[1]
    r, c = iota(expand.shape, 0), iota(expand.shape, 1)
    expand[...] = ones_where(((c & 7) == 0) & (8 * r >= cap * c) & (8 * r < cap * (c + 8)))
    row, lane = iota(mine.shape, 0).astype(f32), iota(mine.shape, 1).astype(f32)
    s = row - cap * jnp.floor((row + 0.5) * (1.0 / cap))
    hit = (lane == s) | (lane == s + cap) | (lane == s + 2 * cap) | (lane == s + 3 * cap)
    mine[...] = ones_where(hit)
    for copy in copies:
        copy.wait()


def unpack_rows(back, message, out, scratch):
    width = out.shape[1]
    for j, part in enumerate(read_message(message, scratch, width)):
        out[:, 128 * j : 128 * (j + 1)] = dot(back[...], part.astype(bf16)).astype(bf16)


def halves():
    low = ones_where(iota((CH, 128), 1) < 64)
    return low, ones_where(iota((CH, 128), 1) >= 64)


def block_mask():
    return (iota((128, 128), 0) < 64) == (iota((128, 128), 1) < 64)


def stacked(value, low, high):
    return jnp.concatenate([value * low, value * high], axis=0)


def decay_pair(fade, fade_t, rows, j, p):
    causal = iota((CH, CH), 0) >= iota((CH, CH), 1)
    both, wide = [], []
    turned = fade_t[j]
    here = fade[rows, :]
    for h in (2 * p, 2 * p + 1):
        column = jnp.broadcast_to(here[:, h : h + 1], (CH, CH))
        wide.append(column)
        spread = column - turned[h : h + 1, :]
        both.append(jnp.exp(jnp.where(causal, spread, -1e30)))
    return jnp.concatenate(both, axis=1), jnp.where(iota((CH, CH), 1) < 64, wide[0], wide[1])


def folded(full):
    return full[0:64, :] + full[64:128, :]


def unfolded(half, mask):
    return jnp.where(mask, jnp.concatenate([half, half], axis=0), 0.0)


def write_state(send, state, last, pairs):
    for p in range(pairs):
        send[64 * p : 64 * (p + 1), :] = folded(state[p]).astype(bf16)
    write_marks(send, last, pairs)


def write_marks(send, last, pairs):
    last = jnp.broadcast_to(last, (8, 128))
    high = last.astype(bf16).astype(f32)
    lane = iota(last.shape, 1)
    send[64 * pairs : 64 * pairs + 8, :] = jnp.where(lane < 64, high, last - high).astype(bf16)


def read_marks(ref, pairs):
    marks = ref[64 * pairs : 64 * pairs + 8, :].astype(f32)
    return marks[:, 0:1] + marks[:, 64:65]


def lane_factors(log, p):
    return jnp.exp(
        jnp.where(
            iota((1, 128), 1) < 64,
            jnp.broadcast_to(log[2 * p : 2 * p + 1, :], (1, 128)),
            jnp.broadcast_to(log[2 * p + 1 : 2 * p + 2, :], (1, 128)),
        )
    )


def join_pair(near, far, out, pairs):
    log = read_marks(near, pairs)
    for p in range(pairs):
        rows = slice(64 * p, 64 * (p + 1))
        joined = near[rows, :].astype(f32) + lane_factors(log, p) * far[rows, :].astype(f32)
        out[rows, :] = joined.astype(bf16)
    write_marks(out, log + read_marks(far, pairs), pairs)


def join_ahead(info, own, other, out):
    join(info[1] == 1, own, other, out)


def join_back(info, own, other, out):
    join(info[1] == 0, own, other, out)


def join(own_is_near, own, other, out):
    pairs = own.shape[0] // 64

    @pl.when(own_is_near)
    def _():
        join_pair(own, other, out, pairs)

    @pl.when(jnp.logical_not(own_is_near))
    def _():
        join_pair(other, own, out, pairs)


def gathered_state(partner_counts, partner, received, pairs):
    log = read_marks(partner, pairs) * partner_counts
    total = [partner[64 * p : 64 * (p + 1), :].astype(f32) * partner_counts for p in range(pairs)]
    for ref in received:
        for p in range(pairs):
            total[p] += lane_factors(log, p) * ref[64 * p : 64 * (p + 1), :].astype(f32)
        log = log + read_marks(ref, pairs)
    return total


def forward_state(
    info, rates, message_in, weights, expand, own_lanes,
    x_out, keys, values, keys_out, values_out, fade, fade_t, marks, fall, send,
    scratch, memory, message, mine, x, sems,
):
    arrival = fetched(message_in, message, sems.at[0])
    fetch = fetched(weights.at[info[0], pl.ds(1, 2)], mine, sems.at[1])
    slots, width = x.shape
    pairs = width // 128
    blocks = slots // CH
    owners = message.shape[0]
    cap = slots // owners
    per = cap * pairs
    arrival.wait()
    for j, part in enumerate(read_message(message, scratch, width)):
        x[:, 128 * j : 128 * (j + 1)] = part.astype(bf16)
    stores = [fetched(x, x_out, sems.at[2])]
    times = message[:, per : per + 8, :].astype(f32).reshape(owners * 8, 128).astype(bf16)
    own = dot(expand[...], times).astype(bf16) * own_lanes[...]
    kind, head = iota((128, 128), 0), iota((128, 128), 1) & 7
    rate = jnp.zeros((128, 128), f32)
    for h in range(rates.shape[1]):
        rate = jnp.where(head == h, rates[info[0], h], rate)
    to_heads = jnp.where(kind < 2 * cap, -rate, jnp.where(kind < 4 * cap, -1.0, 0.0))
    tri = ones_where(iota((CH, CH), 0) >= iota((CH, CH), 1))
    before = jnp.zeros((1, 128), f32)
    start = jnp.zeros((1, 128), f32)
    ends = []
    for j in range(blocks):
        running = dot(tri, own[CH * j : CH * (j + 1), :]) + before
        before = running[CH - 1 : CH, :]
        here = dot(running, to_heads, NN, EXACT)
        fade[CH * j : CH * (j + 1), :] = here
        fade_t[j] = here.T[0:8, :]
        start = here[CH - 1 : CH, :]
        ends.append(start)
    ends = jnp.concatenate(ends + [jnp.zeros((8 - blocks, 128), f32)], axis=0)
    wide_ends = dot(parts_of(ends, 3), spread_all(3, width))
    for j in range(blocks):
        for p in range(pairs):
            cols = slice(128 * p, 128 * (p + 1))
            marks[j, pairs + p : pairs + p + 1, :] = wide_ends[j : j + 1, cols]
            if j == 0:
                marks[j, p : p + 1, :] = jnp.zeros((1, 128), f32)
            else:
                marks[j, p : p + 1, :] = wide_ends[j - 1 : j, cols]
    fall[...] = parts_of(jnp.exp(start - fade[...]), 2)
    fetch.wait()
    mask = block_mask()
    for n in range(0, width, WIDE):
        cols = slice(n, n + WIDE)
        keys[:, cols] = dot(x[...], mine[0, :, cols]).astype(bf16)
        values[:, cols] = dot(x[...], mine[1, :, cols]).astype(bf16)
    hot = spread_all(2, width)
    for p in range(pairs):
        cols = slice(128 * p, 128 * (p + 1))
        kf = (keys[:, cols].astype(f32) * dot(fall[...], hot[:, cols])).astype(bf16)
        memory[p] = jnp.where(mask, dot(kf, values[:, cols], TN), 0.0)
    stores.append(fetched(keys, keys_out, sems.at[3]))
    stores.append(fetched(values, values_out, sems.at[4]))
    write_state(send, memory, fade_t[blocks - 1][:, CH - 1 : CH], pairs)
    for store in stores:
        store.wait()


def attend(
    info, x_in, weights, keys, values, fade, fade_t, marks,
    q8, attended_out, states, lift,
    memory, attended, x, mine, in_sems, sems,
):
    arrival = fetched(x_in, x, in_sems.at[0])
    fetch = fetched(weights.at[info[0], 0], mine, in_sems.at[1])
    lift[...] = parts_of(jnp.exp(fade[...]), 2)
    arrival.wait()
    fetch.wait()
    for n in range(0, x.shape[1], WIDE):
        cols = slice(n, n + WIDE)
        query = dot(x[...], mine[:, cols]).astype(bf16).astype(f32)
        q8[:, cols] = (query * 0.125).astype(bf16)
    slots, width = q8.shape
    pairs = width // 128
    low, high = halves()
    mask = block_mask()
    memory[...] = jnp.zeros(memory.shape, f32)

    def block(j, carry):
        rows = pl.ds(pl.multiple_of(j * CH, CH), CH)
        edge = marks[j]
        for p in range(pairs):
            cols = slice(128 * p, 128 * (p + 1))
            start, end = edge[p : p + 1, :], edge[pairs + p : pairs + p + 1, :]
            qp, kp, vp = q8[rows, cols], keys[rows, cols], values[rows, cols]
            scores = dot(qp, stacked(kp, low, high), NT)
            fading, g = decay_pair(fade, fade_t, rows, j, p)
            mix = (scores * fading).astype(bf16)
            within = dot(mix, stacked(vp, low, high))
            now = memory[p]
            states[j, p] = folded(now).astype(bf16)
            lifted = (qp.astype(f32) * jnp.exp(g - start)).astype(bf16)
            attended[rows, cols] = within + dot(lifted, now.astype(bf16))
            kf = (kp.astype(f32) * jnp.exp(end - g)).astype(bf16)
            memory[p] = jnp.exp(end - start) * now + jnp.where(mask, dot(kf, vp, TN), 0.0)
        rows_copy(attended, attended_out, sems, j).start()
        return carry

    lax.fori_loop(0, slots // CH, block, 0, unroll=True)
    for j in range(slots // CH):
        rows_copy(attended, attended_out, sems, j).wait()


def turn(info, q8, lift, fade_t, attended_in, x_in, weights, message_in, partner, *rest):
    received = rest[:-20]
    (
        encoded, grads_out, grad_full, incoming, send,
        scratch, message, mine, x, attended, grads, grad_normed, normed, lifts,
        wide, narrow, states, memory, sems, out_sems,
    ) = rest[-20:]
    arrival = fetched(message_in, message, sems.at[2])
    fetch = fetched(weights.at[info[0], 3], mine, sems.at[0])
    rows_in = fetched(x_in, x, sems.at[1])
    attended_here = fetched(attended_in, attended, sems.at[3])
    slots, width = x.shape
    pairs = width // 128
    blocks = slots // CH
    mask = block_mask()
    for p, state in enumerate(gathered_state(info[1].astype(f32), partner, received, pairs)):
        incoming[p] = state
        states[p] = unfolded(state, mask).astype(bf16)
    arrival.wait()
    for j, part in enumerate(read_message(message, scratch, width)):
        grads[:, 128 * j : 128 * (j + 1)] = part.astype(bf16)
    store = fetched(grads, grads_out, sems.at[4])
    fetch.wait()
    for n in range(0, width, WIDE):
        cols = slice(n, n + WIDE)
        grad_normed[:, cols] = dot(grads[...], mine[cols, :], NT).astype(bf16)
    attended_here.wait()

    hot = spread_all(2, width)

    def block(j, carry):
        rows = pl.ds(pl.multiple_of(j * CH, CH), CH)
        factors = dot(lift[rows, :], hot)
        values = []
        square = jnp.zeros((CH, 1), f32)
        for p in range(pairs):
            cols = slice(128 * p, 128 * (p + 1))
            lifted = (q8[rows, cols].astype(f32) * factors[:, cols]).astype(bf16)
            lifts[rows, cols] = lifted
            value = attended[rows, cols] + dot(lifted, states[p])
            values.append(value)
            square += jnp.sum(value * value, axis=1, keepdims=True)
        here = jnp.concatenate(values, axis=1)
        scale = lax.rsqrt(square * (1.0 / width) + 1e-06)
        normed[rows, :] = (here * scale).astype(bf16)
        grad = grad_normed[rows, :].astype(f32)
        along = jnp.mean(here * grad, axis=1, keepdims=True)
        grad_full[rows, :] = (scale * grad - here * (scale * scale * scale * along)).astype(bf16)
        return carry

    lax.fori_loop(0, blocks, block, 0, unroll=True)
    for p in range(pairs):
        cols = slice(128 * p, 128 * (p + 1))
        memory[p] = jnp.where(mask, dot(lifts[:, cols], grad_full[:, cols], TN), 0.0)
    write_state(send, memory, fade_t[blocks - 1][:, CH - 1 : CH], pairs)
    rows_in.wait()
    for n in range(0, width, WIDE):
        cols = slice(n, n + WIDE)
        attended[:, cols] = x[:, cols].astype(f32) + dot(normed[...], mine[:, cols])
    sender = Sender(encoded, wide, narrow, out_sems, pairs)

    def put(j, carry):
        sender.put(j, attended[pl.ds(pl.multiple_of(j * CH, CH), CH), :])
        return carry

    lax.fori_loop(0, blocks, put, 0)
    sender.finish(blocks)
    store.wait()


def backward_local(
    info, q8, keys_in, values_in, fade, fade_t, marks, grad_full, states, incoming,
    grads_in, weights,
    grad_keys, grad_values, partial,
    memory, grad_q, grads, mine, keys, values, sems, key_sems, value_sems,
):
    for j in reversed(range(q8.shape[0] // CH)):
        rows_copy(keys_in, keys, key_sems, j).start()
        rows_copy(values_in, values, value_sems, j).start()
    arrival = fetched(grads_in, grads, sems.at[0])
    fetch = fetched(weights.at[info[0], 0], mine, sems.at[1])
    slots, width = q8.shape
    pairs = width // 128
    blocks = slots // CH
    low, high = halves()
    lower = iota((CH, 128), 1) < 64
    mask = block_mask()
    memory[...] = jnp.zeros(memory.shape, f32)

    def block(i, carry):
        j = blocks - 1 - i
        rows_copy(keys_in, keys, key_sems, j).wait()
        rows_copy(values_in, values, value_sems, j).wait()
        rows = pl.ds(pl.multiple_of(j * CH, CH), CH)
        edge = marks[j]
        for p in range(pairs):
            cols = slice(128 * p, 128 * (p + 1))
            start, end = edge[p : p + 1, :], edge[pairs + p : pairs + p + 1, :]
            qp, kp, vp = q8[rows, cols], keys[rows, cols], values[rows, cols]
            da = grad_full[rows, cols]
            ks, vs = stacked(kp, low, high), stacked(vp, low, high)
            fading, g = decay_pair(fade, fade_t, rows, j, p)
            mix = (dot(qp, ks, NT) * fading).astype(bf16)
            grad_scores = (dot(da, vs, NT) * fading).astype(bf16)
            lift = jnp.exp(g - start)
            fall = jnp.exp(end - g)
            state = states[j, p].astype(f32) + jnp.exp(start) * incoming[p]
            state = unfolded(state, mask).astype(bf16)
            grad_q[rows, cols] = (
                0.125 * (dot(grad_scores, ks) + lift * dot(da, state, NT))
            ).astype(bf16)
            gk = dot(grad_scores, qp, TN)
            gv = dot(mix, da, TN)
            now = memory[p]
            narrow = now.astype(bf16)
            kf = (kp.astype(f32) * fall).astype(bf16)
            grad_keys[rows, cols] = jnp.where(lower, gk[0:CH], gk[CH:]) + fall * dot(vp, narrow, NT)
            grad_values[rows, cols] = jnp.where(lower, gv[0:CH], gv[CH:]) + dot(kf, narrow)
            lifted = (qp.astype(f32) * lift).astype(bf16)
            memory[p] = jnp.exp(end - start) * now + jnp.where(mask, dot(lifted, da, TN), 0.0)
        return carry

    lax.fori_loop(0, blocks, block, 0, unroll=True)
    arrival.wait()
    fetch.wait()
    for n in range(0, width, WIDE):
        cols = slice(n, n + WIDE)
        partial[:, cols] = grads[:, cols].astype(f32) + dot(grad_q[...], mine[cols, :], NT)


def backward_finish(
    info, partial, grad_keys, grad_values, keys_in, values_in, fall, weights, partner, *rest
):
    received = rest[:-12]
    out, mine, wide, narrow, states, gk, gv, total, keys, values, sems, out_sems = rest[-12:]
    keys_here = fetched(keys_in, keys, sems.at[1])
    values_here = fetched(values_in, values, sems.at[2])
    fetch = fetched(weights.at[info[0], pl.ds(1, 2)], mine, sems.at[0])
    slots, width = partial.shape
    pairs = width // 128
    blocks = slots // CH
    mask = block_mask()
    arrived = gathered_state((1 - info[1]).astype(f32), partner, received, pairs)
    for p, state in enumerate(arrived):
        states[p] = unfolded(state, mask).astype(bf16)
    hot = spread_all(2, width)
    keys_here.wait()
    values_here.wait()
    for p in range(pairs):
        cols = slice(128 * p, 128 * (p + 1))
        factor = dot(fall[...], hot[:, cols])
        kf = (keys[:, cols].astype(f32) * factor).astype(bf16)
        state = states[p]
        gk[:, cols] = (grad_keys[:, cols] + factor * dot(values[:, cols], state, NT)).astype(bf16)
        gv[:, cols] = (grad_values[:, cols] + dot(kf, state)).astype(bf16)
    fetch.wait()
    for n in range(0, width, WIDE):
        cols = slice(n, n + WIDE)
        total[:, cols] = (
            partial[:, cols] + dot(gk[...], mine[0, cols, :], NT) + dot(gv[...], mine[1, cols, :], NT)
        )
    sender = Sender(out, wide, narrow, out_sems, pairs)

    def put(j, carry):
        sender.put(j, total[pl.ds(pl.multiple_of(j * CH, CH), CH), :])
        return carry

    lax.fori_loop(0, blocks, put, 0)
    sender.finish(blocks)


def swapped(value, axis):
    return lax.ppermute(value, axis, [(i, i ^ 1) for i in range(lax.axis_size(axis))])


def exchange(value, axis, sign):
    count = lax.axis_size(axis)
    return [
        lax.ppermute(
            value, axis, [(i, i + sign * k) for i in range(count) if 0 <= i + sign * k < count]
        )
        for k in range(2, count, 2)
    ]


def regroup(value):
    return lax.all_to_all(value, "log", split_axis=0, concat_axis=0, tiled=True)


def shards(events, owner_ids, elapsed, resets, decay_rates, weights, cotangent):
    rows, width = events.shape[2:]
    owners = lax.axis_size("log")
    cap = 5 * rows // (4 * owners)
    slots = owners * cap
    pairs = width // 128
    blocks = slots // CH
    per = cap * pairs
    flat = pltpu.VMEM((slots * pairs, 128), f32)
    state_vmem = pltpu.VMEM((pairs, 128, 128), f32)
    state_msg = ((64 * pairs + 8, 128), bf16)
    wide16, wide32 = ((slots, width), bf16), ((slots, width), f32)

    tower = lax.axis_index("log") // (owners // decay_rates.shape[0])
    info = jnp.stack([tower, lax.axis_index("ctx") % 2]).astype(jnp.int32)
    sem = pltpu.SemaphoreType.DMA

    message, spots = call(
        pack_events,
        [((owners, per + 8, 128), bf16), ((2, rows), jnp.int32)],
        [
            owner_ids.reshape(1, rows),
            events.reshape(rows, width),
            elapsed.reshape(1, rows),
            resets.reshape(1, rows),
        ],
        [
            flat,
            pltpu.VMEM((slots, rows), bf16),
            pltpu.VMEM((1, rows), jnp.int32),
            pltpu.VMEM((rows, width), bf16),
            pltpu.VMEM((1, rows), f32),
            pltpu.VMEM((1, rows), f32),
            pltpu.SemaphoreType.DMA((4,)),
        ],
        {0: HBM, 1: HBM, 2: HBM, 3: HBM},
    )
    events_in = regroup(message)
    flat_msg = ((slots * pairs, 128), bf16)
    message, back, expand, own_lanes = call(
        pack_grads,
        [
            flat_msg, ((rows, slots), bf16), ((slots, owners * 8), bf16), ((slots, 128), bf16),
        ],
        [info, spots, cotangent.reshape(rows, width)],
        [flat, pltpu.VMEM(*flat_msg), pltpu.VMEM((rows, slots), bf16), sem((2,))],
        {0: SMEM},
        (0, 1),
    )
    grads_in = regroup(message.reshape(owners, per, 128))
    one = pltpu.VMEM((width, width), bf16)
    two = pltpu.VMEM((2, width, width), bf16)
    half_states = ((pairs, 64, 128), f32)
    block_wide = pltpu.VMEM((CH * pairs, 128), f32)
    flat_narrow = pltpu.VMEM(*flat_msg)
    rows16, rows32 = pltpu.VMEM(*wide16), pltpu.VMEM(*wide32)
    narrow_states = pltpu.VMEM((pairs, 128, 128), bf16)
    x, keys, values, keys_far, values_far, fade, fade_t, marks, fall, send = call(
        forward_state,
        [
            wide16, wide16, wide16, wide16, wide16, ((slots, 128), f32), ((blocks, 8, 128), f32),
            ((blocks, 2 * pairs, 128), f32), ((slots, 128), bf16), state_msg,
        ],
        [info, decay_rates, events_in, weights, expand, own_lanes],
        [flat, state_vmem, pltpu.VMEM((owners, per + 8, 128), bf16), two, rows16, sem((5,))],
        {0: SMEM, 1: SMEM, 2: HBM, 3: HBM},
        (0, 3, 4),
    )
    partner = swapped(send, "ctx")
    (joined,) = call(join_ahead, [state_msg], [info, send, partner], (), {0: SMEM})
    received = exchange(joined, "ctx", 1)
    q8, attended, kept, lift = call(
        attend,
        [wide16, wide32, ((blocks, pairs, 64, 128), bf16), ((slots, 128), bf16)],
        [info, x, weights, keys, values, fade, fade_t, marks],
        [state_vmem, rows32, rows16, one, sem((2,)), sem((blocks,))],
        {0: SMEM, 1: HBM, 2: HBM},
        (1,),
    )
    message, grads, grad_full, incoming, send = call(
        turn,
        [flat_msg, wide16, wide16, half_states, state_msg],
        [info, q8, lift, fade_t, attended, x, weights, grads_in, partner, *received],
        [
            flat, pltpu.VMEM((owners, per, 128), bf16), one, rows16, rows32, rows16, rows16, rows16,
            rows16, block_wide, flat_narrow, narrow_states, state_vmem, sem((5,)), sem((blocks,)),
        ],
        {0: SMEM, 4: HBM, 5: HBM, 6: HBM, 7: ANY},
        (0, 1),
    )
    partner = swapped(send, "ctx")
    encoded_in = regroup(message.reshape(owners, per, 128))
    grad_keys, grad_values, partial = call(
        backward_local,
        [wide32, wide32, wide32],
        [
            info, q8, keys_far, values_far, fade, fade_t, marks, grad_full, kept, incoming, grads,
            weights,
        ],
        [
            state_vmem, rows16, rows16, one, rows16, rows16, sem((2,)), sem((blocks,)),
            sem((blocks,)),
        ],
        {0: SMEM, 2: HBM, 3: HBM, 10: HBM, 11: HBM},
    )
    (joined,) = call(join_back, [state_msg], [info, send, partner], (), {0: SMEM})
    received = exchange(joined, "ctx", -1)
    (message,) = call(
        backward_finish,
        [flat_msg],
        [
            info, partial, grad_keys, grad_values, keys_far, values_far, fall, weights, partner,
            *received,
        ],
        [
            two, block_wide, flat_narrow, narrow_states,
            rows16, rows16, rows32, rows16, rows16, sem((3,)), sem((blocks,)),
        ],
        {0: SMEM, 4: HBM, 5: HBM, 7: HBM},
        (0,),
    )
    grad_in = regroup(message.reshape(owners, per, 128))
    (encoded,) = call(unpack_rows, [((rows, width), bf16)], [back, encoded_in], [flat])
    (grad,) = call(unpack_rows, [((rows, width), bf16)], [back, grad_in], [flat])
    return encoded.reshape(events.shape), grad.reshape(events.shape)


def solution(mesh):
    wide = P("ctx", "log", None, None)
    flat = P("ctx", "log", None)
    return jax.shard_map(
        shards,
        mesh=mesh,
        in_specs=(wide, wide, flat, flat, P(), P(), wide),
        out_specs=(wide, wide),
        check_vma=False,
    )
```

```python
import jax
import jax.numpy as jnp
from jax import lax
from jax.experimental import pallas as pl
from jax.experimental.pallas import tpu as pltpu
from jax.sharding import PartitionSpec as P


bf16 = jnp.bfloat16
f32 = jnp.float32
CH = 128
NN = (((1,), (0,)), ((), ()))
NT = (((1,), (1,)), ((), ()))
TN = (((0,), (0,)), ((), ()))
EXACT = lax.Precision.HIGHEST
LIMIT = 16 << 20
WIDE = 256


def dot(a, b, dims=NN, precision=None):
    return lax.dot_general(a, b, dims, preferred_element_type=f32, precision=precision)


def iota(shape, dim):
    return lax.broadcasted_iota(jnp.int32, shape, dim)


def ones_where(cond, dtype=bf16):
    return jnp.where(cond, 1.0, 0.0).astype(dtype)


VMEM = pl.BlockSpec(memory_space=pltpu.VMEM)
SMEM = pl.BlockSpec(memory_space=pltpu.SMEM)
HBM = pl.BlockSpec(memory_space=pltpu.HBM)


def call(body, outs, ins, scratch=(), spaces=None, out_hbm=()):
    ins = [
        pltpu.with_memory_space_constraint(v, pltpu.HBM) if (spaces or {}).get(i) is HBM else v
        for i, v in enumerate(ins)
    ]
    return pl.pallas_call(
        body,
        out_shape=[
            pltpu.HBM(s, d) if i in out_hbm else jax.ShapeDtypeStruct(s, d)
            for i, (s, d) in enumerate(outs)
        ],
        in_specs=[(spaces or {}).get(i, VMEM) for i in range(len(ins))],
        out_specs=[HBM if i in out_hbm else VMEM for i in range(len(outs))],
        scratch_shapes=list(scratch),
        compiler_params=pltpu.CompilerParams(vmem_limit_bytes=LIMIT),
    )(*ins)


def write_rows(scratch, tile_of, parts):
    count = scratch.shape[0] // parts
    for j in range(0, parts, 2):
        tile = tile_of(slice(128 * j, 128 * j + WIDE))
        scratch[pl.ds(j, count, stride=parts), :] = tile[:, 0:128]
        scratch[pl.ds(j + 1, count, stride=parts), :] = tile[:, 128:WIDE]


def write_message(message, scratch, tile_of, width):
    write_rows(scratch, tile_of, width // 128)
    owners = message.shape[0]
    per = scratch.shape[0] // owners
    message[:, 0:per, :] = scratch[...].reshape(owners, per, 128).astype(bf16)


def read_message(message, scratch, width):
    parts = width // 128
    count = scratch.shape[0] // parts
    owners = message.shape[0]
    per = scratch.shape[0] // owners
    scratch[...] = message[:, 0:per, :].astype(f32).reshape(scratch.shape)
    return [scratch[pl.ds(j, count, stride=parts), :] for j in range(parts)]


class Sender:
    def __init__(self, out, wide, narrow, sems, parts):
        self.out, self.wide, self.narrow, self.sems, self.parts = out, wide, narrow, sems, parts

    def copy(self, j):
        size = CH * self.parts
        span = pl.ds(pl.multiple_of(j * size, size), size)
        return pltpu.make_async_copy(self.narrow.at[span, :], self.out.at[span, :], self.sems.at[j])

    def put(self, j, value):
        size = CH * self.parts
        for p in range(self.parts):
            self.wide[pl.ds(p, CH, stride=self.parts), :] = value[:, 128 * p : 128 * (p + 1)]
        span = pl.ds(pl.multiple_of(j * size, size), size)
        self.narrow[span, :] = self.wide[...].astype(bf16)
        self.copy(j).start()

    def finish(self, blocks):
        for j in range(blocks):
            self.copy(j).wait()


def fetched(source, target, sem):
    copy = pltpu.make_async_copy(source, target, sem)
    copy.start()
    return copy


def rows_copy(source, target, sems, j):
    rows = pl.ds(pl.multiple_of(j * CH, CH), CH)
    return pltpu.make_async_copy(source.at[rows, :], target.at[rows, :], sems.at[j])


def parts_of(value, count):
    group = iota(value.shape, 1) >> 3
    out = jnp.zeros(value.shape, f32)
    for n in range(count):
        part = value.astype(bf16).astype(f32)
        out = jnp.where(group == n, part, out)
        value = value - part
    return out.astype(bf16)


def spread_all(count, width):
    q, c = iota((128, width), 0), iota((128, width), 1)
    return ones_where((q < 8 * count) & ((q & 7) == (c >> 6)))


def pack_events(
    owner_in, events_in, elapsed_in, resets_in, message, spots,
    scratch, place, owner, events, elapsed, resets, sems,
):
    copies = [
        pltpu.make_async_copy(source, target, sems.at[i])
        for i, (source, target) in enumerate(
            (
                (owner_in, owner),
                (elapsed_in, elapsed),
                (resets_in, resets),
                (events_in, events),
            )
        )
    ]
    for copy in copies:
        copy.start()
    copies[0].wait()
    rows, width = events.shape
    owners = message.shape[0]
    slots = place.shape[0]
    cap = slots // owners
    own = owner[...]
    hit = iota((owners, rows), 0) == own
    earlier = ones_where(iota((rows, rows), 0) < iota((rows, rows), 1))
    before = dot(ones_where(hit), earlier)
    rank = jnp.sum(jnp.where(hit, before, 0.0), axis=0, keepdims=True).astype(jnp.int32)
    spots[0:1, :] = own
    spots[1:2, :] = own * cap + rank
    place[...] = ones_where(iota((slots, rows), 0) == own * cap + rank)
    for copy in copies[1:]:
        copy.wait()
    write_message(
        message,
        scratch,
        lambda cols: dot(place[...], events[:, cols]),
        width,
    )
    lanes = iota((128, rows), 0)
    times = jnp.zeros((owners, 128), f32)
    for k, ref in enumerate((elapsed, resets)):
        value = ref[...]
        high = value.astype(bf16).astype(f32)
        for m, part in enumerate((high, value - high)):
            spot = ones_where(lanes == rank + cap * (2 * k + m))
            times += dot(jnp.where(hit, part, 0.0).astype(bf16), spot, NT)
    spread = ones_where(iota((owners * 8, owners), 0) == 8 * iota((owners * 8, owners), 1))
    extra = dot(spread, times.astype(bf16)).reshape(owners, 8, 128)
    per = scratch.shape[0] // owners
    message[:, per : per + 8, :] = extra.astype(bf16)


def pack_grads(info, spots, grads, message, back, expand, mine, scratch, narrow, turned, sems):
    rows, width = grads.shape
    slots = turned.shape[1]
    place = ones_where(iota((slots, rows), 0) == spots[1:2, :])
    write_rows(scratch, lambda cols: dot(place, grads[:, cols]), width // 128)
    narrow[...] = scratch[...].astype(bf16)
    copies = [fetched(narrow, message, sems.at[0])]
    same = ones_where(iota((rows, rows), 0) == iota((rows, rows), 1))
    turned[...] = dot(same, place, NT).astype(bf16)
    copies.append(fetched(turned, back, sems.at[1]))
    cap = slots * 8 // expand.shape[1]
    r, c = iota(expand.shape, 0), iota(expand.shape, 1)
    expand[...] = ones_where(((c & 7) == 0) & (8 * r >= cap * c) & (8 * r < cap * (c + 8)))
    row, lane = iota(mine.shape, 0).astype(f32), iota(mine.shape, 1).astype(f32)
    s = row - cap * jnp.floor((row + 0.5) * (1.0 / cap))
    hit = (lane == s) | (lane == s + cap) | (lane == s + 2 * cap) | (lane == s + 3 * cap)
    mine[...] = ones_where(hit)
    for copy in copies:
        copy.wait()


def unpack_rows(back, message, out, scratch):
    width = out.shape[1]
    parts = read_message(message, scratch, width)
    for j in range(0, len(parts), 2):
        both = jnp.concatenate([parts[j], parts[j + 1]], axis=1).astype(bf16)
        out[:, 128 * j : 128 * j + WIDE] = dot(back[...], both).astype(bf16)


def halves():
    low = ones_where(iota((CH, 128), 1) < 64)
    return low, ones_where(iota((CH, 128), 1) >= 64)


def block_mask():
    return (iota((128, 128), 0) < 64) == (iota((128, 128), 1) < 64)


def stacked(value, low, high):
    return jnp.concatenate([value * low, value * high], axis=0)


def decay_pair(fade, fade_t, rows, j, p):
    causal = iota((CH, CH), 0) >= iota((CH, CH), 1)
    both, wide = [], []
    turned = fade_t[j]
    here = fade[rows, :]
    for h in (2 * p, 2 * p + 1):
        column = jnp.broadcast_to(here[:, h : h + 1], (CH, CH))
        wide.append(column)
        spread = column - turned[h : h + 1, :]
        both.append(jnp.exp(jnp.where(causal, spread, -1e30)))
    return jnp.concatenate(both, axis=1), jnp.where(iota((CH, CH), 1) < 64, wide[0], wide[1])


def folded(full):
    return full[0:64, :] + full[64:128, :]


def unfolded(half, mask):
    return jnp.where(mask, jnp.concatenate([half, half], axis=0), 0.0)


def set_states(states, arrived):
    mask = block_mask()
    none = jnp.zeros((128, 128), f32)
    for n in range(states.shape[0]):
        first = jnp.concatenate([unfolded(arrived[2 * n], mask), none], axis=1)
        second = jnp.concatenate([none, unfolded(arrived[2 * n + 1], mask)], axis=1)
        states[n] = jnp.concatenate([first, second], axis=0).astype(bf16)


def set_memory(memory, both, n):
    mask = block_mask()
    memory[2 * n] = jnp.where(mask, both[0:128, 0:128], 0.0)
    memory[2 * n + 1] = jnp.where(mask, both[128:WIDE, 128:WIDE], 0.0)


def write_state(send, state, last, pairs):
    for p in range(pairs):
        send[64 * p : 64 * (p + 1), :] = folded(state[p]).astype(bf16)
    write_marks(send, last, pairs)


def write_marks(send, last, pairs):
    last = jnp.broadcast_to(last, (8, 128))
    high = last.astype(bf16).astype(f32)
    lane = iota(last.shape, 1)
    send[64 * pairs : 64 * pairs + 8, :] = jnp.where(lane < 64, high, last - high).astype(bf16)


def read_marks(ref, pairs):
    marks = ref[64 * pairs : 64 * pairs + 8, :].astype(f32)
    return marks[:, 0:1] + marks[:, 64:65]


def lane_factors(log, p):
    return jnp.exp(
        jnp.where(
            iota((1, 128), 1) < 64,
            jnp.broadcast_to(log[2 * p : 2 * p + 1, :], (1, 128)),
            jnp.broadcast_to(log[2 * p + 1 : 2 * p + 2, :], (1, 128)),
        )
    )


def join_pair(near, far, out, pairs):
    log = read_marks(near, pairs)
    for p in range(pairs):
        rows = slice(64 * p, 64 * (p + 1))
        joined = near[rows, :].astype(f32) + lane_factors(log, p) * far[rows, :].astype(f32)
        out[rows, :] = joined.astype(bf16)
    write_marks(out, log + read_marks(far, pairs), pairs)


def join_ahead(info, own, other, out):
    join(info[1] == 1, own, other, out)


def join_back(info, own, other, out):
    join(info[1] == 0, own, other, out)


def join(own_is_near, own, other, out):
    pairs = own.shape[0] // 64

    @pl.when(own_is_near)
    def _():
        join_pair(own, other, out, pairs)

    @pl.when(jnp.logical_not(own_is_near))
    def _():
        join_pair(other, own, out, pairs)


def gathered_state(partner_counts, partner, received, pairs):
    log = read_marks(partner, pairs) * partner_counts
    total = [partner[64 * p : 64 * (p + 1), :].astype(f32) * partner_counts for p in range(pairs)]
    for ref in received:
        for p in range(pairs):
            total[p] += lane_factors(log, p) * ref[64 * p : 64 * (p + 1), :].astype(f32)
        log = log + read_marks(ref, pairs)
    return total


def forward_state(
    info, rates, message, weights, expand, own_lanes,
    x_out, keys, values, keys_out, values_out, fade, fade_t, marks, fall, send,
    scratch, memory, mine, x, sems,
):
    fetch = fetched(weights.at[info[0], pl.ds(1, 2)], mine, sems.at[1])
    slots, width = x.shape
    pairs = width // 128
    blocks = slots // CH
    owners = message.shape[0]
    cap = slots // owners
    per = cap * pairs
    for j, part in enumerate(read_message(message, scratch, width)):
        x[:, 128 * j : 128 * (j + 1)] = part.astype(bf16)
    stores = [fetched(x, x_out, sems.at[2])]
    times = message[:, per : per + 8, :].astype(f32).reshape(owners * 8, 128).astype(bf16)
    own = dot(expand[...], times).astype(bf16) * own_lanes[...]
    kind, head = iota((128, 128), 0), iota((128, 128), 1) & 7
    rate = jnp.zeros((128, 128), f32)
    for h in range(rates.shape[1]):
        rate = jnp.where(head == h, rates[info[0], h], rate)
    to_heads = jnp.where(kind < 2 * cap, -rate, jnp.where(kind < 4 * cap, -1.0, 0.0))
    tri = ones_where(iota((CH, CH), 0) >= iota((CH, CH), 1))
    before = jnp.zeros((1, 128), f32)
    start = jnp.zeros((1, 128), f32)
    ends = []
    for j in range(blocks):
        running = dot(tri, own[CH * j : CH * (j + 1), :]) + before
        before = running[CH - 1 : CH, :]
        here = dot(running, to_heads, NN, EXACT)
        fade[CH * j : CH * (j + 1), :] = here
        fade_t[j] = here.T[0:8, :]
        start = here[CH - 1 : CH, :]
        ends.append(start)
    ends = jnp.concatenate(ends + [jnp.zeros((8 - blocks, 128), f32)], axis=0)
    wide_ends = dot(parts_of(ends, 3), spread_all(3, width))
    for j in range(blocks):
        for p in range(pairs):
            cols = slice(128 * p, 128 * (p + 1))
            marks[j, pairs + p : pairs + p + 1, :] = wide_ends[j : j + 1, cols]
            if j == 0:
                marks[j, p : p + 1, :] = jnp.zeros((1, 128), f32)
            else:
                marks[j, p : p + 1, :] = wide_ends[j - 1 : j, cols]
    fall[...] = parts_of(jnp.exp(start - fade[...]), 2)
    fetch.wait()
    for n in range(0, width, WIDE):
        cols = slice(n, n + WIDE)
        keys[:, cols] = dot(x[...], mine[0, :, cols]).astype(bf16)
        values[:, cols] = dot(x[...], mine[1, :, cols]).astype(bf16)
    hot = spread_all(2, width)
    for n in range(pairs // 2):
        cols = slice(WIDE * n, WIDE * (n + 1))
        kf = (keys[:, cols].astype(f32) * dot(fall[...], hot[:, cols])).astype(bf16)
        set_memory(memory, dot(kf, values[:, cols], TN), n)
    stores.append(fetched(keys, keys_out, sems.at[3]))
    stores.append(fetched(values, values_out, sems.at[4]))
    write_state(send, memory, fade_t[blocks - 1][:, CH - 1 : CH], pairs)
    for store in stores:
        store.wait()


def attend(
    info, x_in, weights, keys, values, fade, fade_t, marks,
    q8, attended_out, states, lift,
    memory, attended, x, mine, in_sems, sems,
):
    arrival = fetched(x_in, x, in_sems.at[0])
    fetch = fetched(weights.at[info[0], 0], mine, in_sems.at[1])
    lift[...] = parts_of(jnp.exp(fade[...]), 2)
    arrival.wait()
    fetch.wait()
    for n in range(0, x.shape[1], WIDE):
        cols = slice(n, n + WIDE)
        query = dot(x[...], mine[:, cols]).astype(bf16).astype(f32)
        q8[:, cols] = (query * 0.125).astype(bf16)
    slots, width = q8.shape
    pairs = width // 128
    low, high = halves()
    mask = block_mask()
    memory[...] = jnp.zeros(memory.shape, f32)

    def block(j, carry):
        rows = pl.ds(pl.multiple_of(j * CH, CH), CH)
        edge = marks[j]
        for p in range(pairs):
            cols = slice(128 * p, 128 * (p + 1))
            start, end = edge[p : p + 1, :], edge[pairs + p : pairs + p + 1, :]
            qp, kp, vp = q8[rows, cols], keys[rows, cols], values[rows, cols]
            scores = dot(qp, stacked(kp, low, high), NT)
            fading, g = decay_pair(fade, fade_t, rows, j, p)
            mix = (scores * fading).astype(bf16)
            within = dot(mix, stacked(vp, low, high))
            now = memory[p]
            states[j, p] = folded(now).astype(bf16)
            lifted = (qp.astype(f32) * jnp.exp(g - start)).astype(bf16)
            attended[rows, cols] = within + dot(lifted, now.astype(bf16))
            kf = (kp.astype(f32) * jnp.exp(end - g)).astype(bf16)
            memory[p] = jnp.exp(end - start) * now + jnp.where(mask, dot(kf, vp, TN), 0.0)
        rows_copy(attended, attended_out, sems, j).start()
        return carry

    lax.fori_loop(0, slots // CH, block, 0, unroll=True)
    for j in range(slots // CH):
        rows_copy(attended, attended_out, sems, j).wait()


def turn(info, q8, lift, fade_t, attended_in, x_in, weights, message, partner, *rest):
    received = rest[:-19]
    (
        encoded, grads_out, grad_full, incoming, send,
        scratch, mine, x, attended, grads, grad_normed, normed, lifts,
        wide, narrow, states, memory, sems, out_sems,
    ) = rest[-19:]
    fetch = fetched(weights.at[info[0], 3], mine, sems.at[0])
    rows_in = fetched(x_in, x, sems.at[1])
    attended_here = fetched(attended_in, attended, sems.at[3])
    slots, width = x.shape
    pairs = width // 128
    blocks = slots // CH
    arrived = gathered_state(info[1].astype(f32), partner, received, pairs)
    for p in range(pairs):
        incoming[p] = arrived[p]
    set_states(states, arrived)
    for j, part in enumerate(read_message(message, scratch, width)):
        grads[:, 128 * j : 128 * (j + 1)] = part.astype(bf16)
    store = fetched(grads, grads_out, sems.at[4])
    fetch.wait()
    for n in range(0, width, WIDE):
        cols = slice(n, n + WIDE)
        grad_normed[:, cols] = dot(grads[...], mine[cols, :], NT).astype(bf16)
    attended_here.wait()

    hot = spread_all(2, width)

    def block(j, carry):
        rows = pl.ds(pl.multiple_of(j * CH, CH), CH)
        factors = dot(lift[rows, :], hot)
        values = []
        square = jnp.zeros((CH, 1), f32)
        for n in range(pairs // 2):
            cols = slice(WIDE * n, WIDE * (n + 1))
            lifted = (q8[rows, cols].astype(f32) * factors[:, cols]).astype(bf16)
            lifts[rows, cols] = lifted
            value = attended[rows, cols] + dot(lifted, states[n])
            values.append(value)
            square += jnp.sum(value * value, axis=1, keepdims=True)
        here = jnp.concatenate(values, axis=1)
        scale = lax.rsqrt(square * (1.0 / width) + 1e-06)
        normed[rows, :] = (here * scale).astype(bf16)
        grad = grad_normed[rows, :].astype(f32)
        along = jnp.mean(here * grad, axis=1, keepdims=True)
        grad_full[rows, :] = (scale * grad - here * (scale * scale * scale * along)).astype(bf16)
        return carry

    lax.fori_loop(0, blocks, block, 0, unroll=True)
    for n in range(pairs // 2):
        cols = slice(WIDE * n, WIDE * (n + 1))
        set_memory(memory, dot(lifts[:, cols], grad_full[:, cols], TN), n)
    write_state(send, memory, fade_t[blocks - 1][:, CH - 1 : CH], pairs)
    rows_in.wait()
    for n in range(0, width, WIDE):
        cols = slice(n, n + WIDE)
        attended[:, cols] = x[:, cols].astype(f32) + dot(normed[...], mine[:, cols])
    sender = Sender(encoded, wide, narrow, out_sems, pairs)

    def put(j, carry):
        sender.put(j, attended[pl.ds(pl.multiple_of(j * CH, CH), CH), :])
        return carry

    lax.fori_loop(0, blocks, put, 0)
    sender.finish(blocks)
    store.wait()


def backward_local(
    info, q8, keys_in, values_in, fade, fade_t, marks, grad_full, states, incoming,
    grads_in, weights,
    grad_keys, grad_values, partial,
    memory, grad_q, grads, mine, keys, values, sems, key_sems, value_sems,
):
    for j in reversed(range(q8.shape[0] // CH)):
        rows_copy(keys_in, keys, key_sems, j).start()
        rows_copy(values_in, values, value_sems, j).start()
    arrival = fetched(grads_in, grads, sems.at[0])
    fetch = fetched(weights.at[info[0], 0], mine, sems.at[1])
    slots, width = q8.shape
    pairs = width // 128
    blocks = slots // CH
    low, high = halves()
    lower = iota((CH, 128), 1) < 64
    mask = block_mask()
    memory[...] = jnp.zeros(memory.shape, f32)

    def block(i, carry):
        j = blocks - 1 - i
        rows_copy(keys_in, keys, key_sems, j).wait()
        rows_copy(values_in, values, value_sems, j).wait()
        rows = pl.ds(pl.multiple_of(j * CH, CH), CH)
        edge = marks[j]
        for p in range(pairs):
            cols = slice(128 * p, 128 * (p + 1))
            start, end = edge[p : p + 1, :], edge[pairs + p : pairs + p + 1, :]
            qp, kp, vp = q8[rows, cols], keys[rows, cols], values[rows, cols]
            da = grad_full[rows, cols]
            ks, vs = stacked(kp, low, high), stacked(vp, low, high)
            fading, g = decay_pair(fade, fade_t, rows, j, p)
            mix = (dot(qp, ks, NT) * fading).astype(bf16)
            grad_scores = (dot(da, vs, NT) * fading).astype(bf16)
            lift = jnp.exp(g - start)
            fall = jnp.exp(end - g)
            state = states[j, p].astype(f32) + jnp.exp(start) * incoming[p]
            state = unfolded(state, mask).astype(bf16)
            grad_q[rows, cols] = (
                0.125 * (dot(grad_scores, ks) + lift * dot(da, state, NT))
            ).astype(bf16)
            gk = dot(grad_scores, qp, TN)
            gv = dot(mix, da, TN)
            now = memory[p]
            narrow = now.astype(bf16)
            kf = (kp.astype(f32) * fall).astype(bf16)
            grad_keys[rows, cols] = jnp.where(lower, gk[0:CH], gk[CH:]) + fall * dot(vp, narrow, NT)
            grad_values[rows, cols] = jnp.where(lower, gv[0:CH], gv[CH:]) + dot(kf, narrow)
            lifted = (qp.astype(f32) * lift).astype(bf16)
            memory[p] = jnp.exp(end - start) * now + jnp.where(mask, dot(lifted, da, TN), 0.0)
        return carry

    lax.fori_loop(0, blocks, block, 0, unroll=True)
    arrival.wait()
    fetch.wait()
    for n in range(0, width, WIDE):
        cols = slice(n, n + WIDE)
        partial[:, cols] = grads[:, cols].astype(f32) + dot(grad_q[...], mine[cols, :], NT)


def backward_finish(
    info, partial, grad_keys, grad_values, keys_in, values_in, fall, weights, partner, *rest
):
    received = rest[:-12]
    out, mine, wide, narrow, states, gk, gv, total, keys, values, sems, out_sems = rest[-12:]
    keys_here = fetched(keys_in, keys, sems.at[1])
    values_here = fetched(values_in, values, sems.at[2])
    fetch = fetched(weights.at[info[0], pl.ds(1, 2)], mine, sems.at[0])
    slots, width = partial.shape
    pairs = width // 128
    blocks = slots // CH
    set_states(states, gathered_state((1 - info[1]).astype(f32), partner, received, pairs))
    hot = spread_all(2, width)
    keys_here.wait()
    values_here.wait()
    for n in range(pairs // 2):
        cols = slice(WIDE * n, WIDE * (n + 1))
        factor = dot(fall[...], hot[:, cols])
        kf = (keys[:, cols].astype(f32) * factor).astype(bf16)
        gk[:, cols] = (grad_keys[:, cols] + factor * dot(values[:, cols], states[n], NT)).astype(bf16)
        gv[:, cols] = (grad_values[:, cols] + dot(kf, states[n])).astype(bf16)
    fetch.wait()
    for n in range(0, width, WIDE):
        cols = slice(n, n + WIDE)
        total[:, cols] = (
            partial[:, cols] + dot(gk[...], mine[0, cols, :], NT) + dot(gv[...], mine[1, cols, :], NT)
        )
    sender = Sender(out, wide, narrow, out_sems, pairs)

    def put(j, carry):
        sender.put(j, total[pl.ds(pl.multiple_of(j * CH, CH), CH), :])
        return carry

    lax.fori_loop(0, blocks, put, 0)
    sender.finish(blocks)


def swapped(value, axis):
    return lax.ppermute(value, axis, [(i, i ^ 1) for i in range(lax.axis_size(axis))])


def exchange(value, axis, sign):
    count = lax.axis_size(axis)
    return [
        lax.ppermute(
            value, axis, [(i, i + sign * k) for i in range(count) if 0 <= i + sign * k < count]
        )
        for k in range(2, count, 2)
    ]


def regroup(value):
    return lax.all_to_all(value, "log", split_axis=0, concat_axis=0, tiled=True)


def shards(events, owner_ids, elapsed, resets, decay_rates, weights, cotangent):
    rows, width = events.shape[2:]
    owners = lax.axis_size("log")
    cap = 5 * rows // (4 * owners)
    slots = owners * cap
    pairs = width // 128
    blocks = slots // CH
    per = cap * pairs
    flat = pltpu.VMEM((slots * pairs, 128), f32)
    state_vmem = pltpu.VMEM((pairs, 128, 128), f32)
    state_msg = ((64 * pairs + 8, 128), bf16)
    wide16, wide32 = ((slots, width), bf16), ((slots, width), f32)

    tower = lax.axis_index("log") // (owners // decay_rates.shape[0])
    info = jnp.stack([tower, lax.axis_index("ctx") % 2]).astype(jnp.int32)
    sem = pltpu.SemaphoreType.DMA

    message, spots = call(
        pack_events,
        [((owners, per + 8, 128), bf16), ((2, rows), jnp.int32)],
        [
            owner_ids.reshape(1, rows),
            events.reshape(rows, width),
            elapsed.reshape(1, rows),
            resets.reshape(1, rows),
        ],
        [
            flat,
            pltpu.VMEM((slots, rows), bf16),
            pltpu.VMEM((1, rows), jnp.int32),
            pltpu.VMEM((rows, width), bf16),
            pltpu.VMEM((1, rows), f32),
            pltpu.VMEM((1, rows), f32),
            pltpu.SemaphoreType.DMA((4,)),
        ],
        {0: HBM, 1: HBM, 2: HBM, 3: HBM},
    )
    events_in = regroup(message)
    flat_msg = ((slots * pairs, 128), bf16)
    message, back, expand, own_lanes = call(
        pack_grads,
        [
            flat_msg, ((rows, slots), bf16), ((slots, owners * 8), bf16), ((slots, 128), bf16),
        ],
        [info, spots, cotangent.reshape(rows, width)],
        [flat, pltpu.VMEM(*flat_msg), pltpu.VMEM((rows, slots), bf16), sem((2,))],
        {0: SMEM},
        (0, 1),
    )
    grads_in = regroup(message.reshape(owners, per, 128))
    one = pltpu.VMEM((width, width), bf16)
    two = pltpu.VMEM((2, width, width), bf16)
    half_states = ((pairs, 64, 128), f32)
    block_wide = pltpu.VMEM((CH * pairs, 128), f32)
    flat_narrow = pltpu.VMEM(*flat_msg)
    rows16, rows32 = pltpu.VMEM(*wide16), pltpu.VMEM(*wide32)
    narrow_states = pltpu.VMEM((pairs // 2, WIDE, WIDE), bf16)
    x, keys, values, keys_far, values_far, fade, fade_t, marks, fall, send = call(
        forward_state,
        [
            wide16, wide16, wide16, wide16, wide16, ((slots, 128), f32), ((blocks, 8, 128), f32),
            ((blocks, 2 * pairs, 128), f32), ((slots, 128), bf16), state_msg,
        ],
        [info, decay_rates, events_in, weights, expand, own_lanes],
        [flat, state_vmem, two, rows16, sem((5,))],
        {0: SMEM, 1: SMEM, 3: HBM},
        (0, 3, 4),
    )
    partner = swapped(send, "ctx")
    (joined,) = call(join_ahead, [state_msg], [info, send, partner], (), {0: SMEM})
    received = exchange(joined, "ctx", 1)
    q8, attended, kept, lift = call(
        attend,
        [wide16, wide32, ((blocks, pairs, 64, 128), bf16), ((slots, 128), bf16)],
        [info, x, weights, keys, values, fade, fade_t, marks],
        [state_vmem, rows32, rows16, one, sem((2,)), sem((blocks,))],
        {0: SMEM, 1: HBM, 2: HBM},
        (1,),
    )
    message, grads, grad_full, incoming, send = call(
        turn,
        [flat_msg, wide16, wide16, half_states, state_msg],
        [info, q8, lift, fade_t, attended, x, weights, grads_in, partner, *received],
        [
            flat, one, rows16, rows32, rows16, rows16, rows16,
            rows16, block_wide, flat_narrow, narrow_states, state_vmem, sem((5,)), sem((blocks,)),
        ],
        {0: SMEM, 4: HBM, 5: HBM, 6: HBM},
        (0, 1),
    )
    partner = swapped(send, "ctx")
    encoded_in = regroup(message.reshape(owners, per, 128))
    grad_keys, grad_values, partial = call(
        backward_local,
        [wide32, wide32, wide32],
        [
            info, q8, keys_far, values_far, fade, fade_t, marks, grad_full, kept, incoming, grads,
            weights,
        ],
        [
            state_vmem, rows16, rows16, one, rows16, rows16, sem((2,)), sem((blocks,)),
            sem((blocks,)),
        ],
        {0: SMEM, 2: HBM, 3: HBM, 10: HBM, 11: HBM},
    )
    (joined,) = call(join_back, [state_msg], [info, send, partner], (), {0: SMEM})
    received = exchange(joined, "ctx", -1)
    (message,) = call(
        backward_finish,
        [flat_msg],
        [
            info, partial, grad_keys, grad_values, keys_far, values_far, fall, weights, partner,
            *received,
        ],
        [
            two, block_wide, flat_narrow, narrow_states,
            rows16, rows16, rows32, rows16, rows16, sem((3,)), sem((blocks,)),
        ],
        {0: SMEM, 4: HBM, 5: HBM, 7: HBM},
        (0,),
    )
    grad_in = regroup(message.reshape(owners, per, 128))
    (encoded,) = call(unpack_rows, [((rows, width), bf16)], [back, encoded_in], [flat])
    (grad,) = call(unpack_rows, [((rows, width), bf16)], [back, grad_in], [flat])
    return encoded.reshape(events.shape), grad.reshape(events.shape)


def solution(mesh):
    wide = P("ctx", "log", None, None)
    flat = P("ctx", "log", None)
    return jax.shard_map(
        shards,
        mesh=mesh,
        in_specs=(wide, wide, flat, flat, P(), P(), wide),
        out_specs=(wide, wide),
        check_vma=False,
    )
```

```python
import jax
import jax.numpy as jnp
from jax import lax
from jax.experimental import pallas as pl
from jax.experimental.pallas import tpu as pltpu
from jax.sharding import PartitionSpec as P


bf16 = jnp.bfloat16
f32 = jnp.float32
CH = 128
NN = (((1,), (0,)), ((), ()))
NT = (((1,), (1,)), ((), ()))
TN = (((0,), (0,)), ((), ()))
EXACT = lax.Precision.HIGHEST
LIMIT = 16 << 20
WIDE = 256


def dot(a, b, dims=NN, precision=None):
    return lax.dot_general(a, b, dims, preferred_element_type=f32, precision=precision)


def iota(shape, dim):
    return lax.broadcasted_iota(jnp.int32, shape, dim)


def ones_where(cond, dtype=bf16):
    return jnp.where(cond, 1.0, 0.0).astype(dtype)


VMEM = pl.BlockSpec(memory_space=pltpu.VMEM)
SMEM = pl.BlockSpec(memory_space=pltpu.SMEM)
HBM = pl.BlockSpec(memory_space=pltpu.HBM)


def call(body, outs, ins, scratch=(), spaces=None, out_hbm=()):
    ins = [
        pltpu.with_memory_space_constraint(v, pltpu.HBM) if (spaces or {}).get(i) is HBM else v
        for i, v in enumerate(ins)
    ]
    return pl.pallas_call(
        body,
        out_shape=[
            pltpu.HBM(s, d) if i in out_hbm else jax.ShapeDtypeStruct(s, d)
            for i, (s, d) in enumerate(outs)
        ],
        in_specs=[(spaces or {}).get(i, VMEM) for i in range(len(ins))],
        out_specs=[HBM if i in out_hbm else VMEM for i in range(len(outs))],
        scratch_shapes=list(scratch),
        compiler_params=pltpu.CompilerParams(vmem_limit_bytes=LIMIT),
    )(*ins)


def write_rows(scratch, tile_of, parts):
    count = scratch.shape[0] // parts
    for j in range(0, parts, 2):
        tile = tile_of(slice(128 * j, 128 * j + WIDE))
        scratch[pl.ds(j, count, stride=parts), :] = tile[:, 0:128]
        scratch[pl.ds(j + 1, count, stride=parts), :] = tile[:, 128:WIDE]


def write_message(message, scratch, tile_of, width):
    write_rows(scratch, tile_of, width // 128)
    owners = message.shape[0]
    per = scratch.shape[0] // owners
    message[:, 0:per, :] = scratch[...].reshape(owners, per, 128).astype(bf16)


def read_message(message, scratch, width):
    parts = width // 128
    count = scratch.shape[0] // parts
    owners = message.shape[0]
    per = scratch.shape[0] // owners
    scratch[...] = message[:, 0:per, :].astype(f32).reshape(scratch.shape)
    return [scratch[pl.ds(j, count, stride=parts), :] for j in range(parts)]


class Sender:
    def __init__(self, out, wide, narrow, sems, parts):
        self.out, self.wide, self.narrow, self.sems, self.parts = out, wide, narrow, sems, parts

    def copy(self, j):
        size = CH * self.parts
        span = pl.ds(pl.multiple_of(j * size, size), size)
        return pltpu.make_async_copy(self.narrow.at[span, :], self.out.at[span, :], self.sems.at[j])

    def put(self, j, value):
        size = CH * self.parts
        for p in range(self.parts):
            self.wide[pl.ds(p, CH, stride=self.parts), :] = value[:, 128 * p : 128 * (p + 1)]
        span = pl.ds(pl.multiple_of(j * size, size), size)
        self.narrow[span, :] = self.wide[...].astype(bf16)
        self.copy(j).start()

    def finish(self, blocks):
        for j in range(blocks):
            self.copy(j).wait()


def fetched(source, target, sem):
    copy = pltpu.make_async_copy(source, target, sem)
    copy.start()
    return copy


def rows_copy(source, target, sems, j):
    rows = pl.ds(pl.multiple_of(j * CH, CH), CH)
    return pltpu.make_async_copy(source.at[rows, :], target.at[rows, :], sems.at[j])


def parts_of(value, count):
    group = iota(value.shape, 1) >> 3
    out = jnp.zeros(value.shape, f32)
    for n in range(count):
        part = value.astype(bf16).astype(f32)
        out = jnp.where(group == n, part, out)
        value = value - part
    return out.astype(bf16)


def spread_all(count, width):
    q, c = iota((128, width), 0), iota((128, width), 1)
    return ones_where((q < 8 * count) & ((q & 7) == (c >> 6)))


def pack_events(
    owner_in, events_in, elapsed_in, resets_in, message, spots,
    scratch, place, owner, events, elapsed, resets, sems,
):
    copies = [
        pltpu.make_async_copy(source, target, sems.at[i])
        for i, (source, target) in enumerate(
            (
                (owner_in, owner),
                (elapsed_in, elapsed),
                (resets_in, resets),
                (events_in, events),
            )
        )
    ]
    for copy in copies:
        copy.start()
    copies[0].wait()
    rows, width = events.shape
    owners = message.shape[0]
    slots = place.shape[0]
    cap = slots // owners
    own = owner[...]
    hit = iota((owners, rows), 0) == own
    earlier = ones_where(iota((rows, rows), 0) < iota((rows, rows), 1))
    before = dot(ones_where(hit), earlier)
    rank = jnp.sum(jnp.where(hit, before, 0.0), axis=0, keepdims=True).astype(jnp.int32)
    spots[0:1, :] = own
    spots[1:2, :] = own * cap + rank
    place[...] = ones_where(iota((slots, rows), 0) == own * cap + rank)
    for copy in copies[1:]:
        copy.wait()
    write_message(
        message,
        scratch,
        lambda cols: dot(place[...], events[:, cols]),
        width,
    )
    lanes = iota((128, rows), 0)
    times = jnp.zeros((owners, 128), f32)
    for k, ref in enumerate((elapsed, resets)):
        value = ref[...]
        high = value.astype(bf16).astype(f32)
        for m, part in enumerate((high, value - high)):
            spot = ones_where(lanes == rank + cap * (2 * k + m))
            times += dot(jnp.where(hit, part, 0.0).astype(bf16), spot, NT)
    spread = ones_where(iota((owners * 8, owners), 0) == 8 * iota((owners * 8, owners), 1))
    extra = dot(spread, times.astype(bf16)).reshape(owners, 8, 128)
    per = scratch.shape[0] // owners
    message[:, per : per + 8, :] = extra.astype(bf16)


def pack_grads(info, spots, grads, message, back, expand, mine, scratch, narrow, turned, sems):
    rows, width = grads.shape
    slots = turned.shape[1]
    place = ones_where(iota((slots, rows), 0) == spots[1:2, :])
    write_rows(scratch, lambda cols: dot(place, grads[:, cols]), width // 128)
    narrow[...] = scratch[...].astype(bf16)
    copies = [fetched(narrow, message, sems.at[0])]
    same = ones_where(iota((rows, rows), 0) == iota((rows, rows), 1))
    turned[...] = dot(same, place, NT).astype(bf16)
    copies.append(fetched(turned, back, sems.at[1]))
    cap = slots * 8 // expand.shape[1]
    r, c = iota(expand.shape, 0), iota(expand.shape, 1)
    expand[...] = ones_where(((c & 7) == 0) & (8 * r >= cap * c) & (8 * r < cap * (c + 8)))
    row, lane = iota(mine.shape, 0).astype(f32), iota(mine.shape, 1).astype(f32)
    s = row - cap * jnp.floor((row + 0.5) * (1.0 / cap))
    hit = (lane == s) | (lane == s + cap) | (lane == s + 2 * cap) | (lane == s + 3 * cap)
    mine[...] = ones_where(hit)
    for copy in copies:
        copy.wait()


def unpack_rows(back, message, out, scratch):
    width = out.shape[1]
    parts = read_message(message, scratch, width)
    for j in range(0, len(parts), 2):
        both = jnp.concatenate([parts[j], parts[j + 1]], axis=1).astype(bf16)
        out[:, 128 * j : 128 * j + WIDE] = dot(back[...], both).astype(bf16)


def halves():
    low = ones_where(iota((CH, 128), 1) < 64)
    return low, ones_where(iota((CH, 128), 1) >= 64)


def block_mask():
    return (iota((128, 128), 0) < 64) == (iota((128, 128), 1) < 64)


def stacked(value, low, high):
    return jnp.concatenate([value * low, value * high], axis=0)


def decay_pair(fade, fade_t, rows, j, p):
    causal = iota((CH, CH), 0) >= iota((CH, CH), 1)
    both, wide = [], []
    turned = fade_t[j]
    here = fade[rows, :]
    for h in (2 * p, 2 * p + 1):
        column = jnp.broadcast_to(here[:, h : h + 1], (CH, CH))
        wide.append(column)
        spread = column - turned[h : h + 1, :]
        both.append(jnp.exp(jnp.where(causal, spread, -1e30)))
    return jnp.concatenate(both, axis=1), jnp.where(iota((CH, CH), 1) < 64, wide[0], wide[1])


def folded(full):
    return full[0:64, :] + full[64:128, :]


def unfolded(half, mask):
    return jnp.where(mask, jnp.concatenate([half, half], axis=0), 0.0)


def set_states(states, arrived):
    mask = block_mask()
    none = jnp.zeros((128, 128), f32)
    for n in range(states.shape[0]):
        first = jnp.concatenate([unfolded(arrived[2 * n], mask), none], axis=1)
        second = jnp.concatenate([none, unfolded(arrived[2 * n + 1], mask)], axis=1)
        states[n] = jnp.concatenate([first, second], axis=0).astype(bf16)


def set_memory(memory, both, n):
    mask = block_mask()
    memory[2 * n] = jnp.where(mask, both[0:128, 0:128], 0.0)
    memory[2 * n + 1] = jnp.where(mask, both[128:WIDE, 128:WIDE], 0.0)


def write_state(send, state, last, pairs):
    for p in range(pairs):
        send[64 * p : 64 * (p + 1), :] = folded(state[p]).astype(bf16)
    write_marks(send, last, pairs)


def write_marks(send, last, pairs):
    last = jnp.broadcast_to(last, (8, 128))
    high = last.astype(bf16).astype(f32)
    lane = iota(last.shape, 1)
    send[64 * pairs : 64 * pairs + 8, :] = jnp.where(lane < 64, high, last - high).astype(bf16)


def read_marks(ref, pairs):
    marks = ref[64 * pairs : 64 * pairs + 8, :].astype(f32)
    return marks[:, 0:1] + marks[:, 64:65]


def lane_factors(log, p):
    return jnp.exp(
        jnp.where(
            iota((1, 128), 1) < 64,
            jnp.broadcast_to(log[2 * p : 2 * p + 1, :], (1, 128)),
            jnp.broadcast_to(log[2 * p + 1 : 2 * p + 2, :], (1, 128)),
        )
    )


def join_pair(near, far, out, pairs):
    log = read_marks(near, pairs)
    for p in range(pairs):
        rows = slice(64 * p, 64 * (p + 1))
        joined = near[rows, :].astype(f32) + lane_factors(log, p) * far[rows, :].astype(f32)
        out[rows, :] = joined.astype(bf16)
    write_marks(out, log + read_marks(far, pairs), pairs)


def join_ahead(info, own, other, out):
    join(info[1] == 1, own, other, out)


def join_back(info, own, other, out):
    join(info[1] == 0, own, other, out)


def join(own_is_near, own, other, out):
    pairs = own.shape[0] // 64

    @pl.when(own_is_near)
    def _():
        join_pair(own, other, out, pairs)

    @pl.when(jnp.logical_not(own_is_near))
    def _():
        join_pair(other, own, out, pairs)


def gathered_state(partner_counts, partner, received, pairs):
    log = read_marks(partner, pairs) * partner_counts
    total = [partner[64 * p : 64 * (p + 1), :].astype(f32) * partner_counts for p in range(pairs)]
    for ref in received:
        for p in range(pairs):
            total[p] += lane_factors(log, p) * ref[64 * p : 64 * (p + 1), :].astype(f32)
        log = log + read_marks(ref, pairs)
    return total


def forward_state(
    info, rates, message, weights, expand, own_lanes,
    x_out, keys, values, keys_out, values_out, fade, fade_t, marks, fall, send,
    scratch, memory, mine, x, sems,
):
    fetch = fetched(weights.at[info[0], pl.ds(1, 2)], mine, sems.at[1])
    slots, width = x.shape
    pairs = width // 128
    blocks = slots // CH
    owners = message.shape[0]
    cap = slots // owners
    per = cap * pairs
    for j, part in enumerate(read_message(message, scratch, width)):
        x[:, 128 * j : 128 * (j + 1)] = part.astype(bf16)
    stores = [fetched(x, x_out, sems.at[2])]
    times = message[:, per : per + 8, :].astype(f32).reshape(owners * 8, 128).astype(bf16)
    own = dot(expand[...], times).astype(bf16) * own_lanes[...]
    kind, head = iota((128, 128), 0), iota((128, 128), 1) & 7
    rate = jnp.zeros((128, 128), f32)
    for h in range(rates.shape[1]):
        rate = jnp.where(head == h, rates[info[0], h], rate)
    to_heads = jnp.where(kind < 2 * cap, -rate, jnp.where(kind < 4 * cap, -1.0, 0.0))
    tri = ones_where(iota((CH, CH), 0) >= iota((CH, CH), 1))
    before = jnp.zeros((1, 128), f32)
    start = jnp.zeros((1, 128), f32)
    ends = []
    for j in range(blocks):
        running = dot(tri, own[CH * j : CH * (j + 1), :]) + before
        before = running[CH - 1 : CH, :]
        here = dot(running, to_heads, NN, EXACT)
        fade[CH * j : CH * (j + 1), :] = here
        fade_t[j] = here.T[0:8, :]
        start = here[CH - 1 : CH, :]
        ends.append(start)
    ends = jnp.concatenate(ends + [jnp.zeros((8 - blocks, 128), f32)], axis=0)
    wide_ends = dot(parts_of(ends, 3), spread_all(3, width))
    for j in range(blocks):
        for p in range(pairs):
            cols = slice(128 * p, 128 * (p + 1))
            marks[j, pairs + p : pairs + p + 1, :] = wide_ends[j : j + 1, cols]
            if j == 0:
                marks[j, p : p + 1, :] = jnp.zeros((1, 128), f32)
            else:
                marks[j, p : p + 1, :] = wide_ends[j - 1 : j, cols]
    fall[...] = parts_of(jnp.exp(start - fade[...]), 2)
    fetch.wait()
    for n in range(0, width, WIDE):
        cols = slice(n, n + WIDE)
        keys[:, cols] = dot(x[...], mine[0, :, cols]).astype(bf16)
        values[:, cols] = dot(x[...], mine[1, :, cols]).astype(bf16)
    hot = spread_all(2, width)
    for n in range(pairs // 2):
        cols = slice(WIDE * n, WIDE * (n + 1))
        kf = (keys[:, cols].astype(f32) * dot(fall[...], hot[:, cols])).astype(bf16)
        set_memory(memory, dot(kf, values[:, cols], TN), n)
    stores.append(fetched(keys, keys_out, sems.at[3]))
    stores.append(fetched(values, values_out, sems.at[4]))
    write_state(send, memory, fade_t[blocks - 1][:, CH - 1 : CH], pairs)
    for store in stores:
        store.wait()


def attend(
    info, x_in, weights, keys, values, fade, fade_t, marks,
    q8, attended_out, states, lift,
    memory, attended, x, mine, in_sems, sems,
):
    arrival = fetched(x_in, x, in_sems.at[0])
    fetch = fetched(weights.at[info[0], 0], mine, in_sems.at[1])
    lift[...] = parts_of(jnp.exp(fade[...]), 2)
    arrival.wait()
    fetch.wait()
    for n in range(0, x.shape[1], WIDE):
        cols = slice(n, n + WIDE)
        query = dot(x[...], mine[:, cols]).astype(bf16).astype(f32)
        q8[:, cols] = (query * 0.125).astype(bf16)
    slots, width = q8.shape
    pairs = width // 128
    low, high = halves()
    mask = block_mask()
    memory[...] = jnp.zeros(memory.shape, f32)

    def block(j, carry):
        rows = pl.ds(pl.multiple_of(j * CH, CH), CH)
        edge = marks[j]
        for p in range(pairs):
            cols = slice(128 * p, 128 * (p + 1))
            start, end = edge[p : p + 1, :], edge[pairs + p : pairs + p + 1, :]
            qp, kp, vp = q8[rows, cols], keys[rows, cols], values[rows, cols]
            scores = dot(qp, stacked(kp, low, high), NT)
            fading, g = decay_pair(fade, fade_t, rows, j, p)
            mix = (scores * fading).astype(bf16)
            within = dot(mix, stacked(vp, low, high))
            now = memory[p]
            states[j, p] = folded(now).astype(bf16)
            lifted = (qp.astype(f32) * jnp.exp(g - start)).astype(bf16)
            attended[rows, cols] = within + dot(lifted, now.astype(bf16))
            kf = (kp.astype(f32) * jnp.exp(end - g)).astype(bf16)
            memory[p] = jnp.exp(end - start) * now + jnp.where(mask, dot(kf, vp, TN), 0.0)
        rows_copy(attended, attended_out, sems, j).start()
        return carry

    lax.fori_loop(0, slots // CH, block, 0, unroll=True)
    for j in range(slots // CH):
        rows_copy(attended, attended_out, sems, j).wait()


def encode(info, q8, lift, attended_in, x_in, weights, partner, *rest):
    received = rest[:-12]
    (
        encoded, full_out, incoming,
        mine, x, attended, normed, wide, narrow, states, sems, full_sems,
    ) = rest[-12:]
    attended_here = fetched(attended_in, attended, sems.at[0])
    fetch = fetched(weights.at[info[0], 3], mine, sems.at[1])
    rows_in = fetched(x_in, x, sems.at[2])
    slots, width = x.shape
    pairs = width // 128
    blocks = slots // CH
    arrived = gathered_state(info[1].astype(f32), partner, received, pairs)
    for p in range(pairs):
        incoming[p] = arrived[p]
    set_states(states, arrived)
    hot = spread_all(2, width)
    attended_here.wait()

    def block(j, carry):
        rows = pl.ds(pl.multiple_of(j * CH, CH), CH)
        factors = dot(lift[rows, :], hot)
        values = []
        square = jnp.zeros((CH, 1), f32)
        for n in range(pairs // 2):
            cols = slice(WIDE * n, WIDE * (n + 1))
            lifted = (q8[rows, cols].astype(f32) * factors[:, cols]).astype(bf16)
            value = attended[rows, cols] + dot(lifted, states[n])
            attended[rows, cols] = value
            values.append(value)
            square += jnp.sum(value * value, axis=1, keepdims=True)
        scale = lax.rsqrt(square * (1.0 / width) + 1e-06)
        normed[rows, :] = (jnp.concatenate(values, axis=1) * scale).astype(bf16)
        rows_copy(attended, full_out, full_sems, j).start()
        return carry

    lax.fori_loop(0, blocks, block, 0, unroll=True)
    rows_in.wait()
    fetch.wait()
    halves_out = [
        x[:, n : n + WIDE].astype(f32) + dot(normed[...], mine[:, n : n + WIDE])
        for n in range(0, width, WIDE)
    ]
    for n, half in enumerate(halves_out):
        wide[pl.ds(2 * n, slots, stride=pairs), :] = half[:, 0:128]
        wide[pl.ds(2 * n + 1, slots, stride=pairs), :] = half[:, 128:WIDE]
    narrow[...] = wide[...].astype(bf16)
    out = fetched(narrow, encoded, sems.at[3])
    for j in range(blocks):
        rows_copy(attended, full_out, full_sems, j).wait()
    out.wait()


def turn(
    info, q8, lift, fade_t, full_in, weights, message,
    grads_out, grad_full, send,
    scratch, mine, full, grads, grad_normed, lifts, memory, sems,
):
    full_here = fetched(full_in, full, sems.at[0])
    fetch = fetched(weights.at[info[0], 3], mine, sems.at[1])
    slots, width = full.shape
    pairs = width // 128
    blocks = slots // CH
    for j, part in enumerate(read_message(message, scratch, width)):
        grads[:, 128 * j : 128 * (j + 1)] = part.astype(bf16)
    store = fetched(grads, grads_out, sems.at[2])
    fetch.wait()
    for n in range(0, width, WIDE):
        cols = slice(n, n + WIDE)
        grad_normed[:, cols] = dot(grads[...], mine[cols, :], NT).astype(bf16)
    hot = spread_all(2, width)
    for n in range(0, width, WIDE):
        cols = slice(n, n + WIDE)
        factors = dot(lift[...], hot[:, cols])
        lifts[:, cols] = (q8[:, cols].astype(f32) * factors).astype(bf16)
    full_here.wait()

    def block(j, carry):
        rows = pl.ds(pl.multiple_of(j * CH, CH), CH)
        here = full[rows, :]
        scale = lax.rsqrt(jnp.mean(here * here, axis=1, keepdims=True) + 1e-06)
        grad = grad_normed[rows, :].astype(f32)
        along = jnp.mean(here * grad, axis=1, keepdims=True)
        grad_full[rows, :] = (scale * grad - here * (scale * scale * scale * along)).astype(bf16)
        return carry

    lax.fori_loop(0, blocks, block, 0, unroll=True)
    for n in range(pairs // 2):
        cols = slice(WIDE * n, WIDE * (n + 1))
        set_memory(memory, dot(lifts[:, cols], grad_full[:, cols], TN), n)
    write_state(send, memory, fade_t[blocks - 1][:, CH - 1 : CH], pairs)
    store.wait()


def backward_local(
    q8, keys_in, values_in, fade, fade_t, marks, grad_full, states, incoming,
    grad_q, grad_keys, grad_values,
    memory, keys, values, key_sems, value_sems,
):
    for j in reversed(range(q8.shape[0] // CH)):
        rows_copy(keys_in, keys, key_sems, j).start()
        rows_copy(values_in, values, value_sems, j).start()
    slots, width = q8.shape
    pairs = width // 128
    blocks = slots // CH
    low, high = halves()
    lower = iota((CH, 128), 1) < 64
    mask = block_mask()
    memory[...] = jnp.zeros(memory.shape, f32)

    def block(i, carry):
        j = blocks - 1 - i
        rows_copy(keys_in, keys, key_sems, j).wait()
        rows_copy(values_in, values, value_sems, j).wait()
        rows = pl.ds(pl.multiple_of(j * CH, CH), CH)
        edge = marks[j]
        for p in range(pairs):
            cols = slice(128 * p, 128 * (p + 1))
            start, end = edge[p : p + 1, :], edge[pairs + p : pairs + p + 1, :]
            qp, kp, vp = q8[rows, cols], keys[rows, cols], values[rows, cols]
            da = grad_full[rows, cols]
            ks, vs = stacked(kp, low, high), stacked(vp, low, high)
            fading, g = decay_pair(fade, fade_t, rows, j, p)
            mix = (dot(qp, ks, NT) * fading).astype(bf16)
            grad_scores = (dot(da, vs, NT) * fading).astype(bf16)
            lift = jnp.exp(g - start)
            fall = jnp.exp(end - g)
            state = states[j, p].astype(f32) + jnp.exp(start) * incoming[p]
            state = unfolded(state, mask).astype(bf16)
            grad_q[rows, cols] = (
                0.125 * (dot(grad_scores, ks) + lift * dot(da, state, NT))
            ).astype(bf16)
            gk = dot(grad_scores, qp, TN)
            gv = dot(mix, da, TN)
            now = memory[p]
            narrow = now.astype(bf16)
            kf = (kp.astype(f32) * fall).astype(bf16)
            grad_keys[rows, cols] = jnp.where(lower, gk[0:CH], gk[CH:]) + fall * dot(vp, narrow, NT)
            grad_values[rows, cols] = jnp.where(lower, gv[0:CH], gv[CH:]) + dot(kf, narrow)
            lifted = (qp.astype(f32) * lift).astype(bf16)
            memory[p] = jnp.exp(end - start) * now + jnp.where(mask, dot(lifted, da, TN), 0.0)
        return carry

    lax.fori_loop(0, blocks, block, 0, unroll=True)


def project_back(info, grads_in, grad_q, weights, partial, mine, grads, sems):
    arrival = fetched(grads_in, grads, sems.at[0])
    fetch = fetched(weights.at[info[0], 0], mine, sems.at[1])
    fetch.wait()
    arrival.wait()
    for n in range(0, grads.shape[1], WIDE):
        cols = slice(n, n + WIDE)
        partial[:, cols] = grads[:, cols].astype(f32) + dot(grad_q[...], mine[cols, :], NT)


def backward_finish(
    info, partial, grad_keys, grad_values, keys_in, values_in, fall, weights, partner, *rest
):
    received = rest[:-12]
    out, mine, wide, narrow, states, gk, gv, total, keys, values, sems, out_sems = rest[-12:]
    keys_here = fetched(keys_in, keys, sems.at[1])
    values_here = fetched(values_in, values, sems.at[2])
    fetch = fetched(weights.at[info[0], pl.ds(1, 2)], mine, sems.at[0])
    slots, width = partial.shape
    pairs = width // 128
    blocks = slots // CH
    set_states(states, gathered_state((1 - info[1]).astype(f32), partner, received, pairs))
    hot = spread_all(2, width)
    keys_here.wait()
    values_here.wait()
    for n in range(pairs // 2):
        cols = slice(WIDE * n, WIDE * (n + 1))
        factor = dot(fall[...], hot[:, cols])
        kf = (keys[:, cols].astype(f32) * factor).astype(bf16)
        gk[:, cols] = (grad_keys[:, cols] + factor * dot(values[:, cols], states[n], NT)).astype(bf16)
        gv[:, cols] = (grad_values[:, cols] + dot(kf, states[n])).astype(bf16)
    fetch.wait()
    for n in range(0, width, WIDE):
        cols = slice(n, n + WIDE)
        total[:, cols] = (
            partial[:, cols] + dot(gk[...], mine[0, cols, :], NT) + dot(gv[...], mine[1, cols, :], NT)
        )
    sender = Sender(out, wide, narrow, out_sems, pairs)

    def put(j, carry):
        sender.put(j, total[pl.ds(pl.multiple_of(j * CH, CH), CH), :])
        return carry

    lax.fori_loop(0, blocks, put, 0)
    sender.finish(blocks)


def swapped(value, axis):
    return lax.ppermute(value, axis, [(i, i ^ 1) for i in range(lax.axis_size(axis))])


def exchange(value, axis, sign):
    count = lax.axis_size(axis)
    return [
        lax.ppermute(
            value, axis, [(i, i + sign * k) for i in range(count) if 0 <= i + sign * k < count]
        )
        for k in range(2, count, 2)
    ]


def regroup(value):
    return lax.all_to_all(value, "log", split_axis=0, concat_axis=0, tiled=True)


def shards(events, owner_ids, elapsed, resets, decay_rates, weights, cotangent):
    rows, width = events.shape[2:]
    owners = lax.axis_size("log")
    cap = 5 * rows // (4 * owners)
    slots = owners * cap
    pairs = width // 128
    blocks = slots // CH
    per = cap * pairs
    flat = pltpu.VMEM((slots * pairs, 128), f32)
    state_vmem = pltpu.VMEM((pairs, 128, 128), f32)
    state_msg = ((64 * pairs + 8, 128), bf16)
    wide16, wide32 = ((slots, width), bf16), ((slots, width), f32)

    tower = lax.axis_index("log") // (owners // decay_rates.shape[0])
    info = jnp.stack([tower, lax.axis_index("ctx") % 2]).astype(jnp.int32)
    sem = pltpu.SemaphoreType.DMA

    message, spots = call(
        pack_events,
        [((owners, per + 8, 128), bf16), ((2, rows), jnp.int32)],
        [
            owner_ids.reshape(1, rows),
            events.reshape(rows, width),
            elapsed.reshape(1, rows),
            resets.reshape(1, rows),
        ],
        [
            flat,
            pltpu.VMEM((slots, rows), bf16),
            pltpu.VMEM((1, rows), jnp.int32),
            pltpu.VMEM((rows, width), bf16),
            pltpu.VMEM((1, rows), f32),
            pltpu.VMEM((1, rows), f32),
            pltpu.SemaphoreType.DMA((4,)),
        ],
        {0: HBM, 1: HBM, 2: HBM, 3: HBM},
    )
    events_in = regroup(message)
    flat_msg = ((slots * pairs, 128), bf16)
    message, back, expand, own_lanes = call(
        pack_grads,
        [
            flat_msg, ((rows, slots), bf16), ((slots, owners * 8), bf16), ((slots, 128), bf16),
        ],
        [info, spots, cotangent.reshape(rows, width)],
        [flat, pltpu.VMEM(*flat_msg), pltpu.VMEM((rows, slots), bf16), sem((2,))],
        {0: SMEM},
        (0, 1),
    )
    grads_in = regroup(message.reshape(owners, per, 128))
    one = pltpu.VMEM((width, width), bf16)
    two = pltpu.VMEM((2, width, width), bf16)
    half_states = ((pairs, 64, 128), f32)
    block_wide = pltpu.VMEM((CH * pairs, 128), f32)
    flat_narrow = pltpu.VMEM(*flat_msg)
    rows16, rows32 = pltpu.VMEM(*wide16), pltpu.VMEM(*wide32)
    narrow_states = pltpu.VMEM((pairs // 2, WIDE, WIDE), bf16)
    x, keys, values, keys_far, values_far, fade, fade_t, marks, fall, send = call(
        forward_state,
        [
            wide16, wide16, wide16, wide16, wide16, ((slots, 128), f32), ((blocks, 8, 128), f32),
            ((blocks, 2 * pairs, 128), f32), ((slots, 128), bf16), state_msg,
        ],
        [info, decay_rates, events_in, weights, expand, own_lanes],
        [flat, state_vmem, two, rows16, sem((5,))],
        {0: SMEM, 1: SMEM, 3: HBM},
        (0, 3, 4),
    )
    partner = swapped(send, "ctx")
    (joined,) = call(join_ahead, [state_msg], [info, send, partner], (), {0: SMEM})
    received = exchange(joined, "ctx", 1)
    q8, attended, kept, lift = call(
        attend,
        [wide16, wide32, ((blocks, pairs, 64, 128), bf16), ((slots, 128), bf16)],
        [info, x, weights, keys, values, fade, fade_t, marks],
        [state_vmem, rows32, rows16, one, sem((2,)), sem((blocks,))],
        {0: SMEM, 1: HBM, 2: HBM},
        (1,),
    )
    message, full, incoming = call(
        encode,
        [flat_msg, wide32, half_states],
        [info, q8, lift, attended, x, weights, partner, *received],
        [
            one, rows16, rows32, rows16, flat, flat_narrow, narrow_states, sem((4,)),
            sem((blocks,)),
        ],
        {0: SMEM, 3: HBM, 4: HBM, 5: HBM},
        (0, 1),
    )
    encoded_in = regroup(message.reshape(owners, per, 128))
    grads, grad_full, send = call(
        turn,
        [wide16, wide16, state_msg],
        [info, q8, lift, fade_t, full, weights, grads_in],
        [flat, one, rows32, rows16, rows16, rows16, state_vmem, sem((3,))],
        {0: SMEM, 4: HBM, 5: HBM},
        (0,),
    )
    partner = swapped(send, "ctx")
    grad_q, grad_keys, grad_values = call(
        backward_local,
        [wide16, wide32, wide32],
        [q8, keys_far, values_far, fade, fade_t, marks, grad_full, kept, incoming],
        [state_vmem, rows16, rows16, sem((blocks,)), sem((blocks,))],
        {1: HBM, 2: HBM},
    )
    (joined,) = call(join_back, [state_msg], [info, send, partner], (), {0: SMEM})
    received = exchange(joined, "ctx", -1)
    (partial,) = call(
        project_back,
        [wide32],
        [info, grads, grad_q, weights],
        [one, rows16, sem((2,))],
        {0: SMEM, 1: HBM, 3: HBM},
    )
    (message,) = call(
        backward_finish,
        [flat_msg],
        [
            info, partial, grad_keys, grad_values, keys_far, values_far, fall, weights, partner,
            *received,
        ],
        [
            two, block_wide, flat_narrow, narrow_states,
            rows16, rows16, rows32, rows16, rows16, sem((3,)), sem((blocks,)),
        ],
        {0: SMEM, 4: HBM, 5: HBM, 7: HBM},
        (0,),
    )
    grad_in = regroup(message.reshape(owners, per, 128))
    (encoded,) = call(unpack_rows, [((rows, width), bf16)], [back, encoded_in], [flat])
    (grad,) = call(unpack_rows, [((rows, width), bf16)], [back, grad_in], [flat])
    return encoded.reshape(events.shape), grad.reshape(events.shape)


def solution(mesh):
    wide = P("ctx", "log", None, None)
    flat = P("ctx", "log", None)
    return jax.shard_map(
        shards,
        mesh=mesh,
        in_specs=(wide, wide, flat, flat, P(), P(), wide),
        out_specs=(wide, wide),
        check_vma=False,
    )
```

```python
import jax
import jax.numpy as jnp
from jax import lax
from jax.experimental import pallas as pl
from jax.experimental.pallas import tpu as pltpu
from jax.sharding import PartitionSpec as P


bf16 = jnp.bfloat16
f32 = jnp.float32
CH = 128
NN = (((1,), (0,)), ((), ()))
NT = (((1,), (1,)), ((), ()))
TN = (((0,), (0,)), ((), ()))
EXACT = lax.Precision.HIGHEST
LIMIT = 16 << 20
WIDE = 256


def dot(a, b, dims=NN, precision=None):
    return lax.dot_general(a, b, dims, preferred_element_type=f32, precision=precision)


def iota(shape, dim):
    return lax.broadcasted_iota(jnp.int32, shape, dim)


def ones_where(cond, dtype=bf16):
    return jnp.where(cond, 1.0, 0.0).astype(dtype)


VMEM = pl.BlockSpec(memory_space=pltpu.VMEM)
SMEM = pl.BlockSpec(memory_space=pltpu.SMEM)
HBM = pl.BlockSpec(memory_space=pltpu.HBM)


def call(body, outs, ins, scratch=(), spaces=None, out_hbm=()):
    ins = [
        pltpu.with_memory_space_constraint(v, pltpu.HBM) if (spaces or {}).get(i) is HBM else v
        for i, v in enumerate(ins)
    ]
    return pl.pallas_call(
        body,
        out_shape=[
            pltpu.HBM(s, d) if i in out_hbm else jax.ShapeDtypeStruct(s, d)
            for i, (s, d) in enumerate(outs)
        ],
        in_specs=[(spaces or {}).get(i, VMEM) for i in range(len(ins))],
        out_specs=[HBM if i in out_hbm else VMEM for i in range(len(outs))],
        scratch_shapes=list(scratch),
        compiler_params=pltpu.CompilerParams(vmem_limit_bytes=LIMIT),
    )(*ins)


def write_rows(scratch, tile_of, parts):
    count = scratch.shape[0] // parts
    for j in range(0, parts, 2):
        tile = tile_of(slice(128 * j, 128 * j + WIDE))
        scratch[pl.ds(j, count, stride=parts), :] = tile[:, 0:128]
        scratch[pl.ds(j + 1, count, stride=parts), :] = tile[:, 128:WIDE]


def write_message(message, scratch, tile_of, width):
    write_rows(scratch, tile_of, width // 128)
    owners = message.shape[0]
    per = scratch.shape[0] // owners
    message[:, 0:per, :] = scratch[...].reshape(owners, per, 128).astype(bf16)


def read_message(message, scratch, width):
    parts = width // 128
    count = scratch.shape[0] // parts
    owners = message.shape[0]
    per = scratch.shape[0] // owners
    scratch[...] = message[:, 0:per, :].astype(f32).reshape(scratch.shape)
    return [scratch[pl.ds(j, count, stride=parts), :] for j in range(parts)]


class Sender:
    def __init__(self, out, wide, narrow, sems, parts):
        self.out, self.wide, self.narrow, self.sems, self.parts = out, wide, narrow, sems, parts

    def copy(self, j):
        size = CH * self.parts
        span = pl.ds(pl.multiple_of(j * size, size), size)
        return pltpu.make_async_copy(self.narrow.at[span, :], self.out.at[span, :], self.sems.at[j])

    def put(self, j, value):
        size = CH * self.parts
        for p in range(self.parts):
            self.wide[pl.ds(p, CH, stride=self.parts), :] = value[:, 128 * p : 128 * (p + 1)]
        span = pl.ds(pl.multiple_of(j * size, size), size)
        self.narrow[span, :] = self.wide[...].astype(bf16)
        self.copy(j).start()

    def finish(self, blocks):
        for j in range(blocks):
            self.copy(j).wait()


def fetched(source, target, sem):
    copy = pltpu.make_async_copy(source, target, sem)
    copy.start()
    return copy


def rows_copy(source, target, sems, j):
    rows = pl.ds(pl.multiple_of(j * CH, CH), CH)
    return pltpu.make_async_copy(source.at[rows, :], target.at[rows, :], sems.at[j])


def parts_of(value, count):
    group = iota(value.shape, 1) >> 3
    out = jnp.zeros(value.shape, f32)
    for n in range(count):
        part = value.astype(bf16).astype(f32)
        out = jnp.where(group == n, part, out)
        value = value - part
    return out.astype(bf16)


def spread_all(count, width):
    q, c = iota((128, width), 0), iota((128, width), 1)
    return ones_where((q < 8 * count) & ((q & 7) == (c >> 6)))


def pack_events(
    owner_in, events_in, elapsed_in, resets_in, message, spots,
    scratch, place, earlier, owner, events, elapsed, resets, sems,
):
    copies = [
        pltpu.make_async_copy(source, target, sems.at[i])
        for i, (source, target) in enumerate(
            (
                (owner_in, owner),
                (elapsed_in, elapsed),
                (resets_in, resets),
                (events_in, events),
            )
        )
    ]
    for copy in copies:
        copy.start()
    rows, width = events.shape
    earlier[...] = ones_where(iota((rows, rows), 0) < iota((rows, rows), 1))
    copies[0].wait()
    owners = message.shape[0]
    slots = place.shape[0]
    cap = slots // owners
    own = owner[...]
    hit = iota((owners, rows), 0) == own
    before = dot(ones_where(hit), earlier[...])
    rank = jnp.sum(jnp.where(hit, before, 0.0), axis=0, keepdims=True).astype(jnp.int32)
    spots[0:1, :] = own
    spots[1:2, :] = own * cap + rank
    place[...] = ones_where(iota((slots, rows), 0) == own * cap + rank)
    for copy in copies[1:]:
        copy.wait()
    write_message(
        message,
        scratch,
        lambda cols: dot(place[...], events[:, cols]),
        width,
    )
    lanes = iota((128, rows), 0)
    times = jnp.zeros((owners, 128), f32)
    for k, ref in enumerate((elapsed, resets)):
        value = ref[...]
        high = value.astype(bf16).astype(f32)
        for m, part in enumerate((high, value - high)):
            spot = ones_where(lanes == rank + cap * (2 * k + m))
            times += dot(jnp.where(hit, part, 0.0).astype(bf16), spot, NT)
    spread = ones_where(iota((owners * 8, owners), 0) == 8 * iota((owners * 8, owners), 1))
    extra = dot(spread, times.astype(bf16)).reshape(owners, 8, 128)
    per = scratch.shape[0] // owners
    message[:, per : per + 8, :] = extra.astype(bf16)


def pack_grads(info, spots, grads, message, back, expand, mine, scratch, narrow, turned, sems):
    rows, width = grads.shape
    slots = turned.shape[1]
    place = ones_where(iota((slots, rows), 0) == spots[1:2, :])
    write_rows(scratch, lambda cols: dot(place, grads[:, cols]), width // 128)
    narrow[...] = scratch[...].astype(bf16)
    copies = [fetched(narrow, message, sems.at[0])]
    same = ones_where(iota((rows, rows), 0) == iota((rows, rows), 1))
    turned[...] = dot(same, place, NT).astype(bf16)
    copies.append(fetched(turned, back, sems.at[1]))
    cap = slots * 8 // expand.shape[1]
    r, c = iota(expand.shape, 0), iota(expand.shape, 1)
    expand[...] = ones_where(((c & 7) == 0) & (8 * r >= cap * c) & (8 * r < cap * (c + 8)))
    row, lane = iota(mine.shape, 0).astype(f32), iota(mine.shape, 1).astype(f32)
    s = row - cap * jnp.floor((row + 0.5) * (1.0 / cap))
    hit = (lane == s) | (lane == s + cap) | (lane == s + 2 * cap) | (lane == s + 3 * cap)
    mine[...] = ones_where(hit)
    for copy in copies:
        copy.wait()


def unpack_rows(back, message, out, scratch):
    width = out.shape[1]
    parts = read_message(message, scratch, width)
    for j in range(0, len(parts), 2):
        both = jnp.concatenate([parts[j], parts[j + 1]], axis=1).astype(bf16)
        out[:, 128 * j : 128 * j + WIDE] = dot(back[...], both).astype(bf16)


def halves():
    low = ones_where(iota((CH, 128), 1) < 64)
    return low, ones_where(iota((CH, 128), 1) >= 64)


def block_mask():
    return (iota((128, 128), 0) < 64) == (iota((128, 128), 1) < 64)


def stacked(value, low, high):
    return jnp.concatenate([value * low, value * high], axis=0)


def decay_pair(fade, fade_t, rows, j, p):
    causal = iota((CH, CH), 0) >= iota((CH, CH), 1)
    both, wide = [], []
    turned = fade_t[j]
    here = fade[rows, :]
    for h in (2 * p, 2 * p + 1):
        column = jnp.broadcast_to(here[:, h : h + 1], (CH, CH))
        wide.append(column)
        spread = column - turned[h : h + 1, :]
        both.append(jnp.exp(jnp.where(causal, spread, -1e30)))
    return jnp.concatenate(both, axis=1), jnp.where(iota((CH, CH), 1) < 64, wide[0], wide[1])


def folded(full):
    return full[0:64, :] + full[64:128, :]


def unfolded(half, mask):
    return jnp.where(mask, jnp.concatenate([half, half], axis=0), 0.0)


def set_states(states, arrived):
    mask = block_mask()
    none = jnp.zeros((128, 128), f32)
    for n in range(states.shape[0]):
        first = jnp.concatenate([unfolded(arrived[2 * n], mask), none], axis=1)
        second = jnp.concatenate([none, unfolded(arrived[2 * n + 1], mask)], axis=1)
        states[n] = jnp.concatenate([first, second], axis=0).astype(bf16)


def set_memory(memory, both, n):
    mask = block_mask()
    memory[2 * n] = jnp.where(mask, both[0:128, 0:128], 0.0)
    memory[2 * n + 1] = jnp.where(mask, both[128:WIDE, 128:WIDE], 0.0)


def write_state(send, state, last, pairs):
    for p in range(pairs):
        send[64 * p : 64 * (p + 1), :] = folded(state[p]).astype(bf16)
    write_marks(send, last, pairs)


def write_marks(send, last, pairs):
    last = jnp.broadcast_to(last, (8, 128))
    high = last.astype(bf16).astype(f32)
    lane = iota(last.shape, 1)
    send[64 * pairs : 64 * pairs + 8, :] = jnp.where(lane < 64, high, last - high).astype(bf16)


def read_marks(ref, pairs):
    marks = ref[64 * pairs : 64 * pairs + 8, :].astype(f32)
    return marks[:, 0:1] + marks[:, 64:65]


def lane_factors(log, p):
    return jnp.exp(
        jnp.where(
            iota((1, 128), 1) < 64,
            jnp.broadcast_to(log[2 * p : 2 * p + 1, :], (1, 128)),
            jnp.broadcast_to(log[2 * p + 1 : 2 * p + 2, :], (1, 128)),
        )
    )


def join_pair(near, far, out, pairs):
    log = read_marks(near, pairs)
    for p in range(pairs):
        rows = slice(64 * p, 64 * (p + 1))
        joined = near[rows, :].astype(f32) + lane_factors(log, p) * far[rows, :].astype(f32)
        out[rows, :] = joined.astype(bf16)
    write_marks(out, log + read_marks(far, pairs), pairs)


def join_ahead(info, own, other, out):
    join(info[1] == 1, own, other, out)


def join_back(info, own, other, out):
    join(info[1] == 0, own, other, out)


def join(own_is_near, own, other, out):
    pairs = own.shape[0] // 64

    @pl.when(own_is_near)
    def _():
        join_pair(own, other, out, pairs)

    @pl.when(jnp.logical_not(own_is_near))
    def _():
        join_pair(other, own, out, pairs)


def gathered_state(partner_counts, partner, received, pairs):
    log = read_marks(partner, pairs) * partner_counts
    total = [partner[64 * p : 64 * (p + 1), :].astype(f32) * partner_counts for p in range(pairs)]
    for ref in received:
        for p in range(pairs):
            total[p] += lane_factors(log, p) * ref[64 * p : 64 * (p + 1), :].astype(f32)
        log = log + read_marks(ref, pairs)
    return total


def forward_state(
    info, rates, message, weights, expand, own_lanes,
    x_out, keys, values, keys_out, values_out, fade, fade_t, marks, fall, send, x,
    scratch, memory, mine, sems,
):
    fetch = fetched(weights.at[info[0], pl.ds(1, 2)], mine, sems.at[1])
    slots, width = x.shape
    pairs = width // 128
    blocks = slots // CH
    owners = message.shape[0]
    cap = slots // owners
    per = cap * pairs
    for j, part in enumerate(read_message(message, scratch, width)):
        x[:, 128 * j : 128 * (j + 1)] = part.astype(bf16)
    stores = [fetched(x, x_out, sems.at[2])]
    times = message[:, per : per + 8, :].astype(f32).reshape(owners * 8, 128).astype(bf16)
    own = dot(expand[...], times).astype(bf16) * own_lanes[...]
    kind, head = iota((128, 128), 0), iota((128, 128), 1) & 7
    rate = jnp.zeros((128, 128), f32)
    for h in range(rates.shape[1]):
        rate = jnp.where(head == h, rates[info[0], h], rate)
    to_heads = jnp.where(kind < 2 * cap, -rate, jnp.where(kind < 4 * cap, -1.0, 0.0))
    tri = ones_where(iota((CH, CH), 0) >= iota((CH, CH), 1))
    before = jnp.zeros((1, 128), f32)
    start = jnp.zeros((1, 128), f32)
    ends = []
    for j in range(blocks):
        running = dot(tri, own[CH * j : CH * (j + 1), :]) + before
        before = running[CH - 1 : CH, :]
        here = dot(running, to_heads, NN, EXACT)
        fade[CH * j : CH * (j + 1), :] = here
        fade_t[j] = here.T[0:8, :]
        start = here[CH - 1 : CH, :]
        ends.append(start)
    ends = jnp.concatenate(ends + [jnp.zeros((8 - blocks, 128), f32)], axis=0)
    wide_ends = dot(parts_of(ends, 3), spread_all(3, width))
    for j in range(blocks):
        for p in range(pairs):
            cols = slice(128 * p, 128 * (p + 1))
            marks[j, pairs + p : pairs + p + 1, :] = wide_ends[j : j + 1, cols]
            if j == 0:
                marks[j, p : p + 1, :] = jnp.zeros((1, 128), f32)
            else:
                marks[j, p : p + 1, :] = wide_ends[j - 1 : j, cols]
    fall[...] = parts_of(jnp.exp(start - fade[...]), 2)
    fetch.wait()
    for n in range(0, width, WIDE):
        cols = slice(n, n + WIDE)
        keys[:, cols] = dot(x[...], mine[0, :, cols]).astype(bf16)
        values[:, cols] = dot(x[...], mine[1, :, cols]).astype(bf16)
    hot = spread_all(2, width)
    for n in range(pairs // 2):
        cols = slice(WIDE * n, WIDE * (n + 1))
        kf = (keys[:, cols].astype(f32) * dot(fall[...], hot[:, cols])).astype(bf16)
        set_memory(memory, dot(kf, values[:, cols], TN), n)
    stores.append(fetched(keys, keys_out, sems.at[3]))
    stores.append(fetched(values, values_out, sems.at[4]))
    write_state(send, memory, fade_t[blocks - 1][:, CH - 1 : CH], pairs)
    for store in stores:
        store.wait()


def attend(
    info, x, weights, keys, values, fade, fade_t, marks,
    q8, attended_out, states, lift,
    memory, attended, mine, in_sem, sems,
):
    fetch = fetched(weights.at[info[0], 0], mine, in_sem)
    lift[...] = parts_of(jnp.exp(fade[...]), 2)
    fetch.wait()
    for n in range(0, x.shape[1], WIDE):
        cols = slice(n, n + WIDE)
        query = dot(x[...], mine[:, cols]).astype(bf16).astype(f32)
        q8[:, cols] = (query * 0.125).astype(bf16)
    slots, width = q8.shape
    pairs = width // 128
    low, high = halves()
    mask = block_mask()
    memory[...] = jnp.zeros(memory.shape, f32)

    def block(j, carry):
        rows = pl.ds(pl.multiple_of(j * CH, CH), CH)
        edge = marks[j]
        for p in range(pairs):
            cols = slice(128 * p, 128 * (p + 1))
            start, end = edge[p : p + 1, :], edge[pairs + p : pairs + p + 1, :]
            qp, kp, vp = q8[rows, cols], keys[rows, cols], values[rows, cols]
            scores = dot(qp, stacked(kp, low, high), NT)
            fading, g = decay_pair(fade, fade_t, rows, j, p)
            mix = (scores * fading).astype(bf16)
            within = dot(mix, stacked(vp, low, high))
            now = memory[p]
            states[j, p] = folded(now).astype(bf16)
            lifted = (qp.astype(f32) * jnp.exp(g - start)).astype(bf16)
            attended[rows, cols] = within + dot(lifted, now.astype(bf16))
            kf = (kp.astype(f32) * jnp.exp(end - g)).astype(bf16)
            memory[p] = jnp.exp(end - start) * now + jnp.where(mask, dot(kf, vp, TN), 0.0)
        rows_copy(attended, attended_out, sems, j).start()
        return carry

    lax.fori_loop(0, slots // CH, block, 0, unroll=True)
    for j in range(slots // CH):
        rows_copy(attended, attended_out, sems, j).wait()


def turn(info, q8, lift, fade_t, attended_in, x_in, weights, message, partner, *rest):
    received = rest[:-19]
    (
        encoded, grads_out, grad_full, incoming, send,
        scratch, mine, x, attended, grads, grad_normed, normed, lifts,
        wide, narrow, states, memory, sems, out_sems,
    ) = rest[-19:]
    fetch = fetched(weights.at[info[0], 3], mine, sems.at[0])
    rows_in = fetched(x_in, x, sems.at[1])
    attended_here = fetched(attended_in, attended, sems.at[3])
    slots, width = x.shape
    pairs = width // 128
    blocks = slots // CH
    arrived = gathered_state(info[1].astype(f32), partner, received, pairs)
    for p in range(pairs):
        incoming[p] = arrived[p]
    set_states(states, arrived)
    for j, part in enumerate(read_message(message, scratch, width)):
        grads[:, 128 * j : 128 * (j + 1)] = part.astype(bf16)
    store = fetched(grads, grads_out, sems.at[4])
    fetch.wait()
    for n in range(0, width, WIDE):
        cols = slice(n, n + WIDE)
        grad_normed[:, cols] = dot(grads[...], mine[cols, :], NT).astype(bf16)
    attended_here.wait()

    hot = spread_all(2, width)

    def block(j, carry):
        rows = pl.ds(pl.multiple_of(j * CH, CH), CH)
        factors = dot(lift[rows, :], hot)
        values = []
        square = jnp.zeros((CH, 1), f32)
        for n in range(pairs // 2):
            cols = slice(WIDE * n, WIDE * (n + 1))
            lifted = (q8[rows, cols].astype(f32) * factors[:, cols]).astype(bf16)
            lifts[rows, cols] = lifted
            value = attended[rows, cols] + dot(lifted, states[n])
            values.append(value)
            square += jnp.sum(value * value, axis=1, keepdims=True)
        here = jnp.concatenate(values, axis=1)
        scale = lax.rsqrt(square * (1.0 / width) + 1e-06)
        normed[rows, :] = (here * scale).astype(bf16)
        grad = grad_normed[rows, :].astype(f32)
        along = jnp.mean(here * grad, axis=1, keepdims=True)
        grad_full[rows, :] = (scale * grad - here * (scale * scale * scale * along)).astype(bf16)
        return carry

    lax.fori_loop(0, blocks, block, 0, unroll=True)
    for n in range(pairs // 2):
        cols = slice(WIDE * n, WIDE * (n + 1))
        set_memory(memory, dot(lifts[:, cols], grad_full[:, cols], TN), n)
    write_state(send, memory, fade_t[blocks - 1][:, CH - 1 : CH], pairs)
    rows_in.wait()
    for n in range(0, width, WIDE):
        cols = slice(n, n + WIDE)
        attended[:, cols] = x[:, cols].astype(f32) + dot(normed[...], mine[:, cols])
    sender = Sender(encoded, wide, narrow, out_sems, pairs)

    def put(j, carry):
        sender.put(j, attended[pl.ds(pl.multiple_of(j * CH, CH), CH), :])
        return carry

    lax.fori_loop(0, blocks, put, 0)
    sender.finish(blocks)
    store.wait()


def backward_local(
    info, q8, keys_in, values_in, fade, fade_t, marks, grad_full, states, incoming,
    grads_in, weights,
    grad_keys, grad_values, partial,
    memory, grad_q, grads, mine, keys, values, sems, key_sems, value_sems,
):
    for j in reversed(range(q8.shape[0] // CH)):
        rows_copy(keys_in, keys, key_sems, j).start()
        rows_copy(values_in, values, value_sems, j).start()
    arrival = fetched(grads_in, grads, sems.at[0])
    fetch = fetched(weights.at[info[0], 0], mine, sems.at[1])
    slots, width = q8.shape
    pairs = width // 128
    blocks = slots // CH
    low, high = halves()
    lower = iota((CH, 128), 1) < 64
    mask = block_mask()
    memory[...] = jnp.zeros(memory.shape, f32)

    def block(i, carry):
        j = blocks - 1 - i
        rows_copy(keys_in, keys, key_sems, j).wait()
        rows_copy(values_in, values, value_sems, j).wait()
        rows = pl.ds(pl.multiple_of(j * CH, CH), CH)
        edge = marks[j]
        for p in range(pairs):
            cols = slice(128 * p, 128 * (p + 1))
            start, end = edge[p : p + 1, :], edge[pairs + p : pairs + p + 1, :]
            qp, kp, vp = q8[rows, cols], keys[rows, cols], values[rows, cols]
            da = grad_full[rows, cols]
            ks, vs = stacked(kp, low, high), stacked(vp, low, high)
            fading, g = decay_pair(fade, fade_t, rows, j, p)
            mix = (dot(qp, ks, NT) * fading).astype(bf16)
            grad_scores = (dot(da, vs, NT) * fading).astype(bf16)
            lift = jnp.exp(g - start)
            fall = jnp.exp(end - g)
            state = states[j, p].astype(f32) + jnp.exp(start) * incoming[p]
            state = unfolded(state, mask).astype(bf16)
            grad_q[rows, cols] = (
                0.125 * (dot(grad_scores, ks) + lift * dot(da, state, NT))
            ).astype(bf16)
            gk = dot(grad_scores, qp, TN)
            gv = dot(mix, da, TN)
            now = memory[p]
            narrow = now.astype(bf16)
            kf = (kp.astype(f32) * fall).astype(bf16)
            grad_keys[rows, cols] = jnp.where(lower, gk[0:CH], gk[CH:]) + fall * dot(vp, narrow, NT)
            grad_values[rows, cols] = jnp.where(lower, gv[0:CH], gv[CH:]) + dot(kf, narrow)
            lifted = (qp.astype(f32) * lift).astype(bf16)
            memory[p] = jnp.exp(end - start) * now + jnp.where(mask, dot(lifted, da, TN), 0.0)
        return carry

    lax.fori_loop(0, blocks, block, 0, unroll=True)
    arrival.wait()
    fetch.wait()
    for n in range(0, width, WIDE):
        cols = slice(n, n + WIDE)
        partial[:, cols] = grads[:, cols].astype(f32) + dot(grad_q[...], mine[cols, :], NT)


def backward_finish(
    info, partial, grad_keys, grad_values, keys_in, values_in, fall, weights, partner, *rest
):
    received = rest[:-12]
    out, mine, wide, narrow, states, gk, gv, total, keys, values, sems, out_sems = rest[-12:]
    keys_here = fetched(keys_in, keys, sems.at[1])
    values_here = fetched(values_in, values, sems.at[2])
    fetch = fetched(weights.at[info[0], pl.ds(1, 2)], mine, sems.at[0])
    slots, width = partial.shape
    pairs = width // 128
    blocks = slots // CH
    set_states(states, gathered_state((1 - info[1]).astype(f32), partner, received, pairs))
    hot = spread_all(2, width)
    keys_here.wait()
    values_here.wait()
    for n in range(pairs // 2):
        cols = slice(WIDE * n, WIDE * (n + 1))
        factor = dot(fall[...], hot[:, cols])
        kf = (keys[:, cols].astype(f32) * factor).astype(bf16)
        gk[:, cols] = (grad_keys[:, cols] + factor * dot(values[:, cols], states[n], NT)).astype(bf16)
        gv[:, cols] = (grad_values[:, cols] + dot(kf, states[n])).astype(bf16)
    fetch.wait()
    for n in range(0, width, WIDE):
        cols = slice(n, n + WIDE)
        total[:, cols] = (
            partial[:, cols] + dot(gk[...], mine[0, cols, :], NT) + dot(gv[...], mine[1, cols, :], NT)
        )
    sender = Sender(out, wide, narrow, out_sems, pairs)

    def put(j, carry):
        sender.put(j, total[pl.ds(pl.multiple_of(j * CH, CH), CH), :])
        return carry

    lax.fori_loop(0, blocks, put, 0)
    sender.finish(blocks)


def swapped(value, axis):
    return lax.ppermute(value, axis, [(i, i ^ 1) for i in range(lax.axis_size(axis))])


def exchange(value, axis, sign):
    count = lax.axis_size(axis)
    return [
        lax.ppermute(
            value, axis, [(i, i + sign * k) for i in range(count) if 0 <= i + sign * k < count]
        )
        for k in range(2, count, 2)
    ]


def regroup(value):
    return lax.all_to_all(value, "log", split_axis=0, concat_axis=0, tiled=True)


def shards(events, owner_ids, elapsed, resets, decay_rates, weights, cotangent):
    rows, width = events.shape[2:]
    owners = lax.axis_size("log")
    cap = 5 * rows // (4 * owners)
    slots = owners * cap
    pairs = width // 128
    blocks = slots // CH
    per = cap * pairs
    flat = pltpu.VMEM((slots * pairs, 128), f32)
    state_vmem = pltpu.VMEM((pairs, 128, 128), f32)
    state_msg = ((64 * pairs + 8, 128), bf16)
    wide16, wide32 = ((slots, width), bf16), ((slots, width), f32)

    tower = lax.axis_index("log") // (owners // decay_rates.shape[0])
    info = jnp.stack([tower, lax.axis_index("ctx") % 2]).astype(jnp.int32)
    sem = pltpu.SemaphoreType.DMA

    message, spots = call(
        pack_events,
        [((owners, per + 8, 128), bf16), ((2, rows), jnp.int32)],
        [
            owner_ids.reshape(1, rows),
            events.reshape(rows, width),
            elapsed.reshape(1, rows),
            resets.reshape(1, rows),
        ],
        [
            flat,
            pltpu.VMEM((slots, rows), bf16),
            pltpu.VMEM((rows, rows), bf16),
            pltpu.VMEM((1, rows), jnp.int32),
            pltpu.VMEM((rows, width), bf16),
            pltpu.VMEM((1, rows), f32),
            pltpu.VMEM((1, rows), f32),
            pltpu.SemaphoreType.DMA((4,)),
        ],
        {0: HBM, 1: HBM, 2: HBM, 3: HBM},
    )
    events_in = regroup(message)
    flat_msg = ((slots * pairs, 128), bf16)
    message, back, expand, own_lanes = call(
        pack_grads,
        [
            flat_msg, ((rows, slots), bf16), ((slots, owners * 8), bf16), ((slots, 128), bf16),
        ],
        [info, spots, cotangent.reshape(rows, width)],
        [flat, pltpu.VMEM(*flat_msg), pltpu.VMEM((rows, slots), bf16), sem((2,))],
        {0: SMEM},
        (0, 1),
    )
    grads_in = regroup(message.reshape(owners, per, 128))
    one = pltpu.VMEM((width, width), bf16)
    two = pltpu.VMEM((2, width, width), bf16)
    half_states = ((pairs, 64, 128), f32)
    block_wide = pltpu.VMEM((CH * pairs, 128), f32)
    flat_narrow = pltpu.VMEM(*flat_msg)
    rows16, rows32 = pltpu.VMEM(*wide16), pltpu.VMEM(*wide32)
    narrow_states = pltpu.VMEM((pairs // 2, WIDE, WIDE), bf16)
    x, keys, values, keys_far, values_far, fade, fade_t, marks, fall, send, x_near = call(
        forward_state,
        [
            wide16, wide16, wide16, wide16, wide16, ((slots, 128), f32), ((blocks, 8, 128), f32),
            ((blocks, 2 * pairs, 128), f32), ((slots, 128), bf16), state_msg,
            wide16,
        ],
        [info, decay_rates, events_in, weights, expand, own_lanes],
        [flat, state_vmem, two, sem((5,))],
        {0: SMEM, 1: SMEM, 3: HBM},
        (0, 3, 4),
    )
    partner = swapped(send, "ctx")
    (joined,) = call(join_ahead, [state_msg], [info, send, partner], (), {0: SMEM})
    received = exchange(joined, "ctx", 1)
    q8, attended, kept, lift = call(
        attend,
        [wide16, wide32, ((blocks, pairs, 64, 128), bf16), ((slots, 128), bf16)],
        [info, x_near, weights, keys, values, fade, fade_t, marks],
        [state_vmem, rows32, one, sem, sem((blocks,))],
        {0: SMEM, 2: HBM},
        (1,),
    )
    message, grads, grad_full, incoming, send = call(
        turn,
        [flat_msg, wide16, wide16, half_states, state_msg],
        [info, q8, lift, fade_t, attended, x, weights, grads_in, partner, *received],
        [
            flat, one, rows16, rows32, rows16, rows16, rows16,
            rows16, block_wide, flat_narrow, narrow_states, state_vmem, sem((5,)), sem((blocks,)),
        ],
        {0: SMEM, 4: HBM, 5: HBM, 6: HBM},
        (0, 1),
    )
    partner = swapped(send, "ctx")
    encoded_in = regroup(message.reshape(owners, per, 128))
    grad_keys, grad_values, partial = call(
        backward_local,
        [wide32, wide32, wide32],
        [
            info, q8, keys_far, values_far, fade, fade_t, marks, grad_full, kept, incoming, grads,
            weights,
        ],
        [
            state_vmem, rows16, rows16, one, rows16, rows16, sem((2,)), sem((blocks,)),
            sem((blocks,)),
        ],
        {0: SMEM, 2: HBM, 3: HBM, 10: HBM, 11: HBM},
    )
    (joined,) = call(join_back, [state_msg], [info, send, partner], (), {0: SMEM})
    received = exchange(joined, "ctx", -1)
    (message,) = call(
        backward_finish,
        [flat_msg],
        [
            info, partial, grad_keys, grad_values, keys_far, values_far, fall, weights, partner,
            *received,
        ],
        [
            two, block_wide, flat_narrow, narrow_states,
            rows16, rows16, rows32, rows16, rows16, sem((3,)), sem((blocks,)),
        ],
        {0: SMEM, 4: HBM, 5: HBM, 7: HBM},
        (0,),
    )
    grad_in = regroup(message.reshape(owners, per, 128))
    (encoded,) = call(unpack_rows, [((rows, width), bf16)], [back, encoded_in], [flat])
    (grad,) = call(unpack_rows, [((rows, width), bf16)], [back, grad_in], [flat])
    return encoded.reshape(events.shape), grad.reshape(events.shape)


def solution(mesh):
    wide = P("ctx", "log", None, None)
    flat = P("ctx", "log", None)
    return jax.shard_map(
        shards,
        mesh=mesh,
        in_specs=(wide, wide, flat, flat, P(), P(), wide),
        out_specs=(wide, wide),
        check_vma=False,
    )
```
